32 devices in a mesh: dp: 16 (over z, y, x), tensor: 2 (over core).
Axes of the slice: x: 2, y: 2, z: 4, core: 2. Of those that a mesh axis runs over, the one named last changes fastest.
Arguments:
- hidden_in: bfloat16 [2, 16384, 768], P(None, ('dp', 'tensor')), may hold values from -6 to 6
- segment_ids: int32 [2, 16384], P(None, 'dp'), may hold values from 0 to 53, never falling along the last dimension, each value on 1 to 800 neighbouring positions
- qkv_weight: bfloat16 [3, 768, 768], P(None, 'dp', 'tensor'), may hold values from -0.21875 to 0.21875
- out_weight: bfloat16 [768, 768], P('tensor', 'dp'), may hold values from -1.75 to 1.75
- mlp_weight: bfloat16 [2, 768, 1152], P(None, 'dp', 'tensor'), may hold values from -0.21875 to 0.21875
- down_weight: bfloat16 [1152, 768], P('tensor', 'dp'), may hold values from -0.1875 to 0.1875
- attn_gain: bfloat16 [768], P('dp'), may hold values from 0.099609375 to 1.8984375
- mlp_gain: bfloat16 [768], P('dp'), may hold values from 0.099609375 to 1.8984375
- cotangent: bfloat16 [2, 16384, 768], P(None, ('dp', 'tensor')), may hold values from -6 to 6
Outputs:
- layer_out: bfloat16 [2, 16384, 768], P(None, ('dp', 'tensor'))
- input_grad: float32 [2, 16384, 768], P(None, ('dp', 'tensor'))
- qkv_grad: float32 [3, 768, 768], P(None, 'dp', 'tensor')
- proj_grad: float32 [768, 768], P('tensor', 'dp')
- mlp_grad: float32 [2, 768, 1152], P(None, 'dp', 'tensor')
- down_grad: float32 [1152, 768], P('tensor', 'dp')
- attn_gain_grad: float32 [768], P('dp')
- mlp_gain_grad: float32 [768], P('dp')
The draws below stay inside these ranges and needn't reach their ends.
Inputs may be any that keep to these rules, and one draw needn't show every extreme that they name: `segment_ids`: along each micro-batch's 16384 tokens the segment ids never fall; each document has 1 to 800 tokens and one has exactly 800.
All inputs are finite; a program needn't handle non-finite values.
Results may differ from the reference program's by a relative error of at most 0.018.
Values may be sent and summed in bfloat16 or wider, within the bound.
No kernel may reach another device: no remote copies, remote signals or barrier semaphores. Data moves between devices by JAX's collectives and lax.ppermute only.
A program may use at most 128 MiB of HBM per device.

```python
import math
import jax
import jax.numpy as jnp
import numpy as np
from jax import lax

D = 768
FF = 1152
HEAD_DIM = 64
SEQ = 1024
MB = 2
DOC_MOST = 800
TOKENS_MB = 16384
DOC_COUNT = 54
N_DP = 16


def steps_of(stream_key, shape, cuts, smallest, high):
    level = 1.0
    for dim, shards_of in cuts:
        steps = jax.random.uniform(jax.random.fold_in(jax.random.fold_in(stream_key, 6), dim), (shards_of,), jnp.float32, smallest / len(cuts), high / len(cuts))
        level = level * jnp.repeat(jnp.exp(steps), shape[dim] // shards_of).reshape((-1,) + (1,) * (len(shape) - 1 - dim))
    return level


def profile(number_of, total, limit, skew):
    loads = [(1 << 20) // math.isqrt(standing ** skew) + 1 for standing in range(2, number_of + 1)]
    surplus, counts = total - limit - (number_of - 1), [1] * (number_of - 1)
    while surplus > 0:
        movable = [i for i in range(number_of - 1) if counts[i] < limit]
        mass, left = sum([loads[i] for i in movable]), surplus
        for i in movable:
            addition = min(limit - counts[i], max(1, left * loads[i] // mass), surplus)
            counts[i] = counts[i] + addition
            surplus = surplus - addition
    return np.array([limit] + counts)


def uneven_parts(own_key, number_of, total, most, lean):
    if number_of == 2:
        one = jax.random.randint(own_key, (), max(1, total - most), min(most, total - 1) + 1)
        return jnp.stack([one, total - one])
    lengths = jnp.asarray(profile(number_of, total, most, lean), jnp.int32)
    couples = (number_of - 1) // 2
    donor, taker = lengths[1:1 + 2 * couples:2], lengths[2:2 + 2 * couples:2]
    margin = jnp.minimum(donor - 1, most - taker)
    passed = jax.random.randint(jax.random.fold_in(own_key, 1), (couples,), 0, 1 << 20) % (margin + 1)
    lengths = lengths.at[1:1 + 2 * couples:2].set(donor - passed).at[2:2 + 2 * couples:2].set(taker + passed)
    return lengths[jax.random.permutation(jax.random.fold_in(own_key, 2), number_of)]


def gaussian(stream_key, extent, scale, most, pieces=(), kind=jnp.bfloat16):
    drawn = scale * jax.random.normal(stream_key, extent, jnp.float32)
    if pieces:
        drawn = drawn * steps_of(stream_key, extent, pieces, -0.22, 0.18)
    return jnp.clip(drawn, -most, most).astype(kind)


def setup_inputs(seed: int = 0) -> dict:
    seeds = jax.random.split(jax.random.key(seed), 10)
    return {
        "hidden_in": gaussian(seeds[0], (MB, TOKENS_MB, D), 1.0, 6.0, ((1, 32),)),
        "segment_ids": jax.vmap(lambda own: jnp.searchsorted(jnp.cumsum(uneven_parts(own, DOC_COUNT, TOKENS_MB, DOC_MOST, 1)), jnp.arange(TOKENS_MB), side="right"))(jax.random.split(seeds[1], MB)).reshape((MB, TOKENS_MB)).astype(jnp.int32),
        "qkv_weight": gaussian(seeds[2], (3, D, D), D ** -0.5, 0.21875, ((1, 16), (2, 2))),
        "out_weight": gaussian(seeds[3], (D, D), (D // 64) ** -0.5, 1.75, ((0, 2), (1, 16))),
        "mlp_weight": gaussian(seeds[4], (2, D, FF), D ** -0.5, 0.21875, ((1, 16), (2, 2))),
        "down_weight": gaussian(seeds[5], (FF, D), FF ** -0.5, 0.1875, ((0, 2), (1, 16))),
        "attn_gain": jnp.clip(1.0 + 0.18 * jax.random.normal(seeds[6], (D,), jnp.float32), 0.099609375, 1.8984375).astype(jnp.bfloat16),
        "mlp_gain": jnp.clip(1.0 + 0.18 * jax.random.normal(seeds[7], (D,), jnp.float32), 0.099609375, 1.8984375).astype(jnp.bfloat16),
        "cotangent": gaussian(seeds[8], (MB, TOKENS_MB, D), 1.0, 6.0, ((1, 32),)),
    }


theta_base = 160000.0
eps_norm = 1e-05
highest = lax.Precision.HIGHEST

@jax.custom_vjp
def low(v):
    return lax.optimization_barrier(v.astype(jnp.bfloat16)).astype(jnp.float32)

@jax.custom_vjp
def low_back(v):
    return v

def low_keep(v):
    return (low(v), None)

def low_pass(kept, grad):
    return (grad,)

def back_keep(v):
    return (v, None)

def back_low(kept, grad):
    return (low(grad),)
low.defvjp(low_keep, low_pass)
low_back.defvjp(back_keep, back_low)

def positions_of(segments):
    indices = jnp.arange(segments.shape[0], dtype=jnp.int32)
    change = jnp.concatenate([jnp.ones((1,), dtype=jnp.bool_), segments[1:] != segments[:-1]])
    starts = lax.cummax(jnp.where(change, indices, jnp.zeros_like(indices)), axis=0)
    return indices - starts

def rotary_tables(segments):
    half_dim = HEAD_DIM // 2
    freqs = theta_base ** (-2.0 * jnp.arange(half_dim, dtype=jnp.float32) / HEAD_DIM)
    angles = positions_of(segments).astype(jnp.float32)[:, None] * freqs[None, :]
    return (jnp.cos(angles)[:, None, :], jnp.sin(angles)[:, None, :])

def rotate(values, cosine, sine):
    half_dim = values.shape[-1] // 2
    first_half = values[..., :half_dim]
    second_half = values[..., half_dim:]
    return jnp.concatenate([first_half * cosine - second_half * sine, second_half * cosine + first_half * sine], axis=-1)

def normalize(values):
    center = values - lax.optimization_barrier(jnp.mean(values, axis=-1, keepdims=True))
    return center * lax.rsqrt(lax.optimization_barrier(jnp.mean(center * center, axis=-1, keepdims=True)) + eps_norm)

def layer_forward(hidden, segments, qkv_full, proj_full, mlp_full, down_full, gain_attn, gain_mlp):
    seq_len = hidden.shape[0]
    heads = D // HEAD_DIM
    cosine, sine = rotary_tables(segments)
    normed = low(normalize(hidden) * gain_attn)
    raw = low_back(jnp.einsum('rd,cde->cre', normed, qkv_full, precision=highest))
    queries = low(rotate(raw[0].reshape(seq_len, heads, HEAD_DIM), cosine, sine))
    keys = low(rotate(raw[1].reshape(seq_len, heads, HEAD_DIM), cosine, sine))
    values = low(raw[2].reshape(seq_len, heads, HEAD_DIM))
    scores = low_back(jnp.einsum('qhe,khe->hqk', queries, keys, precision=highest) * HEAD_DIM ** (-0.5))
    allowed = segments[:, None] == segments[None, :]
    scores = jnp.where(allowed[None], scores, -1e+30)
    peak = lax.optimization_barrier(jnp.max(scores, axis=-1, keepdims=True))
    expo = jnp.exp(scores - peak)
    probs = low(expo / lax.optimization_barrier(jnp.sum(expo, axis=-1, keepdims=True)))
    attended = low_back(low(jnp.einsum('hqk,khe->qhe', probs, values, precision=highest))).reshape(seq_len, D)
    branch = low_back(jnp.dot(attended, proj_full, precision=highest))
    middle = hidden + branch
    normed_mlp = low(normalize(middle) * gain_mlp)
    gate_up = low_back(jnp.einsum('rd,cdf->crf', normed_mlp, mlp_full, precision=highest))
    mixed = low(jax.nn.gelu(gate_up[0], approximate=False) * gate_up[1])
    return middle + low_back(jnp.dot(mixed, down_full, precision=highest))

def reference(hidden_in, segment_ids, qkv_weight, out_weight, mlp_weight, down_weight, attn_gain, mlp_gain, cotangent):
    weights = (qkv_weight.astype(jnp.float32), out_weight.astype(jnp.float32), mlp_weight.astype(jnp.float32), down_weight.astype(jnp.float32), attn_gain.astype(jnp.float32), mlp_gain.astype(jnp.float32))
    sequences = MB * N_DP
    inputs = hidden_in.astype(jnp.float32).reshape(sequences, SEQ, D)
    segments_all = segment_ids.reshape(sequences, SEQ)
    cotangents = cotangent.astype(jnp.float32).reshape(sequences, SEQ, D)

    def one_sequence(running, item):
        hidden, segments, grad_out = item

        def forward(hidden_value, qkv_full, proj_full, mlp_full, down_full, gain_attn, gain_mlp):
            return layer_forward(hidden_value, segments, qkv_full, proj_full, mlp_full, down_full, gain_attn, gain_mlp)
        result, pullback = jax.vjp(forward, hidden, *weights)
        grads = pullback(grad_out)
        running = tuple((before + added for before, added in zip(running, grads[1:])))
        return (running, (result.astype(jnp.bfloat16), grads[0]))
    zeros = tuple((jnp.zeros_like(weight) for weight in weights))
    totals, (results, input_grads) = lax.scan(one_sequence, zeros, (inputs, segments_all, cotangents))
    return (results.reshape(MB, N_DP * SEQ, D), input_grads.reshape(MB, N_DP * SEQ, D), totals[0], totals[1], totals[2], totals[3], totals[4], totals[5])
```

```python
import functools

import jax
import jax.numpy as jnp
from jax import lax
from jax.experimental import pallas as pl
from jax.experimental.pallas import tpu as pltpu
from jax.sharding import PartitionSpec as P

HEAD_DIM = 64
LANES = 128
QB = 256
TB = 256
VMEM = 56 << 20
THETA = 160000.0
EPS = 1e-05
BF = jnp.bfloat16
F32 = jnp.float32

ORDER_A = (0, 4, 8, 12, 1, 5, 9, 13, 2, 6, 10, 14, 3, 7, 11, 15)
ORDER_B = (0, 4, 8, 12, 2, 6, 10, 14, 1, 5, 9, 13, 3, 7, 11, 15)


def nn(a, b):
    return lax.dot_general(a, b, (((1,), (0,)), ((), ())), preferred_element_type=F32)


def nt(a, b):
    return lax.dot_general(a, b, (((1,), (1,)), ((), ())), preferred_element_type=F32)


def tn(a, b):
    return lax.dot_general(a, b, (((0,), (0,)), ((), ())), preferred_element_type=F32)


def up_to(n):
    return -(-n // LANES) * LANES


def rotate(u, cos, sin, sign):
    lane = lax.broadcasted_iota(jnp.int32, u.shape, 1)
    half = HEAD_DIM // 2
    partner = jnp.where(
        (lane % HEAD_DIM) < half, pltpu.roll(u, LANES - half, 1), pltpu.roll(u, half, 1)
    )
    return u * cos + partner * sin if sign > 0 else u * cos - partner * sin


def norm(x):
    center = x - jnp.mean(x, axis=-1, keepdims=True)
    inverse = lax.rsqrt(jnp.mean(center * center, axis=-1, keepdims=True) + EPS)
    return center * inverse, inverse


def norm_back(grad, xhat, inverse, gain):
    z = grad * gain
    inner = z - jnp.mean(z, axis=-1, keepdims=True) - xhat * jnp.mean(z * xhat, axis=-1, keepdims=True)
    return inverse * inner


def staged(count, stages):
    live = [None] * len(stages)
    for step in range(count + len(stages) - 1):
        new = [None] * len(stages)
        for s, stage in enumerate(stages):
            if 0 <= step - s < count:
                new[s] = stage(step - s, live[s - 1] if s else None)
        live = new


def call(kernel, name, grid, in_specs, out_specs, out_shape, scratch=(), prefetch=1):
    return pl.pallas_call(
        kernel,
        grid_spec=pltpu.PrefetchScalarGridSpec(
            num_scalar_prefetch=prefetch,
            grid=grid,
            in_specs=in_specs,
            out_specs=out_specs,
            scratch_shapes=list(scratch),
        ),
        out_shape=out_shape,
        compiler_params=pltpu.CompilerParams(vmem_limit_bytes=VMEM),
        name=name,
    )


ANY = pl.BlockSpec(memory_space=pl.ANY)


def load_weights(info, pieces, layout, rows, dest, sems):
    copies = []
    for ref, (r, col, order) in zip(pieces, layout, strict=True):
        cols = pl.ds(col, ref.shape[1])
        if order is None:
            copies.append((ref, dest.at[r, :, cols]))
            continue
        for i, k in enumerate(order):
            row = pl.multiple_of((info[1] ^ k) * rows, rows)
            copies.append((ref.at[pl.ds(i * rows, rows), :], dest.at[r, pl.ds(row, rows), cols]))
    copies = [pltpu.make_async_copy(a, b, sems.at[i]) for i, (a, b) in enumerate(copies)]
    for c in copies:
        c.start()
    for c in copies:
        c.wait()


def copies_of(layout):
    return sum(1 if order is None else len(order) for _, _, order in layout)


def store_rows(info, value_ref, out_ref, cols, order, rows):
    if order is None:
        out_ref[:, cols] = value_ref[...].astype(BF)
        return
    for i, k in enumerate(order):
        row = pl.multiple_of((info[1] ^ k) * rows, rows)
        out_ref[i * rows : (i + 1) * rows, cols] = value_ref[pl.ds(row, rows), :].astype(BF)


def own_block(info, half):
    return pl.program_id(0) // half == info[0]


def qkv_kernel(info, *refs, layout, rows, width, half):
    n = len(layout)
    pieces, (x_ref, recv_ref, cos_ref, sin_ref, qkv_ref, h_ref, gain_ref, w_ref, sems) = refs[:n], refs[n:]

    @pl.when(pl.program_id(0) == 0)
    def _():
        load_weights(info, pieces, layout, rows, w_ref, sems)
        gain_ref[...] = w_ref[0, :, 3 * width :].astype(F32).T[:8]

    x = jnp.where(own_block(info, half), x_ref[...], recv_ref[...]).astype(F32)
    xhat, _ = norm(x)
    h = (xhat * gain_ref[0:1, :]).astype(BF)
    h_ref[...] = h
    cos, sin = cos_ref[...], sin_ref[...]
    for r in range(2):
        raw = nn(h, w_ref[r, :, : 3 * width])
        for b in range(2 * width // LANES):
            cols = slice(b * LANES, (b + 1) * LANES)
            u = rotate(raw[:, cols], cos, sin, 1)
            if b < width // LANES:
                u = u * HEAD_DIM**-0.5
            qkv_ref[r, :, cols] = u.astype(BF)
        qkv_ref[r, :, 2 * width :] = raw[:, 2 * width :].astype(BF)


def token_specs(d, half):
    def clip(b, first):
        return jnp.clip(b - first, 0, half - 1)

    held = pl.BlockSpec((None, TB, d), lambda b, i: (i[0], b % half, 0))
    recv = pl.BlockSpec((TB, d), lambda b, i: (b % half, 0))
    rows = pl.BlockSpec((TB, d), lambda b, i: (b, 0))
    own = pl.BlockSpec((TB, d), lambda b, i: (clip(b, half * i[0]), 0))
    other = pl.BlockSpec((TB, d), lambda b, i: (clip(b, half * (1 - i[0])), 0))
    return held, recv, rows, own, other


def qkv_call(info, pieces, layout, rows, width, x, recv, cos, sin):
    d, s = x.shape[2], cos.shape[0]
    half = s // TB // 2
    held, received, block, _, _ = token_specs(d, half)
    table = pl.BlockSpec((TB, LANES), lambda b, i: (b, 0))
    cols = 3 * width + LANES
    return call(
        functools.partial(qkv_kernel, layout=layout, rows=rows, width=width, half=half),
        "qkv",
        (s // TB,),
        [ANY] * len(layout) + [held, received, table, table],
        [
            pl.BlockSpec((2, TB, 3 * width), lambda b, i: (0, b, 0)),
            block,
            pl.BlockSpec((8, d), lambda b, i: (0, 0)),
        ],
        [
            jax.ShapeDtypeStruct((2, s, 3 * width), BF),
            jax.ShapeDtypeStruct((s, d), BF),
            jax.ShapeDtypeStruct((8, d), F32),
        ],
        [pltpu.VMEM((2, d, cols), BF), pltpu.SemaphoreType.DMA((copies_of(layout),))],
    )(info, *pieces, x, recv, cos, sin)


def same_segment(col, row):
    parts = [
        jnp.where(col == row[:, i * LANES : (i + 1) * LANES], 0.0, -1e30).astype(F32)
        for i in range(row.shape[1] // LANES)
    ]
    return jnp.concatenate(parts, 1)


def by_range(ranges, blocks, run):
    i = pl.program_id(1)
    for n in range(1, blocks + 1):

        @pl.when(ranges[i, 1] == n)
        def _(n=n):
            run(n, pl.ds(pl.multiple_of(ranges[i, 0], QB) if n < blocks else 0, n * QB))


def attend_kernel(ranges, col_ref, row_ref, q_ref, k_ref, v_ref, o_ref, lse_ref, vt_ref):
    s, width = k_ref.shape
    heads = width // HEAD_DIM

    @pl.when(pl.program_id(1) == 0)
    def _():
        vt_ref[...] = v_ref[...].T

    def run(n, keys):
        bias = same_segment(col_ref[keys, :], row_ref[0:1, :])
        outs = [None] * heads

        def lanes(h):
            return slice(h * HEAD_DIM, (h + 1) * HEAD_DIM)

        def scores(h, _):
            x = nn(k_ref[keys, lanes(h)], q_ref[:, lanes(h)].T) + bias
            return x, jnp.max(x, axis=0, keepdims=True)

        def expo(h, a):
            e = jnp.exp(a[0] - a[1])
            return e.astype(BF), jnp.sum(e, axis=0, keepdims=True), a[1]

        def out(h, a):
            outs[h] = nn(vt_ref[lanes(h), keys], a[0]) * (1.0 / a[1])
            lse_ref[h : h + 1, :] = a[2] + jnp.log(a[1])

        staged(heads, [scores, expo, out])
        o_ref[...] = jnp.concatenate(outs, axis=0).T.astype(BF)

    by_range(ranges, s // QB, run)


def attend_call(ranges, col, row, qkv):
    _, s, w3 = qkv.shape
    width = w3 // 3

    def whole(c):
        return pl.BlockSpec((None, s, width), lambda r, i, g: (r, 0, c))

    block = pl.BlockSpec((None, QB, width), lambda r, i, g: (r, i, 0))
    return call(
        attend_kernel,
        "attend",
        (2, s // QB),
        [
            pl.BlockSpec((s, LANES), lambda r, i, g: (0, 0)),
            pl.BlockSpec((8, QB), lambda r, i, g: (0, i)),
            block,
            whole(1),
            whole(2),
        ],
        [block, pl.BlockSpec((None, 8, QB), lambda r, i, g: (r, 0, i))],
        [jax.ShapeDtypeStruct((2, s, width), BF), jax.ShapeDtypeStruct((2, 8, s), F32)],
        [pltpu.VMEM((width, s), BF)],
    )(ranges, col, row, qkv, qkv, qkv)


def attend_back_kernel(
    ranges, col_ref, row_ref, q_ref, k_ref, v_ref, do_ref, o_ref, lse_ref, cos_ref, sin_ref,
    dq_ref, dkv_ref, qt_ref, dot_ref, dqt_ref, delta_ref,
):
    s, width = q_ref.shape
    heads, blocks = width // HEAD_DIM, s // QB
    c = pl.program_id(1)

    def lanes(h):
        return slice(h * HEAD_DIM, (h + 1) * HEAD_DIM)

    @pl.when(c == 0)
    def _():
        qt_ref[...] = q_ref[...].T
        dqt_ref[...] = jnp.zeros_like(dqt_ref)
        for i in range(blocks):
            at = slice(i * QB, (i + 1) * QB)
            dot = do_ref[at, :].astype(F32).T
            dot_ref[:, at] = dot.astype(BF)
            both = dot * o_ref[at, :].astype(F32).T
            for h in range(heads):
                delta_ref[h : h + 1, at] = jnp.sum(both[lanes(h)], axis=0, keepdims=True)

    def run(n, queries):
        bias = same_segment(col_ref[...], row_ref[0:1, queries])
        dks, dvs = [None] * heads, [None] * heads

        def products(h, _):
            return (
                nn(k_ref[:, lanes(h)], qt_ref[lanes(h), queries]) + bias,
                nn(v_ref[:, lanes(h)], dot_ref[lanes(h), queries]),
            )

        def scores(h, a):
            p = jnp.exp(a[0] - lse_ref[h : h + 1, queries])
            return p.astype(BF), (p * (a[1] - delta_ref[h : h + 1, queries])).astype(BF)

        def grads(h, a):
            dvs[h] = nt(dot_ref[lanes(h), queries], a[0])
            dks[h] = nt(qt_ref[lanes(h), queries], a[1])
            dqt_ref[lanes(h), queries] += nn(k_ref[:, lanes(h)].T, a[1])

        staged(heads, [products, scores, grads])
        here = pl.ds(pl.multiple_of(c * QB, QB), QB)
        cos, sin = cos_ref[here, :], sin_ref[here, :]
        for b in range(width // LANES):
            dk = jnp.concatenate(dks[2 * b : 2 * b + 2], 0).T
            dv = jnp.concatenate(dvs[2 * b : 2 * b + 2], 0).T
            dkv_ref[:, b * LANES : (b + 1) * LANES] = rotate(dk, cos, sin, -1).astype(BF)
            dkv_ref[:, width + b * LANES : width + (b + 1) * LANES] = dv.astype(BF)

    by_range(ranges, blocks, run)

    @pl.when(c == blocks - 1)
    def _():
        for i in range(blocks):
            at = slice(i * QB, (i + 1) * QB)
            for b in range(width // LANES):
                cols = slice(b * LANES, (b + 1) * LANES)
                dq = dqt_ref[cols, at].T * HEAD_DIM**-0.5
                dq_ref[at, cols] = rotate(dq, cos_ref[at, :], sin_ref[at, :], -1).astype(BF)


def attend_back_call(ranges, col, row, qkv, do, o, lse, cos, sin):
    _, s, w3 = qkv.shape
    width = w3 // 3
    whole = pl.BlockSpec((None, s, width), lambda r, c, g: (r, 0, 0))
    table = pl.BlockSpec((s, LANES), lambda r, c, g: (0, 0))

    def block(n):
        return pl.BlockSpec((None, QB, width), lambda r, c, g: (r, c, n))

    return call(
        attend_back_kernel,
        "attend_back",
        (2, s // QB),
        [
            pl.BlockSpec((QB, LANES), lambda r, c, g: (c, 0)),
            pl.BlockSpec((8, s), lambda r, c, g: (0, 0)),
            whole,
            block(1),
            block(2),
            whole,
            whole,
            pl.BlockSpec((None, 8, s), lambda r, c, g: (r, 0, 0)),
            table,
            table,
        ],
        [whole, pl.BlockSpec((None, QB, 2 * width), lambda r, c, g: (r, c, 0))],
        [jax.ShapeDtypeStruct((2, s, width), BF), jax.ShapeDtypeStruct((2, s, 2 * width), BF)],
        [
            pltpu.VMEM((width, s), BF),
            pltpu.VMEM((width, s), BF),
            pltpu.VMEM((width, s), F32),
            pltpu.VMEM((8, s), F32),
        ],
    )(ranges, col, row, qkv, qkv, qkv, do, o, lse, cos, sin)


def mlp_kernel(info, *refs, layout, rows, width, units, half):
    n = len(layout)
    (x_ref, xr_ref, dy_ref, dyr_ref, o_ref, gain_ref,
     own_ref, other_ref, dr_ref, do_ref, h_ref, dyo_ref, da_ref, dgu_ref, m_ref, gg_ref,
     w_ref, sems) = refs[n:]
    own = own_block(info, half)

    @pl.when(pl.program_id(0) == 0)
    def _():
        load_weights(info, refs[:n], layout, rows, w_ref, sems)
        gg_ref[...] = jnp.zeros_like(gg_ref)

    c0, c1, c2, c3 = width, width + units, width + 2 * units, width + 3 * units
    gain = gain_ref[1:2, :]
    x = jnp.where(own, x_ref[...], xr_ref[...]).astype(F32)
    dyb = jnp.where(own, dy_ref[...], dyr_ref[...])
    dyo_ref[...] = dyb
    dy = dyb.astype(F32)
    r1 = x + nt(o_ref[0], w_ref[0, :, :c0]) + nt(o_ref[1], w_ref[1, :, :c0])
    xhat, inverse = norm(r1)
    h = (xhat * gain).astype(BF)
    h_ref[...] = h
    out, dh = 0.0, 0.0
    for r in range(2):
        gate = nn(h, w_ref[r, :, c0:c1])
        up = nn(h, w_ref[r, :, c1:c2])
        dm = nn(dyb, w_ref[r, :, c2:c3])
        phi = 0.5 + 0.5 * lax.erf(gate * 0.7071067811865476)
        density = jnp.exp(-0.5 * gate * gate) * 0.3989422804014327
        gelu = gate * phi
        m = (gelu * up).astype(BF)
        dgate = (dm * up * (phi + gate * density)).astype(BF)
        dup = (dm * gelu).astype(BF)
        m_ref[r] = m
        dgu_ref[r, :, :units] = dgate
        dgu_ref[r, :, units:] = dup
        out = out + nt(m, w_ref[r, :, c2:c3])
        dh = dh + nt(dgate, w_ref[r, :, c0:c1]) + nt(dup, w_ref[r, :, c1:c2])
    out = (r1 + out).astype(BF)

    @pl.when(own)
    def _():
        own_ref[...] = out

    @pl.when(jnp.logical_not(own))
    def _():
        other_ref[...] = out

    gg_ref[0:1, :] += jnp.sum(dh * xhat, axis=0, keepdims=True)
    dr = dy + norm_back(dh, xhat, inverse, gain)
    dr_ref[...] = dr
    da = dr.astype(BF)
    da_ref[...] = da
    for r in range(2):
        do_ref[r] = nn(da, w_ref[r, :, :c0]).astype(BF)


def mlp_call(info, pieces, layout, rows, width, units, x, xr, dy, dyr, o, gains):
    d, s = x.shape[2], o.shape[1]
    half = s // TB // 2
    held, received, block, own, other = token_specs(d, half)

    def pair(w):
        return pl.BlockSpec((2, TB, w), lambda b, i: (0, b, 0))

    row = pl.BlockSpec((8, d), lambda b, i: (0, 0))
    return call(
        functools.partial(mlp_kernel, layout=layout, rows=rows, width=width, units=units, half=half),
        "mlp",
        (s // TB,),
        [ANY] * len(layout) + [held, received, held, received, pair(width), row],
        [own, other, block, pair(width), block, block, block, pair(2 * units), pair(units), row],
        [
            jax.ShapeDtypeStruct((s // 2, d), BF),
            jax.ShapeDtypeStruct((s // 2, d), BF),
            jax.ShapeDtypeStruct((s, d), F32),
            jax.ShapeDtypeStruct((2, s, width), BF),
            jax.ShapeDtypeStruct((s, d), BF),
            jax.ShapeDtypeStruct((s, d), BF),
            jax.ShapeDtypeStruct((s, d), BF),
            jax.ShapeDtypeStruct((2, s, 2 * units), BF),
            jax.ShapeDtypeStruct((2, s, units), BF),
            jax.ShapeDtypeStruct((8, d), F32),
        ],
        [pltpu.VMEM((2, d, width + 3 * units), BF), pltpu.SemaphoreType.DMA((copies_of(layout),))],
    )(info, *pieces, x, xr, dy, dyr, o, gains)


def weight_grad_kernel(info, *refs, products, orders, rows):
    n = 1 + max(max(a, b) for a, b, _ in products)
    outs, g_ref = refs[n : n + 2], refs[n + 2]
    for a, b, col in products:
        left, right = refs[a], refs[b]
        for first, out_ref, order, base in zip((0, 1), outs, orders, (0, outs[0].shape[1])):
            start, stop = max(col, base), min(col + right.shape[1], base + out_ref.shape[1])
            if start >= stop:
                continue
            value = g_ref.at[:, pl.ds(0, stop - start)]
            value[...] = tn(left[...], right[:, start - col : stop - col])
            store_rows(info, value, out_ref, slice(start - base, stop - base), order, rows)


def weight_grad_call(name, info, rows, orders, operands, products, split, total):
    specs, arrays = [], []
    for array, lead in operands:
        arrays.append(array)
        if lead is None:
            specs.append(pl.BlockSpec(array.shape, lambda g, i: (0, 0)))
        else:
            specs.append(pl.BlockSpec((None,) + array.shape[1:], lambda g, i, lead=lead: (lead, 0, 0)))
    d = operands[0][0].shape[-1]
    widest = max(a.shape[-1] for a in arrays)
    shapes = [(d, split), (d, total - split)]
    return call(
        functools.partial(weight_grad_kernel, products=products, orders=orders, rows=rows),
        name,
        (1,),
        specs,
        [pl.BlockSpec(shape, lambda g, i: (0, 0)) for shape in shapes],
        [jax.ShapeDtypeStruct(shape, BF) for shape in shapes],
        [pltpu.VMEM((d, widest), F32)],
    )(info, *arrays)


def input_kernel(info, *refs, layout, rows, width, half, order):
    n = len(layout)
    (x_ref, xr_ref, dq_ref, dkv_ref, dr_ref, gain_ref, gg_ref,
     own_ref, other_ref, gcol_ref, w_ref, acc_ref, col_ref, sems) = refs[n:]
    own = own_block(info, half)

    @pl.when(pl.program_id(0) == 0)
    def _():
        load_weights(info, refs[:n], layout, rows, w_ref, sems)
        acc_ref[...] = jnp.zeros_like(acc_ref)
        acc_ref[1:2, :] = gg_ref[0:1, :]

    gain = gain_ref[0:1, :]
    x = jnp.where(own, x_ref[...], xr_ref[...]).astype(F32)
    xhat, inverse = norm(x)
    dh = 0.0
    for r in range(2):
        dh = dh + nt(dq_ref[r], w_ref[r, :, :width]) + nt(dkv_ref[r], w_ref[r, :, width : 3 * width])
    acc_ref[0:1, :] += jnp.sum(dh * xhat, axis=0, keepdims=True)
    grad = dr_ref[...] + norm_back(dh, xhat, inverse, gain)

    @pl.when(own)
    def _():
        own_ref[...] = grad

    @pl.when(jnp.logical_not(own))
    def _():
        other_ref[...] = grad

    @pl.when(pl.program_id(0) == pl.num_programs(0) - 1)
    def _():
        col_ref[...] = acc_ref[...].T
        store_rows(info, col_ref, gcol_ref, slice(0, LANES), order, rows)


def input_call(info, pieces, layout, rows, width, x, xr, dq, dkv, dr, gains, gg, order):
    d, s = x.shape[2], dq.shape[1]
    half = s // TB // 2
    held, received, block, own, other = token_specs(d, half)

    def pair(w):
        return pl.BlockSpec((2, TB, w), lambda b, i: (0, b, 0))

    row = pl.BlockSpec((8, d), lambda b, i: (0, 0))
    return call(
        functools.partial(input_kernel, layout=layout, rows=rows, width=width, half=half, order=order),
        "input_back",
        (s // TB,),
        [ANY] * len(layout) + [held, received, pair(width), pair(2 * width), block, row, row],
        [own, other, pl.BlockSpec((d, LANES), lambda b, i: (0, 0))],
        [
            jax.ShapeDtypeStruct((s // 2, d), F32),
            jax.ShapeDtypeStruct((s // 2, d), F32),
            jax.ShapeDtypeStruct((d, LANES), BF),
        ],
        [
            pltpu.VMEM((2, d, 3 * width + LANES), BF),
            pltpu.VMEM((LANES, d), F32),
            pltpu.VMEM((d, LANES), F32),
            pltpu.SemaphoreType.DMA((copies_of(layout),)),
        ],
    )(info, *pieces, x, xr, dq, dkv, dr, gains, gg)


def swap(x):
    return lax.ppermute(x, "tensor", [(0, 1), (1, 0)])


def peer(x, k):
    return lax.ppermute(x, "dp", [(i, i ^ k) for i in range(16)])


def gather(slab, split, cube):
    if not cube:
        whole = lax.all_gather(slab, "dp", axis=0, tiled=True)
        return [whole, swap(whole)], [(0, 0, None), (1, 0, None)]
    block = jnp.concatenate([slab] + [peer(slab, k) for k in (4, 8, 12)], 0)
    a, b = block[:, :split], block[:, split:]
    a = jnp.concatenate([a, peer(a, 1)], 0)
    b = jnp.concatenate([b, peer(b, 2)], 0)
    own = [a, b, peer(a, 2), peer(b, 1)]
    where = [
        (0, ORDER_A[:8]),
        (split, ORDER_B[:8]),
        (0, ORDER_A[8:]),
        (split, ORDER_B[8:]),
    ]
    layout = [(r, col, order) for r in range(2) for col, order in where]
    return own + [swap(p) for p in own], layout


def add(*terms):
    return functools.reduce(jnp.add, [t.astype(F32) for t in terms])


def scatter(a, b, cube):
    if not cube:
        both = jnp.concatenate([add(*a), add(*b)], 1)
        return lax.psum_scatter(both, "dp", scatter_dimension=0, tiled=True)
    n = a[0].shape[0] // 2
    ra = peer(add(*(t[n:] for t in a)).astype(BF), 2)
    rb = peer(add(*(t[n:] for t in b)).astype(BF), 1)
    a, b = [t[:n] for t in a] + [ra], [t[:n] for t in b] + [rb]
    n = n // 2
    ra = peer(add(*(t[n:] for t in a)).astype(BF), 1)
    rb = peer(add(*(t[n:] for t in b)).astype(BF), 2)
    both = jnp.concatenate([add(*(t[:n] for t in a), ra[:n]), add(*(t[:n] for t in b), rb[:n])], 1)
    n = n // 4
    send = both.astype(BF)
    got = [peer(send[i * n : (i + 1) * n], 4 * i) for i in (1, 2, 3)]
    return add(both[:n], *got)


def local(
    hidden_in, segment_ids, qkv_weight, out_weight, mlp_weight, down_weight, attn_gain, mlp_gain,
    cotangent, *, cube,
):
    t, me = lax.axis_index("tensor"), lax.axis_index("dp")
    info = jnp.stack([t, me]).astype(jnp.int32)
    rows, width = qkv_weight.shape[1:]
    d = hidden_in.shape[2]
    units_here = mlp_weight.shape[2]
    units = up_to(units_here)
    s = segment_ids.shape[1]

    def other_half(x):
        return swap(lax.dynamic_index_in_dim(x, 1 - t, 0, False))

    def placed(own, got):
        first = t == 0
        return jnp.stack([jnp.where(first, own, got), jnp.where(first, got, own)])

    x_recv = other_half(hidden_in)
    gain_cols = jnp.stack([attn_gain, mlp_gain], 1)
    gain_cols = jnp.pad(gain_cols, ((0, 0), (0, LANES - 2)))
    slab1 = jnp.concatenate([qkv_weight[0], qkv_weight[1], qkv_weight[2], gain_cols], 1)

    def wide(w):
        return jnp.pad(w, ((0, 0), (0, units - units_here)))

    slab2 = jnp.concatenate(
        [out_weight.T, wide(mlp_weight[0]), wide(mlp_weight[1]), wide(down_weight.T)], 1
    )
    total1, total2 = slab1.shape[1], slab2.shape[1]
    split1, split2 = total1 // 2 // LANES * LANES, total2 // 2 // LANES * LANES
    w1, layout1 = gather(slab1, split1, cube)
    w2, layout2 = gather(slab2, split2, cube)
    dy_recv = other_half(cotangent)

    seg = lax.dynamic_index_in_dim(segment_ids, t, 0, False)
    index = jnp.arange(s, dtype=jnp.int32)
    start = jnp.sum((seg[None, :] < seg[:, None]).astype(jnp.int32), axis=1)
    freqs = THETA ** (-2.0 * jnp.arange(HEAD_DIM // 2, dtype=F32) / HEAD_DIM)
    angles = (index - start).astype(F32)[:, None] * freqs[None, :]
    cos, sin = jnp.cos(angles), jnp.sin(angles)
    cos = jnp.concatenate([cos, cos, cos, cos], 1)
    sin = jnp.concatenate([-sin, sin, -sin, sin], 1)
    col = jnp.broadcast_to(seg[:, None], (s, LANES))
    row = jnp.broadcast_to(seg[None, :], (8, s))
    ends = seg.reshape(s // QB, QB)
    first, last = ends[:, 0], ends[:, -1]
    meet = (first[:, None] <= last[None, :]) & (first[None, :] <= last[:, None])
    block = jnp.arange(s // QB, dtype=jnp.int32)[None, :]
    low = jnp.min(jnp.where(meet, block, s), axis=1)
    high = jnp.max(jnp.where(meet, block, -1), axis=1)
    ranges = jnp.stack([low * QB, high - low + 1], 1).astype(jnp.int32)

    qkv, h1, gains = qkv_call(info, w1, layout1, rows, width, hidden_in, x_recv, cos, sin)
    o, lse = attend_call(ranges, col, row, qkv)
    out_own, out_other, dr, do, h2, dy, da, dgu, m, gg = mlp_call(
        info, w2, layout2, rows, width, units, hidden_in, x_recv, cotangent, dy_recv, o, gains
    )
    layer_out = placed(out_own, swap(out_other))

    orders = (ORDER_A, ORDER_B) if cube else (None, None)

    def grads2(r):
        return weight_grad_call(
            "mlp_weight_grad", info, rows, orders,
            [(da, None), (h2, None), (dy, None), (o, r), (dgu, r), (m, r)],
            [(0, 3, 0), (1, 4, width), (2, 5, width + 2 * units)], split2, total2,
        )

    theirs = [swap(g) for g in grads2(1)]
    mine = grads2(0)
    sum2 = scatter((mine[0], theirs[0]), (mine[1], theirs[1]), cube)

    dq, dkv = attend_back_call(ranges, col, row, qkv, do, o, lse, cos, sin)

    def grads1(r):
        return weight_grad_call(
            "qkv_weight_grad", info, rows, orders,
            [(h1, None), (dq, r), (dkv, r)],
            [(0, 1, 0), (0, 2, width)], split1, total1 - LANES,
        )

    theirs = [swap(g) for g in grads1(1)]
    mine = grads1(0)
    in_own, in_other, gcol = input_call(
        info, w1, layout1, rows, width, hidden_in, x_recv, dq, dkv, dr, gains, gg, orders[1]
    )
    input_grad = placed(in_own, swap(in_other))
    gcol_got = swap(gcol)
    sum1 = scatter(
        (mine[0], theirs[0]),
        (
            jnp.concatenate([mine[1], gcol], 1),
            jnp.concatenate([theirs[1], gcol_got], 1),
        ),
        cube,
    )
    qkv_grad = sum1[:, : 3 * width].reshape(rows, 3, width).transpose(1, 0, 2)
    c = width
    proj_grad = sum2[:, :c].T
    mlp_grad = jnp.stack([sum2[:, c : c + units_here], sum2[:, c + units : c + units + units_here]])
    down_grad = sum2[:, c + 2 * units : c + 2 * units + units_here].T
    return (
        layer_out,
        input_grad,
        qkv_grad,
        proj_grad,
        mlp_grad,
        down_grad,
        sum1[:, 3 * width],
        sum1[:, 3 * width + 1],
    )


def solution(mesh):
    rows = P(None, ("dp", "tensor"), None)
    in_specs = (
        rows,
        P(None, "dp"),
        P(None, "dp", "tensor"),
        P("tensor", "dp"),
        P(None, "dp", "tensor"),
        P("tensor", "dp"),
        P("dp"),
        P("dp"),
        rows,
    )
    out_specs = (
        rows,
        rows,
        P(None, "dp", "tensor"),
        P("tensor", "dp"),
        P(None, "dp", "tensor"),
        P("tensor", "dp"),
        P("dp"),
        P("dp"),
    )
    cube = mesh.shape["dp"] == 16
    return jax.shard_map(
        functools.partial(local, cube=cube), mesh=mesh, in_specs=in_specs, out_specs=out_specs, check_vma=False
    )
```

```python
import functools

import jax
import jax.numpy as jnp
from jax import lax
from jax.experimental import pallas as pl
from jax.experimental.pallas import tpu as pltpu
from jax.sharding import PartitionSpec as P

HEAD_DIM = 64
LANES = 128
QB = 256
TB = 256
VMEM = 56 << 20
THETA = 160000.0
EPS = 1e-05
BF = jnp.bfloat16
F32 = jnp.float32

ORDER_A = (0, 4, 8, 12, 1, 5, 9, 13, 2, 6, 10, 14, 3, 7, 11, 15)
ORDER_B = (0, 4, 8, 12, 2, 6, 10, 14, 1, 5, 9, 13, 3, 7, 11, 15)


def nn(a, b):
    return lax.dot_general(a, b, (((1,), (0,)), ((), ())), preferred_element_type=F32)


def nt(a, b):
    return lax.dot_general(a, b, (((1,), (1,)), ((), ())), preferred_element_type=F32)


def tn(a, b):
    return lax.dot_general(a, b, (((0,), (0,)), ((), ())), preferred_element_type=F32)


def up_to(n):
    return -(-n // LANES) * LANES


def rotate(u, cos, sin, sign):
    lane = lax.broadcasted_iota(jnp.int32, u.shape, 1)
    half = HEAD_DIM // 2
    partner = jnp.where(
        (lane % HEAD_DIM) < half, pltpu.roll(u, LANES - half, 1), pltpu.roll(u, half, 1)
    )
    return u * cos + partner * sin if sign > 0 else u * cos - partner * sin


def norm(x):
    center = x - jnp.mean(x, axis=-1, keepdims=True)
    inverse = lax.rsqrt(jnp.mean(center * center, axis=-1, keepdims=True) + EPS)
    return center * inverse, inverse


def norm_back(grad, xhat, inverse, gain):
    z = grad * gain
    inner = z - jnp.mean(z, axis=-1, keepdims=True) - xhat * jnp.mean(z * xhat, axis=-1, keepdims=True)
    return inverse * inner


def staged(count, stages):
    live = [None] * len(stages)
    for step in range(count + len(stages) - 1):
        new = [None] * len(stages)
        for s, stage in enumerate(stages):
            if 0 <= step - s < count:
                new[s] = stage(step - s, live[s - 1] if s else None)
        live = new


def after(x, *deps):
    return lax.optimization_barrier((x, deps))[0]


def call(kernel, name, us, grid, in_specs, out_specs, out_shape, scratch=(), prefetch=1):
    return pl.pallas_call(
        kernel,
        grid_spec=pltpu.PrefetchScalarGridSpec(
            num_scalar_prefetch=prefetch,
            grid=grid,
            in_specs=in_specs,
            out_specs=out_specs,
            scratch_shapes=list(scratch),
        ),
        out_shape=out_shape,
        compiler_params=pltpu.CompilerParams(vmem_limit_bytes=VMEM),
        cost_estimate=pl.CostEstimate(flops=int(us * 1.15e9), transcendentals=0, bytes_accessed=int(us * 1e6)),
        name=name,
    )


ANY = pl.BlockSpec(memory_space=pl.ANY)


def load_weights(info, pieces, layout, rows, dest, sems):
    copies = []
    for ref, (r, col, order) in zip(pieces, layout, strict=True):
        cols = pl.ds(col, ref.shape[1])
        if order is None:
            copies.append((ref, dest.at[r, :, cols]))
            continue
        for i, k in enumerate(order):
            row = pl.multiple_of((info[1] ^ k) * rows, rows)
            copies.append((ref.at[pl.ds(i * rows, rows), :], dest.at[r, pl.ds(row, rows), cols]))
    copies = [pltpu.make_async_copy(a, b, sems.at[i]) for i, (a, b) in enumerate(copies)]
    for c in copies:
        c.start()
    for c in copies:
        c.wait()


def copies_of(layout):
    return sum(1 if order is None else len(order) for _, _, order in layout)


def store_rows(info, value_ref, out_ref, cols, order, rows):
    if order is None:
        out_ref[:, cols] = value_ref[...].astype(BF)
        return
    for i, k in enumerate(order):
        row = pl.multiple_of((info[1] ^ k) * rows, rows)
        out_ref[i * rows : (i + 1) * rows, cols] = value_ref[pl.ds(row, rows), :].astype(BF)


def own_block(info, half):
    return pl.program_id(0) // half == info[0]


def qkv_kernel(info, *refs, layout, rows, width, half):
    n = len(layout)
    pieces, (x_ref, recv_ref, cos_ref, sin_ref, qkv_ref, h_ref, gain_ref, w_ref, sems) = refs[:n], refs[n:]

    @pl.when(pl.program_id(0) == 0)
    def _():
        load_weights(info, pieces, layout, rows, w_ref, sems)
        gain_ref[...] = w_ref[0, :, 3 * width :].astype(F32).T[:8]

    x = jnp.where(own_block(info, half), x_ref[...], recv_ref[...]).astype(F32)
    xhat, _ = norm(x)
    h = (xhat * gain_ref[0:1, :]).astype(BF)
    h_ref[...] = h
    cos, sin = cos_ref[...], sin_ref[...]
    for r in range(2):
        raw = nn(h, w_ref[r, :, : 3 * width])
        for b in range(2 * width // LANES):
            cols = slice(b * LANES, (b + 1) * LANES)
            u = rotate(raw[:, cols], cos, sin, 1)
            if b < width // LANES:
                u = u * HEAD_DIM**-0.5
            qkv_ref[r, :, cols] = u.astype(BF)
        qkv_ref[r, :, 2 * width :] = raw[:, 2 * width :].astype(BF)


def token_specs(d, half):
    def clip(b, first):
        return jnp.clip(b - first, 0, half - 1)

    held = pl.BlockSpec((None, TB, d), lambda b, i: (i[0], b % half, 0))
    recv = pl.BlockSpec((TB, d), lambda b, i: (b % half, 0))
    rows = pl.BlockSpec((TB, d), lambda b, i: (b, 0))
    own = pl.BlockSpec((TB, d), lambda b, i: (clip(b, half * i[0]), 0))
    other = pl.BlockSpec((TB, d), lambda b, i: (clip(b, half * (1 - i[0])), 0))
    return held, recv, rows, own, other


def qkv_call(info, pieces, layout, rows, width, x, recv, cos, sin):
    d, s = x.shape[2], cos.shape[0]
    half = s // TB // 2
    held, received, block, _, _ = token_specs(d, half)
    table = pl.BlockSpec((TB, LANES), lambda b, i: (b, 0))
    cols = 3 * width + LANES
    return call(
        functools.partial(qkv_kernel, layout=layout, rows=rows, width=width, half=half),
        "qkv",
        12,
        (s // TB,),
        [ANY] * len(layout) + [held, received, table, table],
        [
            pl.BlockSpec((2, TB, 3 * width), lambda b, i: (0, b, 0)),
            block,
            pl.BlockSpec((8, d), lambda b, i: (0, 0)),
        ],
        [
            jax.ShapeDtypeStruct((2, s, 3 * width), BF),
            jax.ShapeDtypeStruct((s, d), BF),
            jax.ShapeDtypeStruct((8, d), F32),
        ],
        [pltpu.VMEM((2, d, cols), BF), pltpu.SemaphoreType.DMA((copies_of(layout),))],
    )(info, *pieces, x, recv, cos, sin)


def same_segment(col, row):
    parts = [
        jnp.where(col == row[:, i * LANES : (i + 1) * LANES], 0.0, -1e30).astype(F32)
        for i in range(row.shape[1] // LANES)
    ]
    return jnp.concatenate(parts, 1)


def by_range(ranges, blocks, run):
    i = pl.program_id(1)
    for n in range(1, blocks + 1):

        @pl.when(ranges[i, 1] == n)
        def _(n=n):
            run(n, pl.ds(pl.multiple_of(ranges[i, 0], QB) if n < blocks else 0, n * QB))


def attend_kernel(ranges, col_ref, row_ref, q_ref, k_ref, v_ref, o_ref, lse_ref, vt_ref):
    s, width = k_ref.shape
    heads = width // HEAD_DIM

    @pl.when(pl.program_id(1) == 0)
    def _():
        vt_ref[...] = v_ref[...].T

    def run(n, keys):
        bias = same_segment(col_ref[keys, :], row_ref[0:1, :])
        outs = [None] * heads

        def lanes(h):
            return slice(h * HEAD_DIM, (h + 1) * HEAD_DIM)

        def scores(h, _):
            x = nn(k_ref[keys, lanes(h)], q_ref[:, lanes(h)].T) + bias
            return x, jnp.max(x, axis=0, keepdims=True)

        def expo(h, a):
            e = jnp.exp(a[0] - a[1])
            return e.astype(BF), jnp.sum(e, axis=0, keepdims=True), a[1]

        def out(h, a):
            outs[h] = nn(vt_ref[lanes(h), keys], a[0]) * (1.0 / a[1])
            lse_ref[h : h + 1, :] = a[2] + jnp.log(a[1])

        staged(heads, [scores, expo, out])
        o_ref[...] = jnp.concatenate(outs, axis=0).T.astype(BF)

    by_range(ranges, s // QB, run)


def attend_call(ranges, col, row, qkv):
    _, s, w3 = qkv.shape
    width = w3 // 3

    def whole(c):
        return pl.BlockSpec((None, s, width), lambda r, i, g: (r, 0, c))

    block = pl.BlockSpec((None, QB, width), lambda r, i, g: (r, i, 0))
    return call(
        attend_kernel,
        "attend",
        20,
        (2, s // QB),
        [
            pl.BlockSpec((s, LANES), lambda r, i, g: (0, 0)),
            pl.BlockSpec((8, QB), lambda r, i, g: (0, i)),
            block,
            whole(1),
            whole(2),
        ],
        [block, pl.BlockSpec((None, 8, QB), lambda r, i, g: (r, 0, i))],
        [jax.ShapeDtypeStruct((2, s, width), BF), jax.ShapeDtypeStruct((2, 8, s), F32)],
        [pltpu.VMEM((width, s), BF)],
    )(ranges, col, row, qkv, qkv, qkv)


def attend_back_kernel(
    ranges, col_ref, row_ref, q_ref, k_ref, v_ref, do_ref, o_ref, lse_ref, cos_ref, sin_ref,
    dq_ref, dkv_ref, qt_ref, dot_ref, dqt_ref, delta_ref,
):
    s, width = q_ref.shape
    heads, blocks = width // HEAD_DIM, s // QB
    c = pl.program_id(1)

    def lanes(h):
        return slice(h * HEAD_DIM, (h + 1) * HEAD_DIM)

    @pl.when(c == 0)
    def _():
        qt_ref[...] = q_ref[...].T
        dqt_ref[...] = jnp.zeros_like(dqt_ref)
        for i in range(blocks):
            at = slice(i * QB, (i + 1) * QB)
            dot = do_ref[at, :].astype(F32).T
            dot_ref[:, at] = dot.astype(BF)
            both = dot * o_ref[at, :].astype(F32).T
            for h in range(heads):
                delta_ref[h : h + 1, at] = jnp.sum(both[lanes(h)], axis=0, keepdims=True)

    def run(n, queries):
        bias = same_segment(col_ref[...], row_ref[0:1, queries])
        dks, dvs = [None] * heads, [None] * heads

        def products(h, _):
            return (
                nn(k_ref[:, lanes(h)], qt_ref[lanes(h), queries]) + bias,
                nn(v_ref[:, lanes(h)], dot_ref[lanes(h), queries]),
            )

        def scores(h, a):
            p = jnp.exp(a[0] - lse_ref[h : h + 1, queries])
            return p.astype(BF), (p * (a[1] - delta_ref[h : h + 1, queries])).astype(BF)

        def grads(h, a):
            dvs[h] = nt(dot_ref[lanes(h), queries], a[0])
            dks[h] = nt(qt_ref[lanes(h), queries], a[1])
            dqt_ref[lanes(h), queries] += nn(k_ref[:, lanes(h)].T, a[1])

        staged(heads, [products, scores, grads])
        here = pl.ds(pl.multiple_of(c * QB, QB), QB)
        cos, sin = cos_ref[here, :], sin_ref[here, :]
        for b in range(width // LANES):
            dk = jnp.concatenate(dks[2 * b : 2 * b + 2], 0).T
            dv = jnp.concatenate(dvs[2 * b : 2 * b + 2], 0).T
            dkv_ref[:, b * LANES : (b + 1) * LANES] = rotate(dk, cos, sin, -1).astype(BF)
            dkv_ref[:, width + b * LANES : width + (b + 1) * LANES] = dv.astype(BF)

    by_range(ranges, blocks, run)

    @pl.when(c == blocks - 1)
    def _():
        for i in range(blocks):
            at = slice(i * QB, (i + 1) * QB)
            for b in range(width // LANES):
                cols = slice(b * LANES, (b + 1) * LANES)
                dq = dqt_ref[cols, at].T * HEAD_DIM**-0.5
                dq_ref[at, cols] = rotate(dq, cos_ref[at, :], sin_ref[at, :], -1).astype(BF)


def attend_back_call(r, ranges, col, row, qkv, do, o, lse, cos, sin):
    _, s, w3 = qkv.shape
    width = w3 // 3
    whole = pl.BlockSpec((None, s, width), lambda _, c, g: (r, 0, 0))
    table = pl.BlockSpec((s, LANES), lambda _, c, g: (0, 0))

    def block(n):
        return pl.BlockSpec((None, QB, width), lambda _, c, g: (r, c, n))

    return call(
        attend_back_kernel,
        "attend_back",
        18,
        (1, s // QB),
        [
            pl.BlockSpec((QB, LANES), lambda _, c, g: (c, 0)),
            pl.BlockSpec((8, s), lambda _, c, g: (0, 0)),
            whole,
            block(1),
            block(2),
            whole,
            whole,
            pl.BlockSpec((None, 8, s), lambda _, c, g: (r, 0, 0)),
            table,
            table,
        ],
        [
            pl.BlockSpec((s, width), lambda _, c, g: (0, 0)),
            pl.BlockSpec((QB, 2 * width), lambda _, c, g: (c, 0)),
        ],
        [jax.ShapeDtypeStruct((s, width), BF), jax.ShapeDtypeStruct((s, 2 * width), BF)],
        [
            pltpu.VMEM((width, s), BF),
            pltpu.VMEM((width, s), BF),
            pltpu.VMEM((width, s), F32),
            pltpu.VMEM((8, s), F32),
        ],
    )(ranges, col, row, qkv, qkv, qkv, do, o, lse, cos, sin)


def mlp_kernel(info, *refs, layout, rows, width, units, half):
    n = len(layout)
    (x_ref, xr_ref, dy_ref, dyr_ref, o_ref, gain_ref,
     own_ref, other_ref, dr_ref, do_ref, h_ref, dyo_ref, da_ref, dgu_ref, m_ref, gg_ref,
     w_ref, sems) = refs[n:]
    own = own_block(info, half)

    @pl.when(pl.program_id(0) == 0)
    def _():
        load_weights(info, refs[:n], layout, rows, w_ref, sems)
        gg_ref[...] = jnp.zeros_like(gg_ref)

    c0, c1, c2, c3 = width, width + units, width + 2 * units, width + 3 * units
    gain = gain_ref[1:2, :]
    x = jnp.where(own, x_ref[...], xr_ref[...]).astype(F32)
    dyb = jnp.where(own, dy_ref[...], dyr_ref[...])
    dyo_ref[...] = dyb
    dy = dyb.astype(F32)
    r1 = x + nt(o_ref[0], w_ref[0, :, :c0]) + nt(o_ref[1], w_ref[1, :, :c0])
    xhat, inverse = norm(r1)
    h = (xhat * gain).astype(BF)
    h_ref[...] = h
    out, dh = 0.0, 0.0
    for r in range(2):
        gate = nn(h, w_ref[r, :, c0:c1])
        up = nn(h, w_ref[r, :, c1:c2])
        dm = nn(dyb, w_ref[r, :, c2:c3])
        phi = 0.5 + 0.5 * lax.erf(gate * 0.7071067811865476)
        density = jnp.exp(-0.5 * gate * gate) * 0.3989422804014327
        gelu = gate * phi
        m = (gelu * up).astype(BF)
        dgate = (dm * up * (phi + gate * density)).astype(BF)
        dup = (dm * gelu).astype(BF)
        m_ref[r] = m
        dgu_ref[r, :, :units] = dgate
        dgu_ref[r, :, units:] = dup
        out = out + nt(m, w_ref[r, :, c2:c3])
        dh = dh + nt(dgate, w_ref[r, :, c0:c1]) + nt(dup, w_ref[r, :, c1:c2])
    out = (r1 + out).astype(BF)

    @pl.when(own)
    def _():
        own_ref[...] = out

    @pl.when(jnp.logical_not(own))
    def _():
        other_ref[...] = out

    gg_ref[0:1, :] += jnp.sum(dh * xhat, axis=0, keepdims=True)
    dr = dy + norm_back(dh, xhat, inverse, gain)
    dr_ref[...] = dr
    da = dr.astype(BF)
    da_ref[...] = da
    for r in range(2):
        do_ref[r] = nn(da, w_ref[r, :, :c0]).astype(BF)


def mlp_call(info, pieces, layout, rows, width, units, x, xr, dy, dyr, o, gains):
    d, s = x.shape[2], o.shape[1]
    half = s // TB // 2
    held, received, block, own, other = token_specs(d, half)

    def pair(w):
        return pl.BlockSpec((2, TB, w), lambda b, i: (0, b, 0))

    row = pl.BlockSpec((8, d), lambda b, i: (0, 0))
    return call(
        functools.partial(mlp_kernel, layout=layout, rows=rows, width=width, units=units, half=half),
        "mlp",
        32,
        (s // TB,),
        [ANY] * len(layout) + [held, received, held, received, pair(width), row],
        [own, other, block, pair(width), block, block, block, pair(2 * units), pair(units), row],
        [
            jax.ShapeDtypeStruct((s // 2, d), BF),
            jax.ShapeDtypeStruct((s // 2, d), BF),
            jax.ShapeDtypeStruct((s, d), F32),
            jax.ShapeDtypeStruct((2, s, width), BF),
            jax.ShapeDtypeStruct((s, d), BF),
            jax.ShapeDtypeStruct((s, d), BF),
            jax.ShapeDtypeStruct((s, d), BF),
            jax.ShapeDtypeStruct((2, s, 2 * units), BF),
            jax.ShapeDtypeStruct((2, s, units), BF),
            jax.ShapeDtypeStruct((8, d), F32),
        ],
        [pltpu.VMEM((2, d, width + 3 * units), BF), pltpu.SemaphoreType.DMA((copies_of(layout),))],
    )(info, *pieces, x, xr, dy, dyr, o, gains)


def weight_grad_kernel(info, *refs, products, orders, rows):
    n = 1 + max(max(a, b) for a, b, _ in products)
    outs, g_ref = refs[n : n + 2], refs[n + 2]
    for a, b, col in products:
        left, right = refs[a], refs[b]
        for first, out_ref, order, base in zip((0, 1), outs, orders, (0, outs[0].shape[1])):
            start, stop = max(col, base), min(col + right.shape[1], base + out_ref.shape[1])
            if start >= stop:
                continue
            value = g_ref.at[:, pl.ds(0, stop - start)]
            value[...] = tn(left[...], right[:, start - col : stop - col])
            store_rows(info, value, out_ref, slice(start - base, stop - base), order, rows)


def weight_grad_call(name, us, info, rows, orders, operands, products, split, total):
    specs, arrays = [], []
    for array, lead in operands:
        arrays.append(array)
        if lead is None:
            specs.append(pl.BlockSpec(array.shape, lambda g, i: (0, 0)))
        else:
            specs.append(pl.BlockSpec((None,) + array.shape[1:], lambda g, i, lead=lead: (lead, 0, 0)))
    d = operands[0][0].shape[-1]
    widest = max(a.shape[-1] for a in arrays)
    shapes = [(d, split), (d, total - split)]
    return call(
        functools.partial(weight_grad_kernel, products=products, orders=orders, rows=rows),
        name,
        us,
        (1,),
        specs,
        [pl.BlockSpec(shape, lambda g, i: (0, 0)) for shape in shapes],
        [jax.ShapeDtypeStruct(shape, BF) for shape in shapes],
        [pltpu.VMEM((d, widest), F32)],
    )(info, *arrays)


def input_kernel(info, *refs, layout, rows, width, half, order):
    n = len(layout)
    (x_ref, xr_ref, dq0_ref, dkv0_ref, dq1_ref, dkv1_ref, dr_ref, gain_ref, gg_ref,
     own_ref, other_ref, gcol_ref, w_ref, acc_ref, col_ref, sems) = refs[n:]
    own = own_block(info, half)

    @pl.when(pl.program_id(0) == 0)
    def _():
        load_weights(info, refs[:n], layout, rows, w_ref, sems)
        acc_ref[...] = jnp.zeros_like(acc_ref)
        acc_ref[1:2, :] = gg_ref[0:1, :]

    gain = gain_ref[0:1, :]
    x = jnp.where(own, x_ref[...], xr_ref[...]).astype(F32)
    xhat, inverse = norm(x)
    dh = 0.0
    for r, dq_ref, dkv_ref in ((0, dq0_ref, dkv0_ref), (1, dq1_ref, dkv1_ref)):
        dh = dh + nt(dq_ref[...], w_ref[r, :, :width])
        dh = dh + nt(dkv_ref[...], w_ref[r, :, width : 3 * width])
    acc_ref[0:1, :] += jnp.sum(dh * xhat, axis=0, keepdims=True)
    grad = dr_ref[...] + norm_back(dh, xhat, inverse, gain)

    @pl.when(own)
    def _():
        own_ref[...] = grad

    @pl.when(jnp.logical_not(own))
    def _():
        other_ref[...] = grad

    @pl.when(pl.program_id(0) == pl.num_programs(0) - 1)
    def _():
        col_ref[...] = acc_ref[...].T
        store_rows(info, col_ref, gcol_ref, slice(0, LANES), order, rows)


def input_call(info, pieces, layout, rows, width, x, xr, draw, dr, gains, gg, order):
    d, s = x.shape[2], dr.shape[0]
    half = s // TB // 2
    held, received, block, own, other = token_specs(d, half)
    dq, dkv = [pl.BlockSpec((TB, w), lambda b, i: (b, 0)) for w in (width, 2 * width)]
    row = pl.BlockSpec((8, d), lambda b, i: (0, 0))
    return call(
        functools.partial(input_kernel, layout=layout, rows=rows, width=width, half=half, order=order),
        "input_back",
        13,
        (s // TB,),
        [ANY] * len(layout) + [held, received, dq, dkv, dq, dkv, block, row, row],
        [own, other, pl.BlockSpec((d, LANES), lambda b, i: (0, 0))],
        [
            jax.ShapeDtypeStruct((s // 2, d), F32),
            jax.ShapeDtypeStruct((s // 2, d), F32),
            jax.ShapeDtypeStruct((d, LANES), BF),
        ],
        [
            pltpu.VMEM((2, d, 3 * width + LANES), BF),
            pltpu.VMEM((LANES, d), F32),
            pltpu.VMEM((d, LANES), F32),
            pltpu.SemaphoreType.DMA((copies_of(layout),)),
        ],
    )(info, *pieces, x, xr, *draw, dr, gains, gg)


def swap(x):
    return lax.ppermute(x, "tensor", [(0, 1), (1, 0)])


def peer(x, k):
    return lax.ppermute(x, "dp", [(i, i ^ k) for i in range(16)])


def under(x, run, *sends):
    x, arrays = after((x, [a for _, a in sends]))
    got = [f(a) for (f, _), a in zip(sends, arrays)]
    return after((run(x), got))


def to(k):
    return lambda x: peer(x, k)


def add(*terms):
    return functools.reduce(jnp.add, [t.astype(F32) for t in terms])


class Gather:
    def __init__(self, split):
        self.split = split

    def first(self, slab):
        return [(to(k), slab) for k in (4, 8, 12)]

    def near(self, slab, got):
        block = jnp.concatenate([slab, *got], 0)
        self.ab = block[:, : self.split], block[:, self.split :]
        return [(to(k), x) for k, x in zip((1, 2), self.ab)]

    def far(self, got):
        self.ab = [jnp.concatenate(x, 0) for x in zip(self.ab, got)]
        return [(to(k), x) for k, x in zip((2, 1), self.ab)]

    def pieces(self, got, theirs, got_theirs):
        where = [(0, ORDER_A[:8]), (self.split, ORDER_B[:8]), (0, ORDER_A[8:]), (self.split, ORDER_B[8:])]
        layout = [(r, col, order) for r in range(2) for col, order in where]
        return [*self.ab, *got, *theirs, *got_theirs], layout


def half_sends(terms, ks):
    n = terms[0][0].shape[0] // 2
    keep = [[t[:n] for t in ts] for ts in terms]
    return keep, [(to(k), add(*(t[n:] for t in ts)).astype(BF)) for k, ts in zip(ks, terms)]


def joined(keep, got):
    return [ts + [g] for ts, g in zip(keep, got)]


def last_sends(terms):
    both = jnp.concatenate([add(*ts) for ts in terms], 1)
    n = both.shape[0] // 4
    send = both[n:].astype(BF)
    return both[:n], [(to(4 * i), send[(i - 1) * n : i * n]) for i in (1, 2, 3)]


def gather_plain(slab):
    whole = lax.all_gather(slab, "dp", axis=0, tiled=True)
    return [whole, swap(whole)], [(0, 0, None), (1, 0, None)]


def scatter_plain(a, b):
    both = jnp.concatenate([add(*a), add(*b)], 1)
    return lax.psum_scatter(both, "dp", scatter_dimension=0, tiled=True)


def local(
    hidden_in, segment_ids, qkv_weight, out_weight, mlp_weight, down_weight, attn_gain, mlp_gain,
    cotangent, *, cube,
):
    t, me = lax.axis_index("tensor"), lax.axis_index("dp")
    info = jnp.stack([t, me]).astype(jnp.int32)
    rows, width = qkv_weight.shape[1:]
    d = hidden_in.shape[2]
    units_here = mlp_weight.shape[2]
    units = up_to(units_here)
    s = segment_ids.shape[1]

    def placed(own, got):
        first = t == 0
        return jnp.stack([jnp.where(first, own, got), jnp.where(first, got, own)])

    def other(x):
        return lax.dynamic_index_in_dim(x, 1 - t, 0, False)

    x_recv = swap(other(hidden_in))
    gain_cols = jnp.stack([attn_gain, mlp_gain], 1)
    gain_cols = jnp.pad(gain_cols, ((0, 0), (0, LANES - 2)))
    slab1 = jnp.concatenate([qkv_weight[0], qkv_weight[1], qkv_weight[2], gain_cols], 1)

    def wide(w):
        return jnp.pad(w, ((0, 0), (0, units - units_here)))

    slab2 = jnp.concatenate(
        [out_weight.T, wide(mlp_weight[0]), wide(mlp_weight[1]), wide(down_weight.T)], 1
    )
    total1, total2 = slab1.shape[1], slab2.shape[1]
    split1, split2 = total1 // 2 // LANES * LANES, total2 // 2 // LANES * LANES
    seg = lax.dynamic_index_in_dim(segment_ids, t, 0, False)
    index = jnp.arange(s, dtype=jnp.int32)
    start = jnp.sum((seg[None, :] < seg[:, None]).astype(jnp.int32), axis=1)
    freqs = THETA ** (-2.0 * jnp.arange(HEAD_DIM // 2, dtype=F32) / HEAD_DIM)
    angles = (index - start).astype(F32)[:, None] * freqs[None, :]
    cos, sin = jnp.cos(angles), jnp.sin(angles)
    cos = jnp.concatenate([cos, cos, cos, cos], 1)
    sin = jnp.concatenate([-sin, sin, -sin, sin], 1)
    col = jnp.broadcast_to(seg[:, None], (s, LANES))
    row = jnp.broadcast_to(seg[None, :], (8, s))
    ends = seg.reshape(s // QB, QB)
    first, last = ends[:, 0], ends[:, -1]
    meet = (first[:, None] <= last[None, :]) & (first[None, :] <= last[:, None])
    block = jnp.arange(s // QB, dtype=jnp.int32)[None, :]
    low = jnp.min(jnp.where(meet, block, s), axis=1)
    high = jnp.max(jnp.where(meet, block, -1), axis=1)
    ranges = jnp.stack([low * QB, high - low + 1], 1).astype(jnp.int32)

    def project(w1):
        return qkv_call(info, w1, layout1, rows, width, hidden_in, x_recv, cos, sin)

    def attend(qkv):
        return attend_call(ranges, col, row, qkv)

    if cube:
        g1, g2 = Gather(split1), Gather(split2)
        got = [f(x) for f, x in g1.first(slab1)]
        sends = g1.near(slab1, got)
        slab2, near = after((slab2, [x for _, x in sends]))
        g1.ab = near
        got = [f(x) for (f, _), x in zip(sends, near)]
        got2 = [f(x) for f, x in g2.first(slab2)]
        sends = g1.far(got)
        theirs = [swap(x) for _, x in sends]
        got = [f(x) for f, x in sends]
        w1, layout1 = g1.pieces(got, theirs, [swap(x) for x in got])
        (qkv, h1, gains), (*got, dy_recv) = under(
            w1, project, *g2.near(slab2, got2), (swap, other(cotangent))
        )
        far = g2.far(got)
        (o, lse), got = under(qkv, attend, *far, *((swap, x) for _, x in far))
        w2, layout2 = g2.pieces(got[:2], got[2:], [swap(x) for x in got[:2]])
    else:
        w1, layout1 = gather_plain(slab1)
        w2, layout2 = gather_plain(slab2)
        dy_recv = swap(other(cotangent))
        qkv, h1, gains = project(w1)
        o, lse = attend(qkv)
    out_own, out_other, dr, do, h2, dy, da, dgu, m, gg = mlp_call(
        info, w2, layout2, rows, width, units, hidden_in, x_recv, cotangent, dy_recv, o, gains
    )
    orders = (ORDER_A, ORDER_B) if cube else (None, None)

    def grads2(r):
        return lambda o: weight_grad_call(
            "mlp_weight_grad", 10, info, rows, orders,
            [(da, None), (h2, None), (dy, None), (o, r), (dgu, r), (m, r)],
            [(0, 3, 0), (1, 4, width), (2, 5, width + 2 * units)], split2, total2,
        )

    def grads1(draw):
        return weight_grad_call(
            "qkv_weight_grad", 6, info, rows, orders,
            [(h1, None), (draw[0], None), (draw[1], None)],
            [(0, 1, 0), (0, 2, width)], split1, total1 - LANES,
        )

    def back(r):
        return lambda do: attend_back_call(r, ranges, col, row, qkv, do, o, lse, cos, sin)

    def input_back(dr):
        return input_call(
            info, w1, layout1, rows, width, hidden_in, x_recv, (*draw0, *draw1), dr, gains, gg, orders[1]
        )

    sent = grads2(1)(o)
    mine, (*theirs, out_recv) = under(o, grads2(0), *((swap, g) for g in sent), (swap, out_other))
    layer_out = placed(out_own, out_recv)
    sums2 = [[a, b] for a, b in zip(mine, theirs)]
    if cube:
        keep, sends = half_sends(sums2, (2, 1))
        draw1, got = under(do, back(1), *sends)
        keep, sends = half_sends(joined(keep, got), (1, 2))
        do, sends2 = after((do, [x for _, x in sends]))
        sent = grads1(after(draw1, sends2))
        draw0, got = under(
            after(do, sent), back(0), *((f, x) for (f, _), x in zip(sends, sends2)), *((swap, g) for g in sent)
        )
        keep2, sends2 = last_sends(joined(keep, got[:2]))
        draw0, last = after((draw0, [x for _, x in sends2]))
        mine = grads1(draw0)
        keep, sends = half_sends([[a, b] for a, b in zip(mine, got[2:])], (2, 1))
        (in_own, in_other, gcol), got = under(
            dr, input_back, *((f, x) for (f, _), x in zip(sends2, last)), *sends
        )
        sum2 = add(keep2, *got[:3])
        n = d // 2
        gcols = gcol, swap(gcol)
        gain_sum = add(*(g[:n] for g in gcols), peer(add(*(g[n:] for g in gcols)).astype(BF), 1))
        keep = joined(keep, got[3:])
        keep, sends = half_sends([keep[0], [jnp.concatenate([add(*keep[1]), gain_sum], 1)]], (1, 2))
        got = [f(x) for f, x in sends]
        in_recv = swap(in_other)
        input_grad = placed(in_own, in_recv)
        keep, sends = last_sends(joined(keep, got))
        sum1 = add(keep, *(f(x) for f, x in sends))
    else:
        sum2 = scatter_plain(*sums2)
        draw1, draw0 = back(1)(do), back(0)(do)
        theirs = [swap(g) for g in grads1(draw1)]
        mine = grads1(draw0)
        in_own, in_other, gcol = input_back(dr)
        input_grad = placed(in_own, swap(in_other))
        b = [jnp.concatenate([g, c], 1) for g, c in zip((mine[1], theirs[1]), (gcol, swap(gcol)))]
        sum1 = scatter_plain((mine[0], theirs[0]), b)
    qkv_grad = sum1[:, : 3 * width].reshape(rows, 3, width).transpose(1, 0, 2)
    c = width
    proj_grad = sum2[:, :c].T
    mlp_grad = jnp.stack([sum2[:, c : c + units_here], sum2[:, c + units : c + units + units_here]])
    down_grad = sum2[:, c + 2 * units : c + 2 * units + units_here].T
    return (
        layer_out,
        input_grad,
        qkv_grad,
        proj_grad,
        mlp_grad,
        down_grad,
        sum1[:, 3 * width],
        sum1[:, 3 * width + 1],
    )


def solution(mesh):
    rows = P(None, ("dp", "tensor"), None)
    in_specs = (
        rows,
        P(None, "dp"),
        P(None, "dp", "tensor"),
        P("tensor", "dp"),
        P(None, "dp", "tensor"),
        P("tensor", "dp"),
        P("dp"),
        P("dp"),
        rows,
    )
    out_specs = (
        rows,
        rows,
        P(None, "dp", "tensor"),
        P("tensor", "dp"),
        P(None, "dp", "tensor"),
        P("tensor", "dp"),
        P("dp"),
        P("dp"),
    )
    cube = mesh.shape["dp"] == 16
    return jax.shard_map(
        functools.partial(local, cube=cube), mesh=mesh, in_specs=in_specs, out_specs=out_specs, check_vma=False
    )
```

```python
import functools

import jax
import jax.numpy as jnp
from jax import lax
from jax.experimental import pallas as pl
from jax.experimental.pallas import tpu as pltpu
from jax.sharding import PartitionSpec as P

HEAD_DIM = 64
LANES = 128
QB = 256
TB = 256
THETA = 160000.0
EPS = 1e-05
BF = jnp.bfloat16
F32 = jnp.float32

ORDER_A = (0, 4, 8, 12, 1, 5, 9, 13, 2, 6, 10, 14, 3, 7, 11, 15)
ORDER_B = (0, 4, 8, 12, 2, 6, 10, 14, 1, 5, 9, 13, 3, 7, 11, 15)


def nn(a, b):
    return lax.dot_general(a, b, (((1,), (0,)), ((), ())), preferred_element_type=F32)


def nt(a, b):
    return lax.dot_general(a, b, (((1,), (1,)), ((), ())), preferred_element_type=F32)


def tn(a, b):
    return lax.dot_general(a, b, (((0,), (0,)), ((), ())), preferred_element_type=F32)


def up_to(n):
    return -(-n // LANES) * LANES


def rotate(u, cos, sin, sign):
    lane = lax.broadcasted_iota(jnp.int32, u.shape, 1)
    half = HEAD_DIM // 2
    partner = jnp.where(
        (lane % HEAD_DIM) < half, pltpu.roll(u, LANES - half, 1), pltpu.roll(u, half, 1)
    )
    return u * cos + partner * sin if sign > 0 else u * cos - partner * sin


def norm(x):
    center = x - jnp.mean(x, axis=-1, keepdims=True)
    inverse = lax.rsqrt(jnp.mean(center * center, axis=-1, keepdims=True) + EPS)
    return center * inverse, inverse


def norm_back(grad, xhat, inverse, gain):
    z = grad * gain
    inner = z - jnp.mean(z, axis=-1, keepdims=True) - xhat * jnp.mean(z * xhat, axis=-1, keepdims=True)
    return inverse * inner


def staged(count, stages):
    live = [None] * len(stages)
    for step in range(count + len(stages) - 1):
        new = [None] * len(stages)
        for s, stage in enumerate(stages):
            if 0 <= step - s < count:
                new[s] = stage(step - s, live[s - 1] if s else None)
        live = new


def after(x, *deps):
    return lax.optimization_barrier((x, deps))[0]


def call(kernel, name, us, vmem, operands, out_shape, scratch=()):
    spaces = [space for _, space in operands]
    return pl.pallas_call(
        kernel,
        in_specs=[pl.BlockSpec(memory_space=space) for space in spaces],
        out_specs=[pl.BlockSpec(memory_space=pltpu.VMEM)] * len(out_shape),
        scratch_shapes=list(scratch),
        out_shape=[jax.ShapeDtypeStruct(shape, dtype) for shape, dtype in out_shape],
        compiler_params=pltpu.CompilerParams(vmem_limit_bytes=vmem << 20),
        cost_estimate=pl.CostEstimate(flops=int(us * 1.15e9), transcendentals=0, bytes_accessed=int(us * 1e6)),
        name=name,
    )(*[array for array, _ in operands])


def vector(*arrays):
    return [(a, pltpu.VMEM) for a in arrays]


def stored(*arrays):
    return [(a, pltpu.HBM) for a in arrays]


def scalar(*arrays):
    return [(a, pltpu.SMEM) for a in arrays]


def load_weights(info, pieces, layout, rows, dest, sems):
    copies = []
    for ref, (r, col, order) in zip(pieces, layout, strict=True):
        cols = pl.ds(col, ref.shape[1])
        if order is None:
            copies.append((ref, dest.at[r, :, cols]))
            continue
        for i, k in enumerate(order):
            row = pl.multiple_of((info[1] ^ k) * rows, rows)
            copies.append((ref.at[pl.ds(i * rows, rows), :], dest.at[r, pl.ds(row, rows), cols]))
    copies = [pltpu.make_async_copy(a, b, sems.at[i]) for i, (a, b) in enumerate(copies)]
    for c in copies:
        c.start()
    for c in copies:
        c.wait()


def copies_of(layout):
    return sum(1 if order is None else len(order) for _, _, order in layout)


def store_rows(info, value_ref, out_ref, cols, order, rows):
    if order is None:
        out_ref[:, cols] = value_ref[...].astype(BF)
        return
    for i, k in enumerate(order):
        row = pl.multiple_of((info[1] ^ k) * rows, rows)
        out_ref[i * rows : (i + 1) * rows, cols] = value_ref[pl.ds(row, rows), :].astype(BF)


def token_blocks(info, half, run):
    for part in range(2):
        first = (info[0] if part == 0 else 1 - info[0]) * half

        @pl.loop(0, half // TB)
        def _(b, part=part, first=first):
            here = pl.multiple_of(b * TB, TB)
            run(part == 0, pl.ds(here, TB), pl.ds(pl.multiple_of(first + here, TB), TB))


def qkv_kernel(info, *refs, layout, rows, width):
    n = len(layout)
    pieces, (x_ref, recv_ref, cos_ref, sin_ref, qkv_ref, h_ref, gain_ref, w_ref, sems) = refs[:n], refs[n:]
    load_weights(info, pieces, layout, rows, w_ref, sems)
    gain_ref[...] = w_ref[0, :, 3 * width :].astype(F32).T[:8]

    def run(held, here, at):
        x = (x_ref[info[0], here, :] if held else recv_ref[here, :]).astype(F32)
        xhat, _ = norm(x)
        h = (xhat * gain_ref[0:1, :]).astype(BF)
        h_ref[at, :] = h
        cos, sin = cos_ref[at, :], sin_ref[at, :]
        for r in range(2):
            raw = nn(h, w_ref[r, :, : 3 * width])
            for b in range(2 * width // LANES):
                cols = slice(b * LANES, (b + 1) * LANES)
                u = rotate(raw[:, cols], cos, sin, 1)
                if b < width // LANES:
                    u = u * HEAD_DIM**-0.5
                qkv_ref[r, at, cols] = u.astype(BF)
            qkv_ref[r, at, 2 * width :] = raw[:, 2 * width :].astype(BF)

    token_blocks(info, recv_ref.shape[0], run)


def qkv_call(info, pieces, layout, rows, width, x, recv, cos, sin):
    d, s = x.shape[2], cos.shape[0]
    return call(
        functools.partial(qkv_kernel, layout=layout, rows=rows, width=width),
        "qkv",
        12,
        16,
        scalar(info) + stored(*pieces) + vector(x, recv, cos, sin),
        [((2, s, 3 * width), BF), ((s, d), BF), ((8, d), F32)],
        [pltpu.VMEM((2, d, 3 * width + LANES), BF), pltpu.SemaphoreType.DMA((copies_of(layout),))],
    )


def same_segment(col, row):
    parts = [
        jnp.where(col == row[:, i * LANES : (i + 1) * LANES], 0.0, -1e30).astype(F32)
        for i in range(row.shape[1] // LANES)
    ]
    return jnp.concatenate(parts, 1)


def by_range(ranges, i, blocks, run):
    for n in range(1, blocks + 1):

        @pl.when(ranges[i, 1] == n)
        def _(n=n):
            run(n, pl.ds(pl.multiple_of(ranges[i, 0], QB) if n < blocks else 0, n * QB))


def head(h):
    return slice(h * HEAD_DIM, (h + 1) * HEAD_DIM)


def attend_kernel(ranges, col_ref, row_ref, qkv_ref, o_ref, lse_ref, vt_ref):
    s, width = o_ref.shape[1:]
    heads, blocks = width // HEAD_DIM, s // QB

    @pl.loop(0, 2 * blocks)
    def _(step):
        r, i = step // blocks, step % blocks
        at = pl.ds(pl.multiple_of(i * QB, QB), QB)

        @pl.when(i == 0)
        def _():
            vt_ref[...] = qkv_ref[r, :, 2 * width :].T

        def run(n, keys):
            bias = same_segment(col_ref[keys, :], row_ref[0:1, at])
            outs, sums = [None] * heads, [None] * heads

            def scores(h, _):
                q = qkv_ref[r, at, head(h)].T
                x = nn(qkv_ref[r, keys, width + h * HEAD_DIM : width + (h + 1) * HEAD_DIM], q) + bias
                return x, jnp.max(x, axis=0, keepdims=True)

            def expo(h, a):
                e = jnp.exp(a[0] - a[1])
                return e.astype(BF), jnp.sum(e, axis=0, keepdims=True), a[1]

            def out(h, a):
                outs[h] = nn(vt_ref[head(h), keys], a[0]) * (1.0 / a[1])
                sums[h] = a[2] + jnp.log(a[1])

            staged(heads, [scores, expo, out])
            o_ref[r, at, :] = jnp.concatenate(outs, axis=0).T.astype(BF)
            for h in range(heads):
                lse_ref[r, h : h + 1, at] = sums[h]

        by_range(ranges, i, blocks, run)


def attend_call(ranges, col, row, qkv):
    _, s, w3 = qkv.shape
    width = w3 // 3
    return call(
        attend_kernel,
        "attend",
        20,
        20,
        scalar(ranges) + vector(col, row, qkv),
        [((2, s, width), BF), ((2, 8, s), F32)],
        [pltpu.VMEM((width, s), BF)],
    )


def attend_back_kernel(
    ranges, col_ref, row_ref, qkv_ref, do_ref, o_ref, lse_ref, cos_ref, sin_ref,
    dq_ref, dkv_ref, qt_ref, dot_ref, dqt_ref, delta_ref, *, r,
):
    s, width = dq_ref.shape
    heads, blocks = width // HEAD_DIM, s // QB
    qt_ref[...] = qkv_ref[r, :, :width].T
    dqt_ref[...] = jnp.zeros_like(dqt_ref)
    for i in range(blocks):
        at = slice(i * QB, (i + 1) * QB)
        dot = do_ref[at, :].astype(F32).T
        dot_ref[:, at] = dot.astype(BF)
        both = dot * o_ref[r, at, :].astype(F32).T
        for h in range(heads):
            delta_ref[h : h + 1, at] = jnp.sum(both[head(h)], axis=0, keepdims=True)

    @pl.loop(0, blocks)
    def _(c):
        here = pl.ds(pl.multiple_of(c * QB, QB), QB)

        def run(n, queries):
            bias = same_segment(col_ref[here, :], row_ref[0:1, queries])
            dks, dvs = [None] * heads, [None] * heads

            def part(h, c):
                return qkv_ref[r, here, c * width + h * HEAD_DIM : c * width + (h + 1) * HEAD_DIM]

            def products(h, _):
                return (
                    nn(part(h, 1), qt_ref[head(h), queries]) + bias,
                    nn(part(h, 2), dot_ref[head(h), queries]),
                )

            def scores(h, a):
                p = jnp.exp(a[0] - lse_ref[r, h : h + 1, queries])
                return p.astype(BF), (p * (a[1] - delta_ref[h : h + 1, queries])).astype(BF)

            def grads(h, a):
                dvs[h] = nt(dot_ref[head(h), queries], a[0])
                dks[h] = nt(qt_ref[head(h), queries], a[1])
                dqt_ref[head(h), queries] += nn(part(h, 1).T, a[1])

            staged(heads, [products, scores, grads])
            cos, sin = cos_ref[here, :], sin_ref[here, :]
            for b in range(width // LANES):
                dk = jnp.concatenate(dks[2 * b : 2 * b + 2], 0).T
                dv = jnp.concatenate(dvs[2 * b : 2 * b + 2], 0).T
                dkv_ref[here, b * LANES : (b + 1) * LANES] = rotate(dk, cos, sin, -1).astype(BF)
                dkv_ref[here, width + b * LANES : width + (b + 1) * LANES] = dv.astype(BF)

        by_range(ranges, c, blocks, run)

    for i in range(blocks):
        at = slice(i * QB, (i + 1) * QB)
        for b in range(width // LANES):
            cols = slice(b * LANES, (b + 1) * LANES)
            dq = dqt_ref[cols, at].T * HEAD_DIM**-0.5
            dq_ref[at, cols] = rotate(dq, cos_ref[at, :], sin_ref[at, :], -1).astype(BF)


def attend_back_call(r, ranges, col, row, qkv, do, o, lse, cos, sin):
    _, s, w3 = qkv.shape
    width = w3 // 3
    return call(
        functools.partial(attend_back_kernel, r=r),
        "attend_back",
        18,
        24,
        scalar(ranges) + vector(col, row, qkv, do, o, lse, cos, sin),
        [((s, width), BF), ((s, 2 * width), BF)],
        [
            pltpu.VMEM((width, s), BF),
            pltpu.VMEM((width, s), BF),
            pltpu.VMEM((width, s), F32),
            pltpu.VMEM((8, s), F32),
        ],
    )


def mlp_kernel(info, *refs, layout, rows, width, units):
    n = len(layout)
    (x_ref, xr_ref, dy_ref, dyr_ref, o_ref, gain_ref,
     own_ref, other_ref, dr_ref, do0_ref, do1_ref, h_ref, dyo_ref, da_ref,
     dgu0_ref, dgu1_ref, m0_ref, m1_ref, gg_ref,
     w_ref, sems) = refs[n:]
    load_weights(info, refs[:n], layout, rows, w_ref, sems)
    gg_ref[...] = jnp.zeros_like(gg_ref)
    c0, c1, c2, c3 = width, width + units, width + 2 * units, width + 3 * units
    gain = gain_ref[1:2, :]

    def run(held, here, at):
        x = (x_ref[info[0], here, :] if held else xr_ref[here, :]).astype(F32)
        dyb = dy_ref[info[0], here, :] if held else dyr_ref[here, :]
        dyo_ref[at, :] = dyb
        r1 = x + nt(o_ref[0, at, :], w_ref[0, :, :c0]) + nt(o_ref[1, at, :], w_ref[1, :, :c0])
        xhat, inverse = norm(r1)
        h = (xhat * gain).astype(BF)
        h_ref[at, :] = h
        outs, dhs = [], []

        def products(r, _):
            return nn(h, w_ref[r, :, c0:c1]), nn(h, w_ref[r, :, c1:c2]), nn(dyb, w_ref[r, :, c2:c3])

        def units_of(r, a):
            gate, up, dm = a
            phi = 0.5 + 0.5 * lax.erf(gate * 0.7071067811865476)
            density = jnp.exp(-0.5 * gate * gate) * 0.3989422804014327
            gelu = gate * phi
            m = (gelu * up).astype(BF)
            dgate = (dm * up * (phi + gate * density)).astype(BF)
            dup = (dm * gelu).astype(BF)
            (m0_ref, m1_ref)[r][at, :] = m
            dgu_ref = (dgu0_ref, dgu1_ref)[r]
            dgu_ref[at, :units] = dgate
            dgu_ref[at, units:] = dup
            return m, dgate, dup

        def sums(r, a):
            outs.append(nt(a[0], w_ref[r, :, c2:c3]))
            dhs.append(nt(a[1], w_ref[r, :, c0:c1]) + nt(a[2], w_ref[r, :, c1:c2]))

        staged(2, [products, units_of, sums])
        out = (r1 + (outs[0] + outs[1])).astype(BF)
        (own_ref if held else other_ref)[here, :] = out
        dh = dhs[0] + dhs[1]
        gg_ref[0:1, :] += jnp.sum(dh * xhat, axis=0, keepdims=True)
        dr = dyb.astype(F32) + norm_back(dh, xhat, inverse, gain)
        dr_ref[at, :] = dr
        da = dr.astype(BF)
        da_ref[at, :] = da
        for r in range(2):
            (do0_ref, do1_ref)[r][at, :] = nn(da, w_ref[r, :, :c0]).astype(BF)

    token_blocks(info, xr_ref.shape[0], run)


def mlp_call(info, pieces, layout, rows, width, units, x, xr, dy, dyr, o, gains):
    d, s = x.shape[2], o.shape[1]
    return call(
        functools.partial(mlp_kernel, layout=layout, rows=rows, width=width, units=units),
        "mlp",
        30,
        24,
        scalar(info) + stored(*pieces) + vector(x, xr, dy, dyr, o, gains),
        [
            ((s // 2, d), BF),
            ((s // 2, d), BF),
            ((s, d), F32),
            ((s, width), BF),
            ((s, width), BF),
            ((s, d), BF),
            ((s, d), BF),
            ((s, d), BF),
            ((s, 2 * units), BF),
            ((s, 2 * units), BF),
            ((s, units), BF),
            ((s, units), BF),
            ((8, d), F32),
        ],
        [pltpu.VMEM((2, d, width + 3 * units), BF), pltpu.SemaphoreType.DMA((copies_of(layout),))],
    )


def weight_grad_kernel(info, *refs, leads, products, orders, rows):
    n = len(leads)
    outs, g_ref = refs[n : n + 2], refs[n + 2]
    for a, b, col in products:
        left, right = refs[a], refs[b]
        for out_ref, order, base in zip(outs, orders, (0, outs[0].shape[1])):
            start, stop = max(col, base), min(col + right.shape[-1], base + out_ref.shape[1])
            if start >= stop:
                continue
            cols = slice(start - col, stop - col)
            value = g_ref.at[:, pl.ds(0, stop - start)]
            value[...] = tn(left[...], right[:, cols] if leads[b] is None else right[leads[b], :, cols]).astype(BF)
            store_rows(info, value, out_ref, slice(start - base, stop - base), order, rows)


def weight_grad_call(name, us, info, rows, orders, operands, products, split, total):
    arrays = [a for a, _ in operands]
    d = arrays[0].shape[-1]
    widest = max(a.shape[-1] for a in arrays)
    leads = [lead for _, lead in operands]
    return call(
        functools.partial(weight_grad_kernel, leads=leads, products=products, orders=orders, rows=rows),
        name,
        us,
        16,
        scalar(info) + vector(*arrays),
        [((d, split), BF), ((d, total - split), BF)],
        [pltpu.VMEM((d, widest), BF)],
    )


def input_kernel(info, *refs, layout, rows, width, order):
    n = len(layout)
    (x_ref, xr_ref, dq0_ref, dkv0_ref, dq1_ref, dkv1_ref, dr_ref, gain_ref, gg_ref,
     own_ref, other_ref, gcol_ref, w_ref, acc_ref, col_ref, sems) = refs[n:]
    load_weights(info, refs[:n], layout, rows, w_ref, sems)
    acc_ref[...] = jnp.zeros_like(acc_ref)
    acc_ref[1:2, :] = gg_ref[0:1, :]
    gain = gain_ref[0:1, :]

    def run(held, here, at):
        x = (x_ref[info[0], here, :] if held else xr_ref[here, :]).astype(F32)
        xhat, inverse = norm(x)
        dh = nt(dq0_ref[at, :], w_ref[0, :, :width]) + nt(dq1_ref[at, :], w_ref[1, :, :width])
        dh = dh + nt(dkv0_ref[at, :], w_ref[0, :, width : 3 * width])
        dh = dh + nt(dkv1_ref[at, :], w_ref[1, :, width : 3 * width])
        acc_ref[0:1, :] += jnp.sum(dh * xhat, axis=0, keepdims=True)
        (own_ref if held else other_ref)[here, :] = dr_ref[at, :] + norm_back(dh, xhat, inverse, gain)

    token_blocks(info, xr_ref.shape[0], run)
    col_ref[...] = acc_ref[...].T
    store_rows(info, col_ref, gcol_ref, slice(0, LANES), order, rows)


def input_call(info, pieces, layout, rows, width, x, xr, draw, dr, gains, gg, order):
    d, s = x.shape[2], dr.shape[0]
    return call(
        functools.partial(input_kernel, layout=layout, rows=rows, width=width, order=order),
        "input_back",
        10,
        16,
        scalar(info) + stored(*pieces) + vector(x, xr, *draw, dr, gains, gg),
        [((s // 2, d), F32), ((s // 2, d), F32), ((d, LANES), BF)],
        [
            pltpu.VMEM((2, d, 3 * width + LANES), BF),
            pltpu.VMEM((LANES, d), F32),
            pltpu.VMEM((d, LANES), F32),
            pltpu.SemaphoreType.DMA((copies_of(layout),)),
        ],
    )


def swap(x):
    return lax.ppermute(x, "tensor", [(0, 1), (1, 0)])


def peer(x, k):
    return lax.ppermute(x, "dp", [(i, i ^ k) for i in range(16)])


def under(x, run, *sends):
    x, arrays = after((x, [a for _, a in sends]))
    got = [f(a) for (f, _), a in zip(sends, arrays)]
    return after((run(x), got))


def to(k):
    return lambda x: peer(x, k)


def add(*terms):
    return functools.reduce(jnp.add, [t.astype(F32) for t in terms])


class Gather:
    def __init__(self, split):
        self.split = split

    def near(self, block):
        self.ab = block[:, : self.split], block[:, self.split :]
        return [(to(k), x) for k, x in zip((1, 2), self.ab)]

    def far(self, got):
        self.ab = [jnp.concatenate(x, 0) for x in zip(self.ab, got)]
        return [(to(k), x) for k, x in zip((2, 1), self.ab)]

    def pieces(self, got, theirs, got_theirs):
        orders = (0, ORDER_A), (self.split, ORDER_B)
        where = [(col, order[8 * i : 8 * i + 8]) for i in range(2) for col, order in orders]
        layout = [(r, *w) for r in range(2) for w in where]
        return [*self.ab, *got, *theirs, *got_theirs], layout


def half_sends(terms, ks):
    n = terms[0][0].shape[0] // 2
    keep = [[t[:n] for t in ts] for ts in terms]
    return keep, [(to(k), add(*(t[n:] for t in ts)).astype(BF)) for k, ts in zip(ks, terms)]


def joined(keep, got):
    return [ts + [g] for ts, g in zip(keep, got)]


def last_sends(terms):
    both = jnp.concatenate([add(*ts) for ts in terms], 1)
    n = both.shape[0] // 4
    send = both[n:].astype(BF)
    return both[:n], [(to(4 * i), send[(i - 1) * n : i * n]) for i in (1, 2, 3)]


def gather_plain(slab):
    whole = lax.all_gather(slab, "dp", axis=0, tiled=True)
    return [whole, swap(whole)], [(0, 0, None), (1, 0, None)]


def scatter_plain(a, b):
    both = jnp.concatenate([add(*a), add(*b)], 1)
    return lax.psum_scatter(both, "dp", scatter_dimension=0, tiled=True)


def local(
    hidden_in, segment_ids, qkv_weight, out_weight, mlp_weight, down_weight, attn_gain, mlp_gain,
    cotangent, *, cube,
):
    t, me = lax.axis_index("tensor"), lax.axis_index("dp")
    info = jnp.stack([t, me]).astype(jnp.int32)
    rows, width = qkv_weight.shape[1:]
    d = hidden_in.shape[2]
    units_here = mlp_weight.shape[2]
    units = up_to(units_here)
    s = segment_ids.shape[1]

    def placed(own, got):
        first = t == 0
        return jnp.stack([jnp.where(first, own, got), jnp.where(first, got, own)])

    def other(x):
        return lax.dynamic_index_in_dim(x, 1 - t, 0, False)

    x_recv = swap(other(hidden_in))
    gain_cols = jnp.stack([attn_gain, mlp_gain], 1)
    gain_cols = jnp.pad(gain_cols, ((0, 0), (0, LANES - 2)))
    slab1 = jnp.concatenate([qkv_weight[0], qkv_weight[1], qkv_weight[2], gain_cols], 1)

    def wide(w):
        return jnp.pad(w, ((0, 0), (0, units - units_here)))

    def second_slab(out_weight, mlp_weight, down_weight):
        return jnp.concatenate(
            [out_weight.T, wide(mlp_weight[0]), wide(mlp_weight[1]), wide(down_weight.T)], 1
        )

    weights2 = out_weight, mlp_weight, down_weight
    total1, total2 = slab1.shape[1], width + 3 * units
    split1, split2 = total1 // 2 // LANES * LANES, total2 // 2 // LANES * LANES
    seg = lax.dynamic_index_in_dim(segment_ids, t, 0, False)
    index = jnp.arange(s, dtype=jnp.int32)
    start = jnp.sum((seg[None, :] < seg[:, None]).astype(jnp.int32), axis=1)
    freqs = THETA ** (-2.0 * jnp.arange(HEAD_DIM // 2, dtype=F32) / HEAD_DIM)
    angles = (index - start).astype(F32)[:, None] * freqs[None, :]
    cos, sin = jnp.cos(angles), jnp.sin(angles)
    cos = jnp.concatenate([cos, cos, cos, cos], 1)
    sin = jnp.concatenate([-sin, sin, -sin, sin], 1)
    col = jnp.broadcast_to(seg[:, None], (s, LANES))
    row = jnp.broadcast_to(seg[None, :], (8, s))
    ends = seg.reshape(s // QB, QB)
    first, last = ends[:, 0], ends[:, -1]
    meet = (first[:, None] <= last[None, :]) & (first[None, :] <= last[:, None])
    block = jnp.arange(s // QB, dtype=jnp.int32)[None, :]
    low = jnp.min(jnp.where(meet, block, s), axis=1)
    high = jnp.max(jnp.where(meet, block, -1), axis=1)
    ranges = jnp.stack([low * QB, high - low + 1], 1).astype(jnp.int32)

    def project(w1):
        return qkv_call(info, w1, layout1, rows, width, hidden_in, x_recv, cos, sin)

    def attend(qkv):
        return attend_call(ranges, col, row, qkv)

    if cube:
        g1 = Gather(split1)
        g2 = Gather(split2)
        sends = g1.near(jnp.concatenate([slab1] + [peer(slab1, k) for k in (4, 8, 12)], 0))
        (weights2, x_recv), g1.ab = after(((weights2, x_recv), [x for _, x in sends]))
        got = [f(x) for (f, _), x in zip(sends, g1.ab)]
        slab2 = second_slab(*weights2)
        block2 = jnp.concatenate([slab2] + [peer(slab2, k) for k in (4, 8, 12)], 0)
        sends = g1.far(got)
        got = [f(x) for f, x in sends]
        got, g1.ab = after((got, g1.ab))
        w1, layout1 = g1.pieces(got, [swap(x) for x in g1.ab], [swap(x) for x in got])
        (qkv, h1, gains), (*got, dy_recv) = under(
            w1, project, *g2.near(block2), (swap, other(cotangent))
        )
        far = g2.far(got)
        (o, lse), got = under(qkv, attend, *far, *((swap, x) for _, x in far))
        w2, layout2 = g2.pieces(got[:2], got[2:], [swap(x) for x in got[:2]])
    else:
        w1, layout1 = gather_plain(slab1)
        w2, layout2 = gather_plain(second_slab(*weights2))
        dy_recv = swap(other(cotangent))
        qkv, h1, gains = project(w1)
        o, lse = attend(qkv)
    out_own, out_other, dr, do0, do1, h2, dy, da, dgu0, dgu1, m0, m1, gg = mlp_call(
        info, w2, layout2, rows, width, units, hidden_in, x_recv, cotangent, dy_recv, o, gains
    )
    orders = (ORDER_A, ORDER_B) if cube else (None, None)

    def grads2(r):
        return lambda o: weight_grad_call(
            "mlp_weight_grad", 10, info, rows, orders,
            [(da, None), (h2, None), (dy, None), (o, r), ((dgu0, dgu1)[r], None), ((m0, m1)[r], None)],
            [(0, 3, 0), (1, 4, width), (2, 5, width + 2 * units)], split2, total2,
        )

    def grads1(draw):
        return weight_grad_call(
            "qkv_weight_grad", 6, info, rows, orders,
            [(h1, None), (draw[0], None), (draw[1], None)],
            [(0, 1, 0), (0, 2, width)], split1, total1 - LANES,
        )

    def back(r):
        return lambda do: attend_back_call(r, ranges, col, row, qkv, do, o, lse, cos, sin)

    def input_back(dr):
        return input_call(
            info, w1, layout1, rows, width, hidden_in, x_recv, (*draw0, *draw1), dr, gains, gg, orders[1]
        )

    sent = grads2(1)(o)
    mine, (*theirs, out_recv) = under(o, grads2(0), *((swap, g) for g in sent), (swap, out_other))
    layer_out = placed(out_own, out_recv)
    sums2 = [[a, b] for a, b in zip(mine, theirs)]
    if cube:
        keep, sends = half_sends(sums2, (2, 1))
        draw1, got = under(do1, back(1), *sends)
        keep, sends = half_sends(joined(keep, got), (1, 2))
        do0, sends2 = after((do0, [x for _, x in sends]))
        sent = grads1(after(draw1, sends2))
        draw0, got = under(
            after(do0, sent), back(0), *((f, x) for (f, _), x in zip(sends, sends2)), *((swap, g) for g in sent)
        )
        keep2, sends2 = last_sends(joined(keep, got[:2]))
        draw0, last = after((draw0, [x for _, x in sends2]))
        mine = grads1(draw0)
        keep, sends = half_sends([[a, b] for a, b in zip(mine, got[2:])], (2, 1))
        (in_own, in_other, gcol), got = under(
            dr, input_back, *((f, x) for (f, _), x in zip(sends2, last)), *sends
        )
        sum2 = add(keep2, *got[:3])
        keep, sends = half_sends(joined(keep, got[3:]), (1, 2))

        def gain_sums(gcol):
            both = add(gcol, swap(gcol))
            for k in (1, 2):
                n = both.shape[0] // 2
                both = add(both[:n], peer(both[n:].astype(BF), k))
            return both

        gain_sum, (*got, in_recv) = under(gcol, gain_sums, *sends, (swap, in_other))
        keep = joined(keep, got)
        keep, sends = last_sends([keep[0], [jnp.concatenate([add(*keep[1]), gain_sum], 1)]])
        input_grad, got = under(in_recv, lambda got: placed(in_own, got), *sends)
        sum1 = add(keep, *got)
    else:
        sum2 = scatter_plain(*sums2)
        draw1, draw0 = back(1)(do1), back(0)(do0)
        theirs = [swap(g) for g in grads1(draw1)]
        mine = grads1(draw0)
        in_own, in_other, gcol = input_back(dr)
        input_grad = placed(in_own, swap(in_other))
        b = [jnp.concatenate([g, c], 1) for g, c in zip((mine[1], theirs[1]), (gcol, swap(gcol)))]
        sum1 = scatter_plain((mine[0], theirs[0]), b)
    qkv_grad = sum1[:, : 3 * width].reshape(rows, 3, width).transpose(1, 0, 2)
    c = width
    proj_grad = sum2[:, :c].T
    mlp_grad = jnp.stack([sum2[:, c : c + units_here], sum2[:, c + units : c + units + units_here]])
    down_grad = sum2[:, c + 2 * units : c + 2 * units + units_here].T
    return (
        layer_out,
        input_grad,
        qkv_grad,
        proj_grad,
        mlp_grad,
        down_grad,
        sum1[:, 3 * width],
        sum1[:, 3 * width + 1],
    )


def solution(mesh):
    rows = P(None, ("dp", "tensor"), None)
    in_specs = (
        rows,
        P(None, "dp"),
        P(None, "dp", "tensor"),
        P("tensor", "dp"),
        P(None, "dp", "tensor"),
        P("tensor", "dp"),
        P("dp"),
        P("dp"),
        rows,
    )
    out_specs = (
        rows,
        rows,
        P(None, "dp", "tensor"),
        P("tensor", "dp"),
        P(None, "dp", "tensor"),
        P("tensor", "dp"),
        P("dp"),
        P("dp"),
    )
    cube = mesh.shape["dp"] == 16
    return jax.shard_map(
        functools.partial(local, cube=cube), mesh=mesh, in_specs=in_specs, out_specs=out_specs, check_vma=False
    )
```

```python
import functools

import jax
import jax.numpy as jnp
from jax import lax
from jax.experimental import pallas as pl
from jax.experimental.pallas import tpu as pltpu
from jax.sharding import PartitionSpec as P

HEAD_DIM = 64
LANES = 128
QB = 256
TB = 512
THETA = 160000.0
EPS = 1e-05
LOG2E = 1.4426950408889634
SAFE = 96.0
BF = jnp.bfloat16
F32 = jnp.float32

ORDER_A = (0, 4, 8, 12, 1, 5, 9, 13, 2, 6, 10, 14, 3, 7, 11, 15)
ORDER_B = (0, 4, 8, 12, 2, 6, 10, 14, 1, 5, 9, 13, 3, 7, 11, 15)


def nn(a, b):
    return lax.dot_general(a, b, (((1,), (0,)), ((), ())), preferred_element_type=F32)


def nt(a, b):
    return lax.dot_general(a, b, (((1,), (1,)), ((), ())), preferred_element_type=F32)


def tn(a, b):
    return lax.dot_general(a, b, (((0,), (0,)), ((), ())), preferred_element_type=F32)


def up_to(n):
    return -(-n // LANES) * LANES


def rotate(u, cos, sin, sign):
    lane = lax.broadcasted_iota(jnp.int32, u.shape, 1)
    half = HEAD_DIM // 2
    partner = jnp.where(
        (lane % HEAD_DIM) < half, pltpu.roll(u, LANES - half, 1), pltpu.roll(u, half, 1)
    )
    return u * cos + partner * sin if sign > 0 else u * cos - partner * sin


def norm(x):
    center = x - jnp.mean(x, axis=-1, keepdims=True)
    inverse = lax.rsqrt(jnp.mean(center * center, axis=-1, keepdims=True) + EPS)
    return center * inverse, inverse


def norm_back(grad, xhat, inverse, gain):
    z = grad * gain
    inner = z - jnp.mean(z, axis=-1, keepdims=True) - xhat * jnp.mean(z * xhat, axis=-1, keepdims=True)
    return inverse * inner


def staged(count, stages):
    live = [None] * len(stages)
    for step in range(count + len(stages) - 1):
        new = [None] * len(stages)
        for s, stage in enumerate(stages):
            if 0 <= step - s < count:
                new[s] = stage(step - s, live[s - 1] if s else None)
        live = new


def after(x, *deps):
    return lax.optimization_barrier((x, deps))[0]


def call(kernel, name, us, vmem, operands, out_shape, scratch=()):
    spaces = [space for _, space in operands]
    return pl.pallas_call(
        kernel,
        in_specs=[pl.BlockSpec(memory_space=space) for space in spaces],
        out_specs=[pl.BlockSpec(memory_space=pltpu.VMEM)] * len(out_shape),
        scratch_shapes=list(scratch),
        out_shape=[jax.ShapeDtypeStruct(shape, dtype) for shape, dtype in out_shape],
        compiler_params=pltpu.CompilerParams(vmem_limit_bytes=vmem << 20),
        cost_estimate=pl.CostEstimate(flops=int(us * 1.15e9), transcendentals=0, bytes_accessed=int(us * 1e6)),
        name=name,
    )(*[array for array, _ in operands])


def vector(*arrays):
    return [(a, pltpu.VMEM) for a in arrays]


def stored(*arrays):
    return [(a, pltpu.HBM) for a in arrays]


def scalar(*arrays):
    return [(a, pltpu.SMEM) for a in arrays]


def load_weights(info, pieces, layout, rows, dest, sems):
    copies = []
    for ref, (r, col, order) in zip(pieces, layout, strict=True):
        cols = pl.ds(col, ref.shape[1])
        if order is None:
            copies.append((ref, dest.at[r, :, cols]))
            continue
        for i, k in enumerate(order):
            row = pl.multiple_of((info[1] ^ k) * rows, rows)
            copies.append((ref.at[pl.ds(i * rows, rows), :], dest.at[r, pl.ds(row, rows), cols]))
    copies = [pltpu.make_async_copy(a, b, sems.at[i]) for i, (a, b) in enumerate(copies)]
    for c in copies:
        c.start()
    for c in copies:
        c.wait()


def copies_of(layout):
    return sum(1 if order is None else len(order) for _, _, order in layout)


def store_rows(info, value_ref, out_ref, cols, order, rows):
    if order is None:
        out_ref[:, cols] = value_ref[...].astype(BF)
        return
    for i, k in enumerate(order):
        row = pl.multiple_of((info[1] ^ k) * rows, rows)
        out_ref[i * rows : (i + 1) * rows, cols] = value_ref[pl.ds(row, rows), :].astype(BF)


def token_blocks(info, half, run, size=TB):
    for part in range(2):
        first = (info[0] if part == 0 else 1 - info[0]) * half

        @pl.loop(0, half // size)
        def _(b, part=part, first=first):
            here = pl.multiple_of(b * size, size)
            run(part == 0, pl.ds(here, size), pl.ds(pl.multiple_of(first + here, size), size))


def qkv_kernel(info, *refs, layout, rows, width):
    n = len(layout)
    pieces, (x_ref, recv_ref, cos_ref, sin_ref, qkv_ref, h_ref, gain_ref, w_ref, sems) = refs[:n], refs[n:]
    load_weights(info, pieces, layout, rows, w_ref, sems)
    gain_ref[...] = w_ref[0, :, 3 * width :].astype(F32).T[:8]

    def run(held, here, at):
        x = (x_ref[info[0], here, :] if held else recv_ref[here, :]).astype(F32)
        xhat, _ = norm(x)
        h = (xhat * gain_ref[0:1, :]).astype(BF)
        h_ref[at, :] = h
        cos, sin = cos_ref[at, :], sin_ref[at, :]
        for r in range(2):
            raw = nn(h, w_ref[r, :, : 3 * width])
            for b in range(2 * width // LANES):
                cols = slice(b * LANES, (b + 1) * LANES)
                u = rotate(raw[:, cols], cos, sin, 1)
                if b < width // LANES:
                    u = u * (HEAD_DIM**-0.5 * LOG2E)
                qkv_ref[r, at, cols] = u.astype(BF)
            qkv_ref[r, at, 2 * width :] = raw[:, 2 * width :].astype(BF)

    token_blocks(info, recv_ref.shape[0], run)


def qkv_call(info, pieces, layout, rows, width, x, recv, cos, sin):
    d, s = x.shape[2], cos.shape[0]
    return call(
        functools.partial(qkv_kernel, layout=layout, rows=rows, width=width),
        "qkv",
        12,
        16,
        scalar(info) + stored(*pieces) + vector(x, recv, cos, sin),
        [((2, s, 3 * width), BF), ((s, d), BF), ((8, d), F32)],
        [pltpu.VMEM((2, d, 3 * width + LANES), BF), pltpu.SemaphoreType.DMA((copies_of(layout),))],
    )


def same_segment(col, row):
    parts = [
        jnp.where(col == row[:, i * LANES : (i + 1) * LANES], 0.0, -1e30).astype(F32)
        for i in range(row.shape[1] // LANES)
    ]
    return jnp.concatenate(parts, 1)


def by_range(ranges, i, blocks, run):
    for n in range(1, blocks + 1):

        @pl.when(ranges[i, 1] == n)
        def _(n=n):
            run(n, pl.ds(pl.multiple_of(ranges[i, 0], QB) if n < blocks else 0, n * QB))


def head(h):
    return slice(h * HEAD_DIM, (h + 1) * HEAD_DIM)


def largest(x):
    x = x.astype(F32)
    sums = [jnp.sum(x[head(h)] * x[head(h)], axis=0, keepdims=True) for h in range(x.shape[0] // HEAD_DIM)]
    return jnp.max(functools.reduce(jnp.maximum, sums))


def attend_kernel(ranges, col_ref, row_ref, qkv_ref, o_ref, lse_ref, qt_ref, vt_ref, safe_ref):
    s, width = o_ref.shape[1:]
    heads, blocks = width // HEAD_DIM, s // QB

    @pl.loop(0, 2 * blocks)
    def _(step):
        r, i = step // blocks, step % blocks
        at = pl.ds(pl.multiple_of(i * QB, QB), QB)

        @pl.when(i == 0)
        def _():
            qt_ref[...] = qkv_ref[r, :, :width].T
            vt_ref[...] = qkv_ref[r, :, 2 * width :].T
            bound = largest(qt_ref[...]) * largest(qkv_ref[r, :, width : 2 * width].T)
            safe_ref[0] = (bound < SAFE * SAFE).astype(jnp.int32)

        def run(n, keys, safe):
            bias = same_segment(col_ref[keys, :], row_ref[0:1, at])
            outs, sums = [None] * heads, [None] * heads

            def scores(h, _):
                k = qkv_ref[r, keys, width + h * HEAD_DIM : width + (h + 1) * HEAD_DIM]
                x = nn(k, qt_ref[head(h), at]) + bias
                return x, None if safe else jnp.max(x, axis=0, keepdims=True)

            def expo(h, a):
                e = jnp.exp2(a[0] if safe else a[0] - a[1])
                return e.astype(BF), jnp.sum(e, axis=0, keepdims=True), a[1]

            def out(h, a):
                outs[h] = nn(vt_ref[head(h), keys], a[0]) * (1.0 / a[1])
                total = jnp.log2(a[1])
                sums[h] = total if safe else a[2] + total

            staged(heads, [scores, expo, out])
            o_ref[r, at, :] = jnp.concatenate(outs, axis=0).T.astype(BF)
            for h in range(heads):
                lse_ref[r, h : h + 1, at] = sums[h]

        @pl.when(safe_ref[0] == 1)
        def _():
            by_range(ranges, i, blocks, functools.partial(run, safe=True))

        @pl.when(safe_ref[0] == 0)
        def _():
            run(blocks, slice(0, s), False)


def attend_call(ranges, col, row, qkv):
    _, s, w3 = qkv.shape
    width = w3 // 3
    return call(
        attend_kernel,
        "attend",
        20,
        20,
        scalar(ranges) + vector(col, row, qkv),
        [((2, s, width), BF), ((2, 8, s), F32)],
        [pltpu.VMEM((width, s), BF), pltpu.VMEM((width, s), BF), pltpu.SMEM((1,), jnp.int32)],
    )


def attend_back_kernel(
    ranges, col_ref, row_ref, qkv_ref, do_ref, o_ref, lse_ref, cos_ref, sin_ref,
    dq_ref, dkv_ref, qt_ref, dot_ref, dqt_ref, delta_ref, *, r,
):
    s, width = dq_ref.shape
    heads, blocks = width // HEAD_DIM, s // QB
    qt_ref[...] = qkv_ref[r, :, :width].T
    dqt_ref[...] = jnp.zeros_like(dqt_ref)
    for i in range(blocks):
        at = slice(i * QB, (i + 1) * QB)
        dot = do_ref[at, :].astype(F32).T
        dot_ref[:, at] = dot.astype(BF)
        both = dot * o_ref[r, at, :].astype(F32).T
        for h in range(heads):
            delta_ref[h : h + 1, at] = jnp.sum(both[head(h)], axis=0, keepdims=True)

    @pl.loop(0, blocks)
    def _(c):
        here = pl.ds(pl.multiple_of(c * QB, QB), QB)

        def run(n, queries):
            bias = same_segment(col_ref[here, :], row_ref[0:1, queries])
            dks, dvs = [None] * heads, [None] * heads

            def part(h, c):
                return qkv_ref[r, here, c * width + h * HEAD_DIM : c * width + (h + 1) * HEAD_DIM]

            def products(h, _):
                return (
                    nn(part(h, 1), qt_ref[head(h), queries]) + bias,
                    nn(part(h, 2), dot_ref[head(h), queries]),
                )

            def scores(h, a):
                p = jnp.exp2(a[0] - lse_ref[r, h : h + 1, queries])
                return p.astype(BF), (p * (a[1] - delta_ref[h : h + 1, queries])).astype(BF)

            def grads(h, a):
                dvs[h] = nt(dot_ref[head(h), queries], a[0])
                dks[h] = nt(qt_ref[head(h), queries], a[1])
                dqt_ref[head(h), queries] += nn(part(h, 1).T, a[1])

            staged(heads, [products, scores, grads])
            cos, sin = cos_ref[here, :], sin_ref[here, :]
            for b in range(width // LANES):
                dk = jnp.concatenate(dks[2 * b : 2 * b + 2], 0).T
                dv = jnp.concatenate(dvs[2 * b : 2 * b + 2], 0).T
                dk = rotate(dk, cos, sin, -1) * (1 / LOG2E)
                dkv_ref[here, b * LANES : (b + 1) * LANES] = dk.astype(BF)
                dkv_ref[here, width + b * LANES : width + (b + 1) * LANES] = dv.astype(BF)

        by_range(ranges, c, blocks, run)

    for i in range(blocks):
        at = slice(i * QB, (i + 1) * QB)
        for b in range(width // LANES):
            cols = slice(b * LANES, (b + 1) * LANES)
            dq = dqt_ref[cols, at].T * HEAD_DIM**-0.5
            dq_ref[at, cols] = rotate(dq, cos_ref[at, :], sin_ref[at, :], -1).astype(BF)


def attend_back_call(r, ranges, col, row, qkv, do, o, lse, cos, sin):
    _, s, w3 = qkv.shape
    width = w3 // 3
    return call(
        functools.partial(attend_back_kernel, r=r),
        "attend_back",
        18,
        24,
        scalar(ranges) + vector(col, row, qkv, do, o, lse, cos, sin),
        [((s, width), BF), ((s, 2 * width), BF)],
        [
            pltpu.VMEM((width, s), BF),
            pltpu.VMEM((width, s), BF),
            pltpu.VMEM((width, s), F32),
            pltpu.VMEM((8, s), F32),
        ],
    )


def mlp_kernel(info, *refs, layout, rows, width, units):
    n = len(layout)
    (x_ref, xr_ref, dy_ref, dyr_ref, o_ref, gain_ref,
     own_ref, other_ref, dr_ref, do0_ref, do1_ref, h_ref, dyo_ref, da_ref,
     dgu0_ref, dgu1_ref, m0_ref, m1_ref, gg_ref,
     w_ref, sems) = refs[n:]
    load_weights(info, refs[:n], layout, rows, w_ref, sems)
    gg_ref[...] = jnp.zeros_like(gg_ref)
    c0, c2, c3 = width, width + 2 * units, width + 3 * units
    gain = gain_ref[1:2, :]

    def run(held, here, at):
        x = (x_ref[info[0], here, :] if held else xr_ref[here, :]).astype(F32)
        dyb = dy_ref[info[0], here, :] if held else dyr_ref[here, :]
        dyo_ref[at, :] = dyb
        r1 = x + nt(o_ref[0, at, :], w_ref[0, :, :c0]) + nt(o_ref[1, at, :], w_ref[1, :, :c0])
        xhat, inverse = norm(r1)
        h = (xhat * gain).astype(BF)
        h_ref[at, :] = h
        outs, dhs = [], []

        def products(r, _):
            return nn(h, w_ref[r, :, c0:c2]), nn(dyb, w_ref[r, :, c2:c3])

        def units_of(r, a):
            gate, up, dm = a[0][:, :units], a[0][:, units:], a[1]
            phi = 0.5 + 0.5 * lax.erf(gate * 0.7071067811865476)
            density = jnp.exp(-0.5 * gate * gate) * 0.3989422804014327
            gelu = gate * phi
            m = (gelu * up).astype(BF)
            dgate = (dm * up * (phi + gate * density)).astype(BF)
            dup = (dm * gelu).astype(BF)
            (m0_ref, m1_ref)[r][at, :] = m
            dgu_ref = (dgu0_ref, dgu1_ref)[r]
            dgu_ref[at, :units] = dgate
            dgu_ref[at, units:] = dup
            return m, jnp.concatenate([dgate, dup], 1)

        def sums(r, a):
            outs.append(nt(a[0], w_ref[r, :, c2:c3]))
            dhs.append(nt(a[1], w_ref[r, :, c0:c2]))

        staged(2, [products, units_of, sums])
        out = (r1 + (outs[0] + outs[1])).astype(BF)
        (own_ref if held else other_ref)[here, :] = out
        dh = dhs[0] + dhs[1]
        gg_ref[0:1, :] += jnp.sum(dh * xhat, axis=0, keepdims=True)
        dr = dyb.astype(F32) + norm_back(dh, xhat, inverse, gain)
        dr_ref[at, :] = dr
        da = dr.astype(BF)
        da_ref[at, :] = da
        for r in range(2):
            (do0_ref, do1_ref)[r][at, :] = nn(da, w_ref[r, :, :c0]).astype(BF)

    token_blocks(info, xr_ref.shape[0], run, TB // 2)


def mlp_call(info, pieces, layout, rows, width, units, x, xr, dy, dyr, o, gains):
    d, s = x.shape[2], o.shape[1]
    return call(
        functools.partial(mlp_kernel, layout=layout, rows=rows, width=width, units=units),
        "mlp",
        30,
        24,
        scalar(info) + stored(*pieces) + vector(x, xr, dy, dyr, o, gains),
        [
            ((s // 2, d), BF),
            ((s // 2, d), BF),
            ((s, d), F32),
            ((s, width), BF),
            ((s, width), BF),
            ((s, d), BF),
            ((s, d), BF),
            ((s, d), BF),
            ((s, 2 * units), BF),
            ((s, 2 * units), BF),
            ((s, units), BF),
            ((s, units), BF),
            ((8, d), F32),
        ],
        [pltpu.VMEM((2, d, width + 3 * units), BF), pltpu.SemaphoreType.DMA((copies_of(layout),))],
    )


def weight_grad_kernel(info, *refs, leads, products, orders, rows):
    n = len(leads)
    outs, g_ref = refs[n : n + 2], refs[n + 2]
    for a, b, col in products:
        left, right = refs[a], refs[b]
        for out_ref, order, base in zip(outs, orders, (0, outs[0].shape[1])):
            start, stop = max(col, base), min(col + right.shape[-1], base + out_ref.shape[1])
            if start >= stop:
                continue
            cols = slice(start - col, stop - col)
            value = g_ref.at[:, pl.ds(0, stop - start)]
            value[...] = tn(left[...], right[:, cols] if leads[b] is None else right[leads[b], :, cols]).astype(BF)
            store_rows(info, value, out_ref, slice(start - base, stop - base), order, rows)


def weight_grad_call(name, us, info, rows, orders, operands, products, split, total):
    arrays = [a for a, _ in operands]
    d = arrays[0].shape[-1]
    widest = max(a.shape[-1] for a in arrays)
    leads = [lead for _, lead in operands]
    return call(
        functools.partial(weight_grad_kernel, leads=leads, products=products, orders=orders, rows=rows),
        name,
        us,
        16,
        scalar(info) + vector(*arrays),
        [((d, split), BF), ((d, total - split), BF)],
        [pltpu.VMEM((d, widest), BF)],
    )


def input_kernel(info, *refs, layout, rows, width, order):
    n = len(layout)
    (x_ref, xr_ref, dq0_ref, dkv0_ref, dq1_ref, dkv1_ref, dr_ref, gain_ref, gg_ref,
     own_ref, other_ref, gcol_ref, w_ref, acc_ref, col_ref, sems) = refs[n:]
    load_weights(info, refs[:n], layout, rows, w_ref, sems)
    acc_ref[...] = jnp.zeros_like(acc_ref)
    acc_ref[1:2, :] = gg_ref[0:1, :]
    gain = gain_ref[0:1, :]

    def run(held, here, at):
        x = (x_ref[info[0], here, :] if held else xr_ref[here, :]).astype(F32)
        xhat, inverse = norm(x)
        dh = nt(dq0_ref[at, :], w_ref[0, :, :width]) + nt(dq1_ref[at, :], w_ref[1, :, :width])
        dh = dh + nt(dkv0_ref[at, :], w_ref[0, :, width : 3 * width])
        dh = dh + nt(dkv1_ref[at, :], w_ref[1, :, width : 3 * width])
        acc_ref[0:1, :] += jnp.sum(dh * xhat, axis=0, keepdims=True)
        (own_ref if held else other_ref)[here, :] = dr_ref[at, :] + norm_back(dh, xhat, inverse, gain)

    token_blocks(info, xr_ref.shape[0], run)
    col_ref[...] = acc_ref[...].T
    store_rows(info, col_ref, gcol_ref, slice(0, LANES), order, rows)


def input_call(info, pieces, layout, rows, width, x, xr, draw, dr, gains, gg, order):
    d, s = x.shape[2], dr.shape[0]
    return call(
        functools.partial(input_kernel, layout=layout, rows=rows, width=width, order=order),
        "input_back",
        10,
        16,
        scalar(info) + stored(*pieces) + vector(x, xr, *draw, dr, gains, gg),
        [((s // 2, d), F32), ((s // 2, d), F32), ((d, LANES), BF)],
        [
            pltpu.VMEM((2, d, 3 * width + LANES), BF),
            pltpu.VMEM((LANES, d), F32),
            pltpu.VMEM((d, LANES), F32),
            pltpu.SemaphoreType.DMA((copies_of(layout),)),
        ],
    )


def swap(x):
    return lax.ppermute(x, "tensor", [(0, 1), (1, 0)])


def peer(x, k):
    return lax.ppermute(x, "dp", [(i, i ^ k) for i in range(16)])


def under(x, run, *sends):
    x, arrays = after((x, [a for _, a in sends]))
    got = [f(a) for (f, _), a in zip(sends, arrays)]
    return after((run(x), got))


def to(k):
    return lambda x: peer(x, k)


def add(*terms):
    return functools.reduce(jnp.add, [t.astype(F32) for t in terms])


class Gather:
    def __init__(self, split):
        self.split = split

    def near(self, block):
        self.ab = block[:, : self.split], block[:, self.split :]
        return [(to(k), x) for k, x in zip((1, 2), self.ab)]

    def far(self, got):
        self.ab = [jnp.concatenate(x, 0) for x in zip(self.ab, got)]
        return [(to(k), x) for k, x in zip((2, 1), self.ab)]

    def pieces(self, got, theirs, got_theirs):
        orders = (0, ORDER_A), (self.split, ORDER_B)
        where = [(col, order[8 * i : 8 * i + 8]) for i in range(2) for col, order in orders]
        layout = [(r, *w) for r in range(2) for w in where]
        return [*self.ab, *got, *theirs, *got_theirs], layout


def half_sends(terms, ks):
    n = terms[0][0].shape[0] // 2
    keep = [[t[:n] for t in ts] for ts in terms]
    return keep, [(to(k), add(*(t[n:] for t in ts)).astype(BF)) for k, ts in zip(ks, terms)]


def joined(keep, got):
    return [ts + [g] for ts, g in zip(keep, got)]


def last_sends(terms):
    both = jnp.concatenate([add(*ts) for ts in terms], 1)
    n = both.shape[0] // 4
    send = both[n:].astype(BF)
    return both[:n], [(to(4 * i), send[(i - 1) * n : i * n]) for i in (1, 2, 3)]


def gather_plain(slab):
    whole = lax.all_gather(slab, "dp", axis=0, tiled=True)
    return [whole, swap(whole)], [(0, 0, None), (1, 0, None)]


def scatter_plain(a, b):
    both = jnp.concatenate([add(*a), add(*b)], 1)
    return lax.psum_scatter(both, "dp", scatter_dimension=0, tiled=True)


def local(
    hidden_in, segment_ids, qkv_weight, out_weight, mlp_weight, down_weight, attn_gain, mlp_gain,
    cotangent, *, cube,
):
    t, me = lax.axis_index("tensor"), lax.axis_index("dp")
    info = jnp.stack([t, me]).astype(jnp.int32)
    rows, width = qkv_weight.shape[1:]
    d = hidden_in.shape[2]
    units_here = mlp_weight.shape[2]
    units = up_to(units_here)
    s = segment_ids.shape[1]

    def placed(own, got):
        first = t == 0
        return jnp.stack([jnp.where(first, own, got), jnp.where(first, got, own)])

    def other(x):
        return lax.dynamic_index_in_dim(x, 1 - t, 0, False)

    x_recv = swap(other(hidden_in))
    gain_cols = jnp.stack([attn_gain, mlp_gain], 1)
    gain_cols = jnp.pad(gain_cols, ((0, 0), (0, LANES - 2)))
    slab1 = jnp.concatenate([qkv_weight[0], qkv_weight[1], qkv_weight[2], gain_cols], 1)

    def wide(w):
        return jnp.pad(w, ((0, 0), (0, units - units_here)))

    def second_slab(out_weight, mlp_weight, down_weight):
        return jnp.concatenate(
            [out_weight.T, wide(mlp_weight[0]), wide(mlp_weight[1]), wide(down_weight.T)], 1
        )

    weights2 = out_weight, mlp_weight, down_weight
    total1, total2 = slab1.shape[1], width + 3 * units
    split1, split2 = total1 // 2 // LANES * LANES, total2 // 2 // LANES * LANES
    seg = lax.dynamic_index_in_dim(segment_ids, t, 0, False)
    index = jnp.arange(s, dtype=jnp.int32)
    start = jnp.sum((seg[None, :] < seg[:, None]).astype(jnp.int32), axis=1)
    freqs = THETA ** (-2.0 * jnp.arange(HEAD_DIM // 2, dtype=F32) / HEAD_DIM)
    angles = (index - start).astype(F32)[:, None] * freqs[None, :]
    cos, sin = jnp.cos(angles), jnp.sin(angles)
    cos = jnp.concatenate([cos, cos, cos, cos], 1)
    sin = jnp.concatenate([-sin, sin, -sin, sin], 1)
    col = jnp.broadcast_to(seg[:, None], (s, LANES))
    row = jnp.broadcast_to(seg[None, :], (8, s))
    ends = seg.reshape(s // QB, QB)
    first, last = ends[:, 0], ends[:, -1]
    meet = (first[:, None] <= last[None, :]) & (first[None, :] <= last[:, None])
    block = jnp.arange(s // QB, dtype=jnp.int32)[None, :]
    low = jnp.min(jnp.where(meet, block, s), axis=1)
    high = jnp.max(jnp.where(meet, block, -1), axis=1)
    ranges = jnp.stack([low * QB, high - low + 1], 1).astype(jnp.int32)

    def project(w1):
        return qkv_call(info, w1, layout1, rows, width, hidden_in, x_recv, cos, sin)

    def attend(qkv):
        return attend_call(ranges, col, row, qkv)

    if cube:
        g1 = Gather(split1)
        g2 = Gather(split2)
        sends = g1.near(jnp.concatenate([slab1] + [peer(slab1, k) for k in (4, 8, 12)], 0))
        (weights2, x_recv), g1.ab = after(((weights2, x_recv), [x for _, x in sends]))
        got = [f(x) for (f, _), x in zip(sends, g1.ab)]
        slab2 = second_slab(*weights2)
        block2 = jnp.concatenate([slab2] + [peer(slab2, k) for k in (4, 8, 12)], 0)
        sends = g1.far(got)
        got = [f(x) for f, x in sends]
        got, g1.ab = after((got, g1.ab))
        w1, layout1 = g1.pieces(got, [swap(x) for x in g1.ab], [swap(x) for x in got])
        (qkv, h1, gains), (*got, dy_recv) = under(
            w1, project, *g2.near(block2), (swap, other(cotangent))
        )
        far = g2.far(got)
        (o, lse), got = under(qkv, attend, *far, *((swap, x) for _, x in far))
        w2, layout2 = g2.pieces(got[:2], got[2:], [swap(x) for x in got[:2]])
    else:
        w1, layout1 = gather_plain(slab1)
        w2, layout2 = gather_plain(second_slab(*weights2))
        dy_recv = swap(other(cotangent))
        qkv, h1, gains = project(w1)
        o, lse = attend(qkv)
    out_own, out_other, dr, do0, do1, h2, dy, da, dgu0, dgu1, m0, m1, gg = mlp_call(
        info, w2, layout2, rows, width, units, hidden_in, x_recv, cotangent, dy_recv, o, gains
    )
    orders = (ORDER_A, ORDER_B) if cube else (None, None)

    def grads2(r):
        return lambda o: weight_grad_call(
            "mlp_weight_grad", 10, info, rows, orders,
            [(da, None), (h2, None), (dy, None), (o, r), ((dgu0, dgu1)[r], None), ((m0, m1)[r], None)],
            [(0, 3, 0), (1, 4, width), (2, 5, width + 2 * units)], split2, total2,
        )

    def grads1(draw):
        return weight_grad_call(
            "qkv_weight_grad", 6, info, rows, orders,
            [(h1, None), (draw[0], None), (draw[1], None)],
            [(0, 1, 0), (0, 2, width)], split1, total1 - LANES,
        )

    def back(r):
        return lambda do: attend_back_call(r, ranges, col, row, qkv, do, o, lse, cos, sin)

    def input_back(dr):
        return input_call(
            info, w1, layout1, rows, width, hidden_in, x_recv, (*draw0, *draw1), dr, gains, gg, orders[1]
        )

    sent = grads2(1)(o)
    mine, (*theirs, out_recv) = under(o, grads2(0), *((swap, g) for g in sent), (swap, out_other))
    layer_out = placed(out_own, out_recv)
    sums2 = [[a, b] for a, b in zip(mine, theirs)]
    if cube:
        keep, sends = half_sends(sums2, (2, 1))
        draw1, got = under(do1, back(1), *sends)
        keep, sends = half_sends(joined(keep, got), (1, 2))
        do0, sends2 = after((do0, [x for _, x in sends]))
        sent = grads1(after(draw1, sends2))
        draw0, got = under(
            after(do0, sent), back(0), *((f, x) for (f, _), x in zip(sends, sends2)), *((swap, g) for g in sent)
        )
        keep2, sends2 = last_sends(joined(keep, got[:2]))
        draw0, last = after((draw0, [x for _, x in sends2]))
        mine = grads1(draw0)
        keep, sends = half_sends([[a, b] for a, b in zip(mine, got[2:])], (2, 1))
        (in_own, in_other, gcol), got = under(
            dr, input_back, *((f, x) for (f, _), x in zip(sends2, last)), *sends
        )
        sum2 = add(keep2, *got[:3])
        keep, sends = half_sends(joined(keep, got[3:]), (1, 2))

        def gain_sums(gcol):
            both = add(gcol, swap(gcol))
            for k in (1, 2):
                n = both.shape[0] // 2
                both = add(both[:n], peer(both[n:].astype(BF), k))
            return both

        gain_sum, (*got, in_recv) = under(gcol, gain_sums, *sends, (swap, in_other))
        keep = joined(keep, got)
        keep, sends = last_sends([keep[0], [jnp.concatenate([add(*keep[1]), gain_sum], 1)]])
        input_grad, got = under(in_recv, lambda got: placed(in_own, got), *sends)
        sum1 = add(keep, *got)
    else:
        sum2 = scatter_plain(*sums2)
        draw1, draw0 = back(1)(do1), back(0)(do0)
        theirs = [swap(g) for g in grads1(draw1)]
        mine = grads1(draw0)
        in_own, in_other, gcol = input_back(dr)
        input_grad = placed(in_own, swap(in_other))
        b = [jnp.concatenate([g, c], 1) for g, c in zip((mine[1], theirs[1]), (gcol, swap(gcol)))]
        sum1 = scatter_plain((mine[0], theirs[0]), b)
    qkv_grad = sum1[:, : 3 * width].reshape(rows, 3, width).transpose(1, 0, 2)
    c = width
    proj_grad = sum2[:, :c].T
    mlp_grad = jnp.stack([sum2[:, c : c + units_here], sum2[:, c + units : c + units + units_here]])
    down_grad = sum2[:, c + 2 * units : c + 2 * units + units_here].T
    return (
        layer_out,
        input_grad,
        qkv_grad,
        proj_grad,
        mlp_grad,
        down_grad,
        sum1[:, 3 * width],
        sum1[:, 3 * width + 1],
    )


def solution(mesh):
    rows = P(None, ("dp", "tensor"), None)
    in_specs = (
        rows,
        P(None, "dp"),
        P(None, "dp", "tensor"),
        P("tensor", "dp"),
        P(None, "dp", "tensor"),
        P("tensor", "dp"),
        P("dp"),
        P("dp"),
        rows,
    )
    out_specs = (
        rows,
        rows,
        P(None, "dp", "tensor"),
        P("tensor", "dp"),
        P(None, "dp", "tensor"),
        P("tensor", "dp"),
        P("dp"),
        P("dp"),
    )
    cube = mesh.shape["dp"] == 16
    return jax.shard_map(
        functools.partial(local, cube=cube), mesh=mesh, in_specs=in_specs, out_specs=out_specs, check_vma=False
    )
```

```python
import functools

import jax
import jax.numpy as jnp
from jax import lax
from jax.experimental import pallas as pl
from jax.experimental.pallas import tpu as pltpu
from jax.sharding import PartitionSpec as P

HEAD_DIM = 64
LANES = 128
QB = 256
TB = 512
THETA = 160000.0
EPS = 1e-05
LOG2E = 1.4426950408889634
SAFE = 96.0
BF = jnp.bfloat16
F32 = jnp.float32

ORDER_A = (0, 4, 8, 12, 1, 5, 9, 13, 2, 6, 10, 14, 3, 7, 11, 15)
ORDER_B = (0, 4, 8, 12, 2, 6, 10, 14, 1, 5, 9, 13, 3, 7, 11, 15)


def nn(a, b):
    return lax.dot_general(a, b, (((1,), (0,)), ((), ())), preferred_element_type=F32)


def nt(a, b):
    return lax.dot_general(a, b, (((1,), (1,)), ((), ())), preferred_element_type=F32)


def tn(a, b):
    return lax.dot_general(a, b, (((0,), (0,)), ((), ())), preferred_element_type=F32)


def up_to(n):
    return -(-n // LANES) * LANES


def rotate(u, cos, sin, sign):
    lane = lax.broadcasted_iota(jnp.int32, u.shape, 1)
    half = HEAD_DIM // 2
    partner = jnp.where(
        (lane % HEAD_DIM) < half, pltpu.roll(u, LANES - half, 1), pltpu.roll(u, half, 1)
    )
    return u * cos + partner * sin if sign > 0 else u * cos - partner * sin


def norm(x):
    center = x - jnp.mean(x, axis=-1, keepdims=True)
    inverse = lax.rsqrt(jnp.mean(center * center, axis=-1, keepdims=True) + EPS)
    return center * inverse, inverse


def norm_back(grad, xhat, inverse, gain):
    z = grad * gain
    inner = z - jnp.mean(z, axis=-1, keepdims=True) - xhat * jnp.mean(z * xhat, axis=-1, keepdims=True)
    return inverse * inner


def staged(count, stages):
    live = [None] * len(stages)
    for step in range(count + len(stages) - 1):
        new = [None] * len(stages)
        for s, stage in enumerate(stages):
            if 0 <= step - s < count:
                new[s] = stage(step - s, live[s - 1] if s else None)
        live = new


def after(x, *deps):
    return lax.optimization_barrier((x, deps))[0]


def call(kernel, name, us, vmem, operands, out_shape, scratch=()):
    spaces = [space for _, space in operands]
    return pl.pallas_call(
        kernel,
        in_specs=[pl.BlockSpec(memory_space=space) for space in spaces],
        out_specs=[pl.BlockSpec(memory_space=pltpu.VMEM)] * len(out_shape),
        scratch_shapes=list(scratch),
        out_shape=[jax.ShapeDtypeStruct(shape, dtype) for shape, dtype in out_shape],
        compiler_params=pltpu.CompilerParams(vmem_limit_bytes=vmem << 20),
        cost_estimate=pl.CostEstimate(flops=int(us * 1.15e9), transcendentals=0, bytes_accessed=int(us * 1e6)),
        name=name,
    )(*[array for array, _ in operands])


def vector(*arrays):
    return [(a, pltpu.VMEM) for a in arrays]


def stored(*arrays):
    return [(a, pltpu.HBM) for a in arrays]


def scalar(*arrays):
    return [(a, pltpu.SMEM) for a in arrays]


def load_weights(info, pieces, layout, rows, dest, sems):
    copies = []
    for ref, (r, col, order) in zip(pieces, layout, strict=True):
        cols = pl.ds(col, ref.shape[1])
        if order is None:
            copies.append((ref, dest.at[r, :, cols]))
            continue
        for i, k in enumerate(order):
            row = pl.multiple_of((info[1] ^ k) * rows, rows)
            copies.append((ref.at[pl.ds(i * rows, rows), :], dest.at[r, pl.ds(row, rows), cols]))
    copies = [pltpu.make_async_copy(a, b, sems.at[i]) for i, (a, b) in enumerate(copies)]
    for c in copies:
        c.start()
    for c in copies:
        c.wait()


def copies_of(layout):
    return sum(1 if order is None else len(order) for _, _, order in layout)


def store_rows(info, value_ref, out_ref, cols, order, rows):
    if order is None:
        out_ref[:, cols] = value_ref[...].astype(BF)
        return
    for i, k in enumerate(order):
        row = pl.multiple_of((info[1] ^ k) * rows, rows)
        out_ref[i * rows : (i + 1) * rows, cols] = value_ref[pl.ds(row, rows), :].astype(BF)


def token_blocks(info, half, run, size=TB):
    count = half // size

    @pl.loop(0, 2 * count)
    def _(step):
        held = step < count
        first = jnp.where(held, info[0], 1 - info[0]) * half
        here = pl.multiple_of((step % count) * size, size)
        run(held, pl.ds(here, size), pl.ds(pl.multiple_of(first + here, size), size))


def held_or_received(held, info, held_ref, received_ref, here):
    return jnp.where(held, held_ref[info[0], here, :], received_ref[here, :])


def store_half(held, own_ref, other_ref, here, value):
    @pl.when(held)
    def _():
        own_ref[here, :] = value

    @pl.when(jnp.logical_not(held))
    def _():
        other_ref[here, :] = value


def qkv_kernel(info, *refs, layout, rows, width):
    n = len(layout)
    pieces, (x_ref, recv_ref, cos_ref, sin_ref, qkv_ref, h_ref, gain_ref, w_ref, sems) = refs[:n], refs[n:]
    load_weights(info, pieces, layout, rows, w_ref, sems)
    gain_ref[...] = w_ref[0, :, 3 * width :].astype(F32).T[:8]

    def run(held, here, at):
        x = held_or_received(held, info, x_ref, recv_ref, here).astype(F32)
        xhat, _ = norm(x)
        h = (xhat * gain_ref[0:1, :]).astype(BF)
        h_ref[at, :] = h
        cos, sin = cos_ref[at, :], sin_ref[at, :]
        for r in range(2):
            raw = nn(h, w_ref[r, :, : 3 * width])
            for b in range(2 * width // LANES):
                cols = slice(b * LANES, (b + 1) * LANES)
                u = rotate(raw[:, cols], cos, sin, 1)
                if b < width // LANES:
                    u = u * (HEAD_DIM**-0.5 * LOG2E)
                qkv_ref[r, at, cols] = u.astype(BF)
            qkv_ref[r, at, 2 * width :] = raw[:, 2 * width :].astype(BF)

    token_blocks(info, recv_ref.shape[0], run)


def qkv_call(info, pieces, layout, rows, width, x, recv, cos, sin):
    d, s = x.shape[2], cos.shape[0]
    return call(
        functools.partial(qkv_kernel, layout=layout, rows=rows, width=width),
        "qkv",
        12,
        16,
        scalar(info) + stored(*pieces) + vector(x, recv, cos, sin),
        [((2, s, 3 * width), BF), ((s, d), BF), ((8, d), F32)],
        [pltpu.VMEM((2, d, 3 * width + LANES), BF), pltpu.SemaphoreType.DMA((copies_of(layout),))],
    )


def same_segment(col, row):
    parts = [
        jnp.where(col == row[:, i * LANES : (i + 1) * LANES], 0.0, -1e30).astype(F32)
        for i in range(row.shape[1] // LANES)
    ]
    return jnp.concatenate(parts, 1)


def by_range(ranges, i, blocks, run):
    few = blocks // 2

    @pl.when(ranges[i, 1] <= few)
    def _():
        first = jnp.minimum(ranges[i, 0], (blocks - few) * QB)
        run(few, pl.ds(pl.multiple_of(first, QB), few * QB))

    @pl.when(ranges[i, 1] > few)
    def _():
        run(blocks, pl.ds(0, blocks * QB))


def head(h):
    return slice(h * HEAD_DIM, (h + 1) * HEAD_DIM)


def largest(x):
    x = x.astype(F32)
    sums = [jnp.sum(x[head(h)] * x[head(h)], axis=0, keepdims=True) for h in range(x.shape[0] // HEAD_DIM)]
    return jnp.max(functools.reduce(jnp.maximum, sums))


def attend_kernel(ranges, col_ref, row_ref, qkv_ref, o_ref, lse_ref, qt_ref, vt_ref, safe_ref):
    s, width = o_ref.shape[1:]
    heads, blocks = width // HEAD_DIM, s // QB

    @pl.loop(0, 2 * blocks)
    def _(step):
        r, i = step // blocks, step % blocks
        at = pl.ds(pl.multiple_of(i * QB, QB), QB)

        @pl.when(i == 0)
        def _():
            qt_ref[...] = qkv_ref[r, :, :width].T
            vt_ref[...] = qkv_ref[r, :, 2 * width :].T
            bound = largest(qt_ref[...]) * largest(qkv_ref[r, :, width : 2 * width].T)
            safe_ref[0] = (bound < SAFE * SAFE).astype(jnp.int32)

        def run(n, keys, safe):
            bias = same_segment(col_ref[keys, :], row_ref[0:1, at])
            outs, sums = [None] * heads, [None] * heads

            def scores(h, _):
                k = qkv_ref[r, keys, width + h * HEAD_DIM : width + (h + 1) * HEAD_DIM]
                x = nn(k, qt_ref[head(h), at]) + bias
                return x, None if safe else jnp.max(x, axis=0, keepdims=True)

            def expo(h, a):
                e = jnp.exp2(a[0] if safe else a[0] - a[1])
                return e.astype(BF), jnp.sum(e, axis=0, keepdims=True), a[1]

            def out(h, a):
                outs[h] = nn(vt_ref[head(h), keys], a[0]) * (1.0 / a[1])
                total = jnp.log2(a[1])
                sums[h] = total if safe else a[2] + total

            staged(heads, [scores, expo, out])
            o_ref[r, at, :] = jnp.concatenate(outs, axis=0).T.astype(BF)
            for h in range(heads):
                lse_ref[r, h : h + 1, at] = sums[h]

        @pl.when(safe_ref[0] == 1)
        def _():
            by_range(ranges, i, blocks, functools.partial(run, safe=True))

        @pl.when(safe_ref[0] == 0)
        def _():
            run(blocks, slice(0, s), False)


def attend_call(ranges, col, row, qkv):
    _, s, w3 = qkv.shape
    width = w3 // 3
    return call(
        attend_kernel,
        "attend",
        20,
        20,
        scalar(ranges) + vector(col, row, qkv),
        [((2, s, width), BF), ((2, 8, s), F32)],
        [pltpu.VMEM((width, s), BF), pltpu.VMEM((width, s), BF), pltpu.SMEM((1,), jnp.int32)],
    )


def attend_back_kernel(
    ranges, which, col_ref, row_ref, qkv_ref, do_ref, o_ref, lse_ref, cos_ref, sin_ref,
    dq_ref, dkv_ref, qt_ref, dot_ref, dqt_ref, delta_ref,
):
    r = which[0]
    s, width = dq_ref.shape
    heads, blocks = width // HEAD_DIM, s // QB
    qt_ref[...] = qkv_ref[r, :, :width].T
    dqt_ref[...] = jnp.zeros_like(dqt_ref)
    for i in range(blocks):
        at = slice(i * QB, (i + 1) * QB)
        dot = do_ref[at, :].astype(F32).T
        dot_ref[:, at] = dot.astype(BF)
        both = dot * o_ref[r, at, :].astype(F32).T
        for h in range(heads):
            delta_ref[h : h + 1, at] = jnp.sum(both[head(h)], axis=0, keepdims=True)

    @pl.loop(0, blocks)
    def _(c):
        here = pl.ds(pl.multiple_of(c * QB, QB), QB)

        def run(n, queries):
            bias = same_segment(col_ref[here, :], row_ref[0:1, queries])
            dks, dvs = [None] * heads, [None] * heads

            def part(h, c):
                return qkv_ref[r, here, c * width + h * HEAD_DIM : c * width + (h + 1) * HEAD_DIM]

            def products(h, _):
                return (
                    nn(part(h, 1), qt_ref[head(h), queries]) + bias,
                    nn(part(h, 2), dot_ref[head(h), queries]),
                )

            def scores(h, a):
                p = jnp.exp2(a[0] - lse_ref[r, h : h + 1, queries])
                return p.astype(BF), (p * (a[1] - delta_ref[h : h + 1, queries])).astype(BF)

            def grads(h, a):
                dvs[h] = nt(dot_ref[head(h), queries], a[0])
                dks[h] = nt(qt_ref[head(h), queries], a[1])
                dqt_ref[head(h), queries] += nn(part(h, 1).T, a[1])

            staged(heads, [products, scores, grads])
            cos, sin = cos_ref[here, :], sin_ref[here, :]
            for b in range(width // LANES):
                dk = jnp.concatenate(dks[2 * b : 2 * b + 2], 0).T
                dv = jnp.concatenate(dvs[2 * b : 2 * b + 2], 0).T
                dk = rotate(dk, cos, sin, -1) * (1 / LOG2E)
                dkv_ref[here, b * LANES : (b + 1) * LANES] = dk.astype(BF)
                dkv_ref[here, width + b * LANES : width + (b + 1) * LANES] = dv.astype(BF)

        by_range(ranges, c, blocks, run)

    for i in range(blocks):
        at = slice(i * QB, (i + 1) * QB)
        for b in range(width // LANES):
            cols = slice(b * LANES, (b + 1) * LANES)
            dq = dqt_ref[cols, at].T * HEAD_DIM**-0.5
            dq_ref[at, cols] = rotate(dq, cos_ref[at, :], sin_ref[at, :], -1).astype(BF)


def attend_back_call(r, ranges, col, row, qkv, do, o, lse, cos, sin):
    _, s, w3 = qkv.shape
    width = w3 // 3
    return call(
        attend_back_kernel,
        "attend_back",
        18,
        24,
        scalar(ranges, jnp.full((1,), r, jnp.int32)) + vector(col, row, qkv, do, o, lse, cos, sin),
        [((s, width), BF), ((s, 2 * width), BF)],
        [
            pltpu.VMEM((width, s), BF),
            pltpu.VMEM((width, s), BF),
            pltpu.VMEM((width, s), F32),
            pltpu.VMEM((8, s), F32),
        ],
    )


def mlp_kernel(info, *refs, layout, rows, width, units):
    n = len(layout)
    (x_ref, xr_ref, dy_ref, dyr_ref, o_ref, gain_ref,
     own_ref, other_ref, dr_ref, do0_ref, do1_ref, h_ref, dyo_ref, da_ref,
     dgu0_ref, dgu1_ref, m0_ref, m1_ref, gg_ref,
     w_ref, sems) = refs[n:]
    load_weights(info, refs[:n], layout, rows, w_ref, sems)
    gg_ref[...] = jnp.zeros_like(gg_ref)
    c0, c2, c3 = width, width + 2 * units, width + 3 * units
    gain = gain_ref[1:2, :]

    def run(held, here, at):
        x = held_or_received(held, info, x_ref, xr_ref, here).astype(F32)
        dyb = held_or_received(held, info, dy_ref, dyr_ref, here)
        dyo_ref[at, :] = dyb
        r1 = x + nt(o_ref[0, at, :], w_ref[0, :, :c0]) + nt(o_ref[1, at, :], w_ref[1, :, :c0])
        xhat, inverse = norm(r1)
        h = (xhat * gain).astype(BF)
        h_ref[at, :] = h
        outs, dhs = [], []

        def products(r, _):
            return nn(h, w_ref[r, :, c0:c2]), nn(dyb, w_ref[r, :, c2:c3])

        def units_of(r, a):
            gate, up, dm = a[0][:, :units], a[0][:, units:], a[1]
            phi = 0.5 + 0.5 * lax.erf(gate * 0.7071067811865476)
            density = jnp.exp(-0.5 * gate * gate) * 0.3989422804014327
            gelu = gate * phi
            m = (gelu * up).astype(BF)
            dgate = (dm * up * (phi + gate * density)).astype(BF)
            dup = (dm * gelu).astype(BF)
            (m0_ref, m1_ref)[r][at, :] = m
            dgu_ref = (dgu0_ref, dgu1_ref)[r]
            dgu_ref[at, :units] = dgate
            dgu_ref[at, units:] = dup
            return m, jnp.concatenate([dgate, dup], 1)

        def sums(r, a):
            outs.append(nt(a[0], w_ref[r, :, c2:c3]))
            dhs.append(nt(a[1], w_ref[r, :, c0:c2]))

        staged(2, [products, units_of, sums])
        out = (r1 + (outs[0] + outs[1])).astype(BF)
        store_half(held, own_ref, other_ref, here, out)
        dh = dhs[0] + dhs[1]
        gg_ref[0:1, :] += jnp.sum(dh * xhat, axis=0, keepdims=True)
        dr = dyb.astype(F32) + norm_back(dh, xhat, inverse, gain)
        dr_ref[at, :] = dr
        da = dr.astype(BF)
        da_ref[at, :] = da
        for r in range(2):
            (do0_ref, do1_ref)[r][at, :] = nn(da, w_ref[r, :, :c0]).astype(BF)

    token_blocks(info, xr_ref.shape[0], run, TB // 2)


def mlp_call(info, pieces, layout, rows, width, units, x, xr, dy, dyr, o, gains):
    d, s = x.shape[2], o.shape[1]
    return call(
        functools.partial(mlp_kernel, layout=layout, rows=rows, width=width, units=units),
        "mlp",
        30,
        24,
        scalar(info) + stored(*pieces) + vector(x, xr, dy, dyr, o, gains),
        [
            ((s // 2, d), BF),
            ((s // 2, d), BF),
            ((s, d), F32),
            ((s, width), BF),
            ((s, width), BF),
            ((s, d), BF),
            ((s, d), BF),
            ((s, d), BF),
            ((s, 2 * units), BF),
            ((s, 2 * units), BF),
            ((s, units), BF),
            ((s, units), BF),
            ((8, d), F32),
        ],
        [pltpu.VMEM((2, d, width + 3 * units), BF), pltpu.SemaphoreType.DMA((copies_of(layout),))],
    )


def weight_grad_kernel(info, *refs, leads, products, orders, rows):
    n = len(leads)
    outs, g_ref = refs[n : n + 2], refs[n + 2]
    for a, b, col in products:
        left, right = refs[a], refs[b]
        for out_ref, order, base in zip(outs, orders, (0, outs[0].shape[1])):
            start, stop = max(col, base), min(col + right.shape[-1], base + out_ref.shape[1])
            if start >= stop:
                continue
            cols = slice(start - col, stop - col)
            value = g_ref.at[:, pl.ds(0, stop - start)]
            value[...] = tn(left[...], right[:, cols] if leads[b] is None else right[leads[b], :, cols]).astype(BF)
            store_rows(info, value, out_ref, slice(start - base, stop - base), order, rows)


def weight_grad_call(name, us, info, rows, orders, operands, products, split, total):
    arrays = [a for a, _ in operands]
    d = arrays[0].shape[-1]
    widest = max(a.shape[-1] for a in arrays)
    leads = [lead for _, lead in operands]
    return call(
        functools.partial(weight_grad_kernel, leads=leads, products=products, orders=orders, rows=rows),
        name,
        us,
        16,
        scalar(info) + vector(*arrays),
        [((d, split), BF), ((d, total - split), BF)],
        [pltpu.VMEM((d, widest), BF)],
    )


def input_kernel(info, *refs, layout, rows, width, order):
    n = len(layout)
    (x_ref, xr_ref, dq0_ref, dkv0_ref, dq1_ref, dkv1_ref, dr_ref, gain_ref, gg_ref,
     own_ref, other_ref, gcol_ref, w_ref, acc_ref, col_ref, sems) = refs[n:]
    load_weights(info, refs[:n], layout, rows, w_ref, sems)
    acc_ref[...] = jnp.zeros_like(acc_ref)
    acc_ref[1:2, :] = gg_ref[0:1, :]
    gain = gain_ref[0:1, :]

    def run(held, here, at):
        x = held_or_received(held, info, x_ref, xr_ref, here).astype(F32)
        xhat, inverse = norm(x)
        dh = nt(dq0_ref[at, :], w_ref[0, :, :width]) + nt(dq1_ref[at, :], w_ref[1, :, :width])
        dh = dh + nt(dkv0_ref[at, :], w_ref[0, :, width : 3 * width])
        dh = dh + nt(dkv1_ref[at, :], w_ref[1, :, width : 3 * width])
        acc_ref[0:1, :] += jnp.sum(dh * xhat, axis=0, keepdims=True)
        store_half(held, own_ref, other_ref, here, dr_ref[at, :] + norm_back(dh, xhat, inverse, gain))

    token_blocks(info, xr_ref.shape[0], run)
    col_ref[...] = acc_ref[...].T
    store_rows(info, col_ref, gcol_ref, slice(0, LANES), order, rows)


def input_call(info, pieces, layout, rows, width, x, xr, draw, dr, gains, gg, order):
    d, s = x.shape[2], dr.shape[0]
    return call(
        functools.partial(input_kernel, layout=layout, rows=rows, width=width, order=order),
        "input_back",
        10,
        16,
        scalar(info) + stored(*pieces) + vector(x, xr, *draw, dr, gains, gg),
        [((s // 2, d), F32), ((s // 2, d), F32), ((d, LANES), BF)],
        [
            pltpu.VMEM((2, d, 3 * width + LANES), BF),
            pltpu.VMEM((LANES, d), F32),
            pltpu.VMEM((d, LANES), F32),
            pltpu.SemaphoreType.DMA((copies_of(layout),)),
        ],
    )


def swap(x):
    return lax.ppermute(x, "tensor", [(0, 1), (1, 0)])


def peer(x, k):
    return lax.ppermute(x, "dp", [(i, i ^ k) for i in range(16)])


def under(x, run, *sends):
    x, arrays = after((x, [a for _, a in sends]))
    got = [f(a) for (f, _), a in zip(sends, arrays)]
    return after((run(x), got))


def to(k):
    return lambda x: peer(x, k)


def add(*terms):
    return functools.reduce(jnp.add, [t.astype(F32) for t in terms])


class Gather:
    def __init__(self, split):
        self.split = split

    def near(self, block):
        self.ab = block[:, : self.split], block[:, self.split :]
        return [(to(k), x) for k, x in zip((1, 2), self.ab)]

    def far(self, got):
        self.ab = [jnp.concatenate(x, 0) for x in zip(self.ab, got)]
        return [(to(k), x) for k, x in zip((2, 1), self.ab)]

    def pieces(self, got, theirs, got_theirs):
        orders = (0, ORDER_A), (self.split, ORDER_B)
        where = [(col, order[8 * i : 8 * i + 8]) for i in range(2) for col, order in orders]
        layout = [(r, *w) for r in range(2) for w in where]
        return [*self.ab, *got, *theirs, *got_theirs], layout


def half_sends(terms, ks):
    n = terms[0][0].shape[0] // 2
    keep = [[t[:n] for t in ts] for ts in terms]
    return keep, [(to(k), add(*(t[n:] for t in ts)).astype(BF)) for k, ts in zip(ks, terms)]


def joined(keep, got):
    return [ts + [g] for ts, g in zip(keep, got)]


def last_sends(terms):
    both = jnp.concatenate([add(*ts) for ts in terms], 1)
    n = both.shape[0] // 4
    send = both[n:].astype(BF)
    return both[:n], [(to(4 * i), send[(i - 1) * n : i * n]) for i in (1, 2, 3)]


def gather_plain(slab):
    whole = lax.all_gather(slab, "dp", axis=0, tiled=True)
    return [whole, swap(whole)], [(0, 0, None), (1, 0, None)]


def scatter_plain(a, b):
    both = jnp.concatenate([add(*a), add(*b)], 1)
    return lax.psum_scatter(both, "dp", scatter_dimension=0, tiled=True)


def local(
    hidden_in, segment_ids, qkv_weight, out_weight, mlp_weight, down_weight, attn_gain, mlp_gain,
    cotangent, *, cube,
):
    t, me = lax.axis_index("tensor"), lax.axis_index("dp")
    info = jnp.stack([t, me]).astype(jnp.int32)
    rows, width = qkv_weight.shape[1:]
    d = hidden_in.shape[2]
    units_here = mlp_weight.shape[2]
    units = up_to(units_here)
    s = segment_ids.shape[1]

    def placed(own, got):
        first = t == 0
        return jnp.stack([jnp.where(first, own, got), jnp.where(first, got, own)])

    def other(x):
        return lax.dynamic_index_in_dim(x, 1 - t, 0, False)

    x_recv = swap(other(hidden_in))
    gain_cols = jnp.stack([attn_gain, mlp_gain], 1)
    gain_cols = jnp.pad(gain_cols, ((0, 0), (0, LANES - 2)))
    slab1 = jnp.concatenate([qkv_weight[0], qkv_weight[1], qkv_weight[2], gain_cols], 1)

    def wide(w):
        return jnp.pad(w, ((0, 0), (0, units - units_here)))

    def second_slab(out_weight, mlp_weight, down_weight):
        return jnp.concatenate(
            [out_weight.T, wide(mlp_weight[0]), wide(mlp_weight[1]), wide(down_weight.T)], 1
        )

    weights2 = out_weight, mlp_weight, down_weight
    total1, total2 = slab1.shape[1], width + 3 * units
    split1, split2 = total1 // 2 // LANES * LANES, total2 // 2 // LANES * LANES
    seg = lax.dynamic_index_in_dim(segment_ids, t, 0, False)
    index = jnp.arange(s, dtype=jnp.int32)
    start = jnp.sum((seg[None, :] < seg[:, None]).astype(jnp.int32), axis=1)
    freqs = THETA ** (-2.0 * jnp.arange(HEAD_DIM // 2, dtype=F32) / HEAD_DIM)
    angles = (index - start).astype(F32)[:, None] * freqs[None, :]
    cos, sin = jnp.cos(angles), jnp.sin(angles)
    cos = jnp.concatenate([cos, cos, cos, cos], 1)
    sin = jnp.concatenate([-sin, sin, -sin, sin], 1)
    col = jnp.broadcast_to(seg[:, None], (s, LANES))
    row = jnp.broadcast_to(seg[None, :], (8, s))
    ends = seg.reshape(s // QB, QB)
    first, last = ends[:, 0], ends[:, -1]
    meet = (first[:, None] <= last[None, :]) & (first[None, :] <= last[:, None])
    block = jnp.arange(s // QB, dtype=jnp.int32)[None, :]
    low = jnp.min(jnp.where(meet, block, s), axis=1)
    high = jnp.max(jnp.where(meet, block, -1), axis=1)
    ranges = jnp.stack([low * QB, high - low + 1], 1).astype(jnp.int32)

    def project(w1):
        return qkv_call(info, w1, layout1, rows, width, hidden_in, x_recv, cos, sin)

    def attend(qkv):
        return attend_call(ranges, col, row, qkv)

    if cube:
        g1 = Gather(split1)
        g2 = Gather(split2)
        sends = g1.near(jnp.concatenate([slab1] + [peer(slab1, k) for k in (4, 8, 12)], 0))
        (weights2, x_recv), g1.ab = after(((weights2, x_recv), [x for _, x in sends]))
        got = [f(x) for (f, _), x in zip(sends, g1.ab)]
        slab2 = second_slab(*weights2)
        block2 = jnp.concatenate([slab2] + [peer(slab2, k) for k in (4, 8, 12)], 0)
        sends = g1.far(got)
        got = [f(x) for f, x in sends]
        got, g1.ab = after((got, g1.ab))
        w1, layout1 = g1.pieces(got, [swap(x) for x in g1.ab], [swap(x) for x in got])
        (qkv, h1, gains), (*got, dy_recv) = under(
            w1, project, *g2.near(block2), (swap, other(cotangent))
        )
        far = g2.far(got)
        (o, lse), got = under(qkv, attend, *far, *((swap, x) for _, x in far))
        w2, layout2 = g2.pieces(got[:2], got[2:], [swap(x) for x in got[:2]])
    else:
        w1, layout1 = gather_plain(slab1)
        w2, layout2 = gather_plain(second_slab(*weights2))
        dy_recv = swap(other(cotangent))
        qkv, h1, gains = project(w1)
        o, lse = attend(qkv)
    out_own, out_other, dr, do0, do1, h2, dy, da, dgu0, dgu1, m0, m1, gg = mlp_call(
        info, w2, layout2, rows, width, units, hidden_in, x_recv, cotangent, dy_recv, o, gains
    )
    orders = (ORDER_A, ORDER_B) if cube else (None, None)

    def grads2(r):
        return lambda o: weight_grad_call(
            "mlp_weight_grad", 10, info, rows, orders,
            [(da, None), (h2, None), (dy, None), (o, r), ((dgu0, dgu1)[r], None), ((m0, m1)[r], None)],
            [(0, 3, 0), (1, 4, width), (2, 5, width + 2 * units)], split2, total2,
        )

    def grads1(draw):
        return weight_grad_call(
            "qkv_weight_grad", 6, info, rows, orders,
            [(h1, None), (draw[0], None), (draw[1], None)],
            [(0, 1, 0), (0, 2, width)], split1, total1 - LANES,
        )

    def back(r):
        return lambda do: attend_back_call(r, ranges, col, row, qkv, do, o, lse, cos, sin)

    def input_back(dr):
        return input_call(
            info, w1, layout1, rows, width, hidden_in, x_recv, (*draw0, *draw1), dr, gains, gg, orders[1]
        )

    sent = grads2(1)(o)
    mine, (*theirs, out_recv) = under(o, grads2(0), *((swap, g) for g in sent), (swap, out_other))
    layer_out = placed(out_own, out_recv)
    sums2 = [[a, b] for a, b in zip(mine, theirs)]
    if cube:
        keep, sends = half_sends(sums2, (2, 1))
        draw1, got = under(do1, back(1), *sends)
        keep, sends = half_sends(joined(keep, got), (1, 2))
        do0, sends2 = after((do0, [x for _, x in sends]))
        sent = grads1(after(draw1, sends2))
        draw0, got = under(
            after(do0, sent), back(0), *((f, x) for (f, _), x in zip(sends, sends2)), *((swap, g) for g in sent)
        )
        keep2, sends2 = last_sends(joined(keep, got[:2]))
        draw0, last = after((draw0, [x for _, x in sends2]))
        mine = grads1(draw0)
        keep, sends = half_sends([[a, b] for a, b in zip(mine, got[2:])], (2, 1))
        (in_own, in_other, gcol), got = under(
            dr, input_back, *((f, x) for (f, _), x in zip(sends2, last)), *sends
        )
        sum2 = add(keep2, *got[:3])
        keep, sends = half_sends(joined(keep, got[3:]), (1, 2))

        def gain_sums(gcol):
            both = add(gcol, swap(gcol))
            for k in (1, 2):
                n = both.shape[0] // 2
                both = add(both[:n], peer(both[n:].astype(BF), k))
            return both

        gain_sum, (*got, in_recv) = under(gcol, gain_sums, *sends, (swap, in_other))
        keep = joined(keep, got)
        keep, sends = last_sends([keep[0], [jnp.concatenate([add(*keep[1]), gain_sum], 1)]])
        input_grad, got = under(in_recv, lambda got: placed(in_own, got), *sends)
        sum1 = add(keep, *got)
    else:
        sum2 = scatter_plain(*sums2)
        draw1, draw0 = back(1)(do1), back(0)(do0)
        theirs = [swap(g) for g in grads1(draw1)]
        mine = grads1(draw0)
        in_own, in_other, gcol = input_back(dr)
        input_grad = placed(in_own, swap(in_other))
        b = [jnp.concatenate([g, c], 1) for g, c in zip((mine[1], theirs[1]), (gcol, swap(gcol)))]
        sum1 = scatter_plain((mine[0], theirs[0]), b)
    qkv_grad = sum1[:, : 3 * width].reshape(rows, 3, width).transpose(1, 0, 2)
    c = width
    proj_grad = sum2[:, :c].T
    mlp_grad = jnp.stack([sum2[:, c : c + units_here], sum2[:, c + units : c + units + units_here]])
    down_grad = sum2[:, c + 2 * units : c + 2 * units + units_here].T
    return (
        layer_out,
        input_grad,
        qkv_grad,
        proj_grad,
        mlp_grad,
        down_grad,
        sum1[:, 3 * width],
        sum1[:, 3 * width + 1],
    )


def solution(mesh):
    rows = P(None, ("dp", "tensor"), None)
    in_specs = (
        rows,
        P(None, "dp"),
        P(None, "dp", "tensor"),
        P("tensor", "dp"),
        P(None, "dp", "tensor"),
        P("tensor", "dp"),
        P("dp"),
        P("dp"),
        rows,
    )
    out_specs = (
        rows,
        rows,
        P(None, "dp", "tensor"),
        P("tensor", "dp"),
        P(None, "dp", "tensor"),
        P("tensor", "dp"),
        P("dp"),
        P("dp"),
    )
    cube = mesh.shape["dp"] == 16
    return jax.shard_map(
        functools.partial(local, cube=cube), mesh=mesh, in_specs=in_specs, out_specs=out_specs, check_vma=False
    )
```

```python
import functools

import jax
import jax.numpy as jnp
from jax import lax
from jax.experimental import pallas as pl
from jax.experimental.pallas import tpu as pltpu
from jax.sharding import PartitionSpec as P

HEAD_DIM = 64
LANES = 128
QB = 256
TB = 512
THETA = 160000.0
EPS = 1e-05
LOG2E = 1.4426950408889634
SAFE = 96.0
BF = jnp.bfloat16
F32 = jnp.float32

ORDER_A = (0, 4, 8, 12, 1, 5, 9, 13, 2, 6, 10, 14, 3, 7, 11, 15)
ORDER_B = (0, 4, 8, 12, 2, 6, 10, 14, 1, 5, 9, 13, 3, 7, 11, 15)


def nn(a, b):
    return lax.dot_general(a, b, (((1,), (0,)), ((), ())), preferred_element_type=F32)


def nt(a, b):
    return lax.dot_general(a, b, (((1,), (1,)), ((), ())), preferred_element_type=F32)


def tn(a, b):
    return lax.dot_general(a, b, (((0,), (0,)), ((), ())), preferred_element_type=F32)


def up_to(n):
    return -(-n // LANES) * LANES


def rotate(u, cos, sin, sign):
    lane = lax.broadcasted_iota(jnp.int32, u.shape, 1)
    half = HEAD_DIM // 2
    partner = jnp.where(
        (lane % HEAD_DIM) < half, pltpu.roll(u, LANES - half, 1), pltpu.roll(u, half, 1)
    )
    return u * cos + partner * sin if sign > 0 else u * cos - partner * sin


def norm(x):
    center = x - jnp.mean(x, axis=-1, keepdims=True)
    inverse = lax.rsqrt(jnp.mean(center * center, axis=-1, keepdims=True) + EPS)
    return center * inverse, inverse


def norm_back(grad, xhat, inverse, gain):
    z = grad * gain
    inner = z - jnp.mean(z, axis=-1, keepdims=True) - xhat * jnp.mean(z * xhat, axis=-1, keepdims=True)
    return inverse * inner


def staged(count, stages):
    live = [None] * len(stages)
    for step in range(count + len(stages) - 1):
        new = [None] * len(stages)
        for s, stage in enumerate(stages):
            if 0 <= step - s < count:
                new[s] = stage(step - s, live[s - 1] if s else None)
        live = new


def after(x, *deps):
    return lax.optimization_barrier((x, deps))[0]


def call(kernel, name, us, vmem, operands, out_shape, scratch=()):
    spaces = [space for _, space in operands]
    return pl.pallas_call(
        kernel,
        in_specs=[pl.BlockSpec(memory_space=space) for space in spaces],
        out_specs=[pl.BlockSpec(memory_space=pltpu.VMEM)] * len(out_shape),
        scratch_shapes=list(scratch),
        out_shape=[jax.ShapeDtypeStruct(shape, dtype) for shape, dtype in out_shape],
        compiler_params=pltpu.CompilerParams(vmem_limit_bytes=vmem << 20),
        cost_estimate=pl.CostEstimate(flops=int(us * 1.15e9), transcendentals=0, bytes_accessed=int(us * 1e6)),
        name=name,
    )(*[array for array, _ in operands])


def vector(*arrays):
    return [(a, pltpu.VMEM) for a in arrays]


def stored(*arrays):
    return [(a, pltpu.HBM) for a in arrays]


def scalar(*arrays):
    return [(a, pltpu.SMEM) for a in arrays]


def load_weights(info, pieces, layout, rows, dest, sems):
    copies = []
    for ref, (r, col, order) in zip(pieces, layout, strict=True):
        cols = pl.ds(col, ref.shape[1])
        if order is None:
            copies.append((ref, dest.at[r, :, cols]))
            continue
        for i, k in enumerate(order):
            row = pl.multiple_of((info[1] ^ k) * rows, rows)
            copies.append((ref.at[pl.ds(i * rows, rows), :], dest.at[r, pl.ds(row, rows), cols]))
    copies = [pltpu.make_async_copy(a, b, sems.at[i]) for i, (a, b) in enumerate(copies)]
    for c in copies:
        c.start()
    for c in copies:
        c.wait()


def copies_of(layout):
    return sum(1 if order is None else len(order) for _, _, order in layout)


def store_rows(info, value_ref, out_ref, cols, order, rows):
    if order is None:
        out_ref[:, cols] = value_ref[...].astype(BF)
        return
    for i, k in enumerate(order):
        row = pl.multiple_of((info[1] ^ k) * rows, rows)
        out_ref[i * rows : (i + 1) * rows, cols] = value_ref[pl.ds(row, rows), :].astype(BF)


def token_blocks(info, half, run, size=TB):
    count = half // size

    @pl.loop(0, 2 * count)
    def _(step):
        held = step < count
        first = jnp.where(held, info[0], 1 - info[0]) * half
        here = pl.multiple_of((step % count) * size, size)
        run(held, pl.ds(here, size), pl.ds(pl.multiple_of(first + here, size), size))


def held_or_received(held, info, held_ref, received_ref, here):
    return jnp.where(held, held_ref[info[0], here, :], received_ref[here, :])


def store_half(held, own_ref, other_ref, here, value):
    @pl.when(held)
    def _():
        own_ref[here, :] = value

    @pl.when(jnp.logical_not(held))
    def _():
        other_ref[here, :] = value


def qkv_kernel(info, *refs, layout, rows, width):
    n = len(layout)
    pieces, (x_ref, recv_ref, cos_ref, sin_ref, qkv_ref, h_ref, gain_ref, w_ref, sems) = refs[:n], refs[n:]
    load_weights(info, pieces, layout, rows, w_ref, sems)
    gain_ref[...] = w_ref[0, :, 3 * width :].astype(F32).T[:8]

    def run(held, here, at):
        x = held_or_received(held, info, x_ref, recv_ref, here).astype(F32)
        xhat, _ = norm(x)
        h = (xhat * gain_ref[0:1, :]).astype(BF)
        h_ref[at, :] = h
        cos, sin = cos_ref[at, :], sin_ref[at, :]
        for r in range(2):
            raw = nn(h, w_ref[r, :, : 3 * width])
            for b in range(2 * width // LANES):
                cols = slice(b * LANES, (b + 1) * LANES)
                u = rotate(raw[:, cols], cos, sin, 1)
                if b < width // LANES:
                    u = u * (HEAD_DIM**-0.5 * LOG2E)
                qkv_ref[r, at, cols] = u.astype(BF)
            qkv_ref[r, at, 2 * width :] = raw[:, 2 * width :].astype(BF)

    token_blocks(info, recv_ref.shape[0], run)


def qkv_call(info, pieces, layout, rows, width, x, recv, cos, sin):
    d, s = x.shape[2], cos.shape[0]
    return call(
        functools.partial(qkv_kernel, layout=layout, rows=rows, width=width),
        "qkv",
        12,
        16,
        scalar(info) + stored(*pieces) + vector(x, recv, cos, sin),
        [((2, s, 3 * width), BF), ((s, d), BF), ((8, d), F32)],
        [pltpu.VMEM((2, d, 3 * width + LANES), BF), pltpu.SemaphoreType.DMA((copies_of(layout),))],
    )


def same_segment(col, row):
    parts = [
        jnp.where(col == row[:, i * LANES : (i + 1) * LANES], 0.0, -1e30).astype(F32)
        for i in range(row.shape[1] // LANES)
    ]
    return jnp.concatenate(parts, 1)


def by_range(ranges, i, blocks, run):
    few = blocks // 2

    @pl.when(ranges[i, 1] <= few)
    def _():
        first = jnp.minimum(ranges[i, 0], (blocks - few) * QB)
        run(few, pl.ds(pl.multiple_of(first, QB), few * QB))

    @pl.when(ranges[i, 1] > few)
    def _():
        run(blocks, pl.ds(0, blocks * QB))


def head(h):
    return slice(h * HEAD_DIM, (h + 1) * HEAD_DIM)


def largest(x):
    x = x.astype(F32)
    sums = [jnp.sum(x[head(h)] * x[head(h)], axis=0, keepdims=True) for h in range(x.shape[0] // HEAD_DIM)]
    return jnp.max(functools.reduce(jnp.maximum, sums))


def attend_kernel(ranges, col_ref, row_ref, qkv_ref, o_ref, lse_ref, qt_ref, vt_ref, safe_ref):
    s, width = o_ref.shape[1:]
    heads, blocks = width // HEAD_DIM, s // QB

    @pl.loop(0, 2 * blocks)
    def _(step):
        r, i = step // blocks, step % blocks
        at = pl.ds(pl.multiple_of(i * QB, QB), QB)

        @pl.when(i == 0)
        def _():
            qt_ref[...] = qkv_ref[r, :, :width].T
            vt_ref[...] = qkv_ref[r, :, 2 * width :].T
            bound = largest(qt_ref[...]) * largest(qkv_ref[r, :, width : 2 * width].T)
            safe_ref[0] = (bound < SAFE * SAFE).astype(jnp.int32)

        def run(n, keys, safe):
            bias = same_segment(col_ref[keys, :], row_ref[0:1, at])
            outs, sums = [None] * heads, [None] * heads

            def scores(h, _):
                k = qkv_ref[r, keys, width + h * HEAD_DIM : width + (h + 1) * HEAD_DIM]
                x = nn(k, qt_ref[head(h), at]) + bias
                return x, None if safe else jnp.max(x, axis=0, keepdims=True)

            def expo(h, a):
                e = jnp.exp2(a[0] if safe else a[0] - a[1])
                return e.astype(BF), jnp.sum(e, axis=0, keepdims=True), a[1]

            def out(h, a):
                outs[h] = nn(vt_ref[head(h), keys], a[0]) * (1.0 / a[1])
                total = jnp.log2(a[1])
                sums[h] = total if safe else a[2] + total

            staged(heads, [scores, expo, out])
            o_ref[r, at, :] = jnp.concatenate(outs, axis=0).T.astype(BF)
            for h in range(heads):
                lse_ref[r, h : h + 1, at] = sums[h]

        @pl.when(safe_ref[0] == 1)
        def _():
            by_range(ranges, i, blocks, functools.partial(run, safe=True))

        @pl.when(safe_ref[0] == 0)
        def _():
            run(blocks, slice(0, s), False)


def attend_call(ranges, col, row, qkv):
    _, s, w3 = qkv.shape
    width = w3 // 3
    return call(
        attend_kernel,
        "attend",
        20,
        20,
        scalar(ranges) + vector(col, row, qkv),
        [((2, s, width), BF), ((2, 8, s), F32)],
        [pltpu.VMEM((width, s), BF), pltpu.VMEM((width, s), BF), pltpu.SMEM((1,), jnp.int32)],
    )


def attend_back_kernel(
    ranges, which, col_ref, row_ref, qkv_ref, do_ref, o_ref, lse_ref, cos_ref, sin_ref,
    dq_ref, dkv_ref, qt_ref, dot_ref, dqt_ref, delta_ref,
):
    r = which[0]
    s, width = dq_ref.shape
    heads, blocks = width // HEAD_DIM, s // QB
    qt_ref[...] = qkv_ref[r, :, :width].T
    dqt_ref[...] = jnp.zeros_like(dqt_ref)
    for i in range(blocks):
        at = slice(i * QB, (i + 1) * QB)
        dot = do_ref[at, :].astype(F32).T
        dot_ref[:, at] = dot.astype(BF)
        both = dot * o_ref[r, at, :].astype(F32).T
        for h in range(heads):
            delta_ref[h : h + 1, at] = jnp.sum(both[head(h)], axis=0, keepdims=True)

    @pl.loop(0, blocks)
    def _(c):
        here = pl.ds(pl.multiple_of(c * QB, QB), QB)

        def run(n, queries):
            bias = same_segment(col_ref[here, :], row_ref[0:1, queries])
            dks, dvs = [None] * heads, [None] * heads

            def part(h, c):
                return qkv_ref[r, here, c * width + h * HEAD_DIM : c * width + (h + 1) * HEAD_DIM]

            def products(h, _):
                return (
                    nn(part(h, 1), qt_ref[head(h), queries]) + bias,
                    nn(part(h, 2), dot_ref[head(h), queries]),
                )

            def scores(h, a):
                p = jnp.exp2(a[0] - lse_ref[r, h : h + 1, queries])
                return p.astype(BF), (p * (a[1] - delta_ref[h : h + 1, queries])).astype(BF)

            def grads(h, a):
                dvs[h] = nt(dot_ref[head(h), queries], a[0])
                dks[h] = nt(qt_ref[head(h), queries], a[1])
                dqt_ref[head(h), queries] += nn(part(h, 1).T, a[1])

            staged(heads, [products, scores, grads])
            cos, sin = cos_ref[here, :], sin_ref[here, :]
            for b in range(width // LANES):
                dk = jnp.concatenate(dks[2 * b : 2 * b + 2], 0).T
                dv = jnp.concatenate(dvs[2 * b : 2 * b + 2], 0).T
                dk = rotate(dk, cos, sin, -1) * (1 / LOG2E)
                dkv_ref[here, b * LANES : (b + 1) * LANES] = dk.astype(BF)
                dkv_ref[here, width + b * LANES : width + (b + 1) * LANES] = dv.astype(BF)

        by_range(ranges, c, blocks, run)

    for i in range(blocks):
        at = slice(i * QB, (i + 1) * QB)
        for b in range(width // LANES):
            cols = slice(b * LANES, (b + 1) * LANES)
            dq = dqt_ref[cols, at].T * HEAD_DIM**-0.5
            dq_ref[at, cols] = rotate(dq, cos_ref[at, :], sin_ref[at, :], -1).astype(BF)


def attend_back_call(r, ranges, col, row, qkv, do, o, lse, cos, sin):
    _, s, w3 = qkv.shape
    width = w3 // 3
    return call(
        attend_back_kernel,
        "attend_back",
        18,
        24,
        scalar(ranges, jnp.full((1,), r, jnp.int32)) + vector(col, row, qkv, do, o, lse, cos, sin),
        [((s, width), BF), ((s, 2 * width), BF)],
        [
            pltpu.VMEM((width, s), BF),
            pltpu.VMEM((width, s), BF),
            pltpu.VMEM((width, s), F32),
            pltpu.VMEM((8, s), F32),
        ],
    )


def mlp_kernel(info, *refs, layout, rows, width, units):
    n = len(layout)
    (x_ref, xr_ref, dy_ref, dyr_ref, o_ref, gain_ref,
     own_ref, other_ref, dr_ref, do0_ref, do1_ref, h_ref, dyo_ref, da_ref,
     dgu0_ref, dgu1_ref, m0_ref, m1_ref, gg_ref,
     w_ref, sems) = refs[n:]
    load_weights(info, refs[:n], layout, rows, w_ref, sems)
    gg_ref[...] = jnp.zeros_like(gg_ref)
    c0, c2, c3 = width, width + 2 * units, width + 3 * units
    gain = gain_ref[1:2, :]

    def run(held, here, at):
        x = held_or_received(held, info, x_ref, xr_ref, here).astype(F32)
        dyb = held_or_received(held, info, dy_ref, dyr_ref, here)
        dyo_ref[at, :] = dyb
        r1 = x + nt(o_ref[0, at, :], w_ref[0, :, :c0]) + nt(o_ref[1, at, :], w_ref[1, :, :c0])
        xhat, inverse = norm(r1)
        h = (xhat * gain).astype(BF)
        h_ref[at, :] = h
        outs, dhs = [], []

        def products(r, _):
            return nn(h, w_ref[r, :, c0:c2]), nn(dyb, w_ref[r, :, c2:c3])

        def units_of(r, a):
            gate, up, dm = a[0][:, :units], a[0][:, units:], a[1]
            phi = 0.5 + 0.5 * lax.erf(gate * 0.7071067811865476)
            density = jnp.exp(-0.5 * gate * gate) * 0.3989422804014327
            gelu = gate * phi
            m = (gelu * up).astype(BF)
            dgate = (dm * up * (phi + gate * density)).astype(BF)
            dup = (dm * gelu).astype(BF)
            (m0_ref, m1_ref)[r][at, :] = m
            dgu_ref = (dgu0_ref, dgu1_ref)[r]
            dgu_ref[at, :units] = dgate
            dgu_ref[at, units:] = dup
            return m, jnp.concatenate([dgate, dup], 1)

        def sums(r, a):
            outs.append(nt(a[0], w_ref[r, :, c2:c3]))
            dhs.append(nt(a[1], w_ref[r, :, c0:c2]))

        staged(2, [products, units_of, sums])
        out = (r1 + (outs[0] + outs[1])).astype(BF)
        store_half(held, own_ref, other_ref, here, out)
        dh = dhs[0] + dhs[1]
        gg_ref[0:1, :] += jnp.sum(dh * xhat, axis=0, keepdims=True)
        dr = dyb.astype(F32) + norm_back(dh, xhat, inverse, gain)
        dr_ref[at, :] = dr
        da = dr.astype(BF)
        da_ref[at, :] = da
        for r in range(2):
            (do0_ref, do1_ref)[r][at, :] = nn(da, w_ref[r, :, :c0]).astype(BF)

    token_blocks(info, xr_ref.shape[0], run, TB // 2)


def mlp_call(info, pieces, layout, rows, width, units, x, xr, dy, dyr, o, gains):
    d, s = x.shape[2], o.shape[1]
    return call(
        functools.partial(mlp_kernel, layout=layout, rows=rows, width=width, units=units),
        "mlp",
        30,
        24,
        scalar(info) + stored(*pieces) + vector(x, xr, dy, dyr, o, gains),
        [
            ((s // 2, d), BF),
            ((s // 2, d), BF),
            ((s, d), F32),
            ((s, width), BF),
            ((s, width), BF),
            ((s, d), BF),
            ((s, d), BF),
            ((s, d), BF),
            ((s, 2 * units), BF),
            ((s, 2 * units), BF),
            ((s, units), BF),
            ((s, units), BF),
            ((8, d), F32),
        ],
        [pltpu.VMEM((2, d, width + 3 * units), BF), pltpu.SemaphoreType.DMA((copies_of(layout),))],
    )


def weight_grad_kernel(info, *refs, leads, products, orders, rows):
    n = len(leads)
    outs, g_ref = refs[n : n + 2], refs[n + 2]
    for a, b, col in products:
        left, right = refs[a], refs[b]
        for out_ref, order, base in zip(outs, orders, (0, outs[0].shape[1])):
            start, stop = max(col, base), min(col + right.shape[-1], base + out_ref.shape[1])
            if start >= stop:
                continue
            cols = slice(start - col, stop - col)
            value = g_ref.at[:, pl.ds(0, stop - start)]
            value[...] = tn(left[...], right[:, cols] if leads[b] is None else right[leads[b], :, cols]).astype(BF)
            store_rows(info, value, out_ref, slice(start - base, stop - base), order, rows)


def weight_grad_call(name, us, info, rows, orders, operands, products, split, total):
    arrays = [a for a, _ in operands]
    d = arrays[0].shape[-1]
    widest = max(a.shape[-1] for a in arrays)
    leads = [lead for _, lead in operands]
    return call(
        functools.partial(weight_grad_kernel, leads=leads, products=products, orders=orders, rows=rows),
        name,
        us,
        16,
        scalar(info) + vector(*arrays),
        [((d, split), BF), ((d, total - split), BF)],
        [pltpu.VMEM((d, widest), BF)],
    )


def input_kernel(info, *refs, layout, rows, width, order):
    n = len(layout)
    (x_ref, xr_ref, dq0_ref, dkv0_ref, dq1_ref, dkv1_ref, dr_ref, gain_ref, gg_ref,
     own_ref, other_ref, gcol_ref, w_ref, acc_ref, col_ref, sems) = refs[n:]
    load_weights(info, refs[:n], layout, rows, w_ref, sems)
    acc_ref[...] = jnp.zeros_like(acc_ref)
    acc_ref[1:2, :] = gg_ref[0:1, :]
    gain = gain_ref[0:1, :]

    def run(held, here, at):
        x = held_or_received(held, info, x_ref, xr_ref, here).astype(F32)
        xhat, inverse = norm(x)
        dh = nt(dq0_ref[at, :], w_ref[0, :, :width]) + nt(dq1_ref[at, :], w_ref[1, :, :width])
        dh = dh + nt(dkv0_ref[at, :], w_ref[0, :, width : 3 * width])
        dh = dh + nt(dkv1_ref[at, :], w_ref[1, :, width : 3 * width])
        acc_ref[0:1, :] += jnp.sum(dh * xhat, axis=0, keepdims=True)
        store_half(held, own_ref, other_ref, here, dr_ref[at, :] + norm_back(dh, xhat, inverse, gain))

    token_blocks(info, xr_ref.shape[0], run)
    col_ref[...] = acc_ref[...].T
    store_rows(info, col_ref, gcol_ref, slice(0, LANES), order, rows)


def input_call(info, pieces, layout, rows, width, x, xr, draw, dr, gains, gg, order):
    d, s = x.shape[2], dr.shape[0]
    return call(
        functools.partial(input_kernel, layout=layout, rows=rows, width=width, order=order),
        "input_back",
        10,
        16,
        scalar(info) + stored(*pieces) + vector(x, xr, *draw, dr, gains, gg),
        [((s // 2, d), F32), ((s // 2, d), F32), ((d, LANES), BF)],
        [
            pltpu.VMEM((2, d, 3 * width + LANES), BF),
            pltpu.VMEM((LANES, d), F32),
            pltpu.VMEM((d, LANES), F32),
            pltpu.SemaphoreType.DMA((copies_of(layout),)),
        ],
    )


def swap(x):
    return lax.ppermute(x, "tensor", [(0, 1), (1, 0)])


def peer(x, k):
    return lax.ppermute(x, "dp", [(i, i ^ k) for i in range(16)])


def under(x, run, *sends):
    x, arrays = after((x, [a for _, a in sends]))
    got = [f(a) for (f, _), a in zip(sends, arrays)]
    return after((run(x), got))


def to(k):
    return lambda x: peer(x, k)


def add(*terms):
    return functools.reduce(jnp.add, [t.astype(F32) for t in terms])


class Gather:
    def __init__(self, split):
        self.split = split

    def near(self, block):
        self.ab = block[:, : self.split], block[:, self.split :]
        return [(to(k), x) for k, x in zip((1, 2), self.ab)]

    def far(self, got):
        self.ab = [jnp.concatenate(x, 0) for x in zip(self.ab, got)]
        return [(to(k), x) for k, x in zip((2, 1), self.ab)]

    def pieces(self, got, theirs, got_theirs):
        orders = (0, ORDER_A), (self.split, ORDER_B)
        where = [(col, order[8 * i : 8 * i + 8]) for i in range(2) for col, order in orders]
        layout = [(r, *w) for r in range(2) for w in where]
        return [*self.ab, *got, *theirs, *got_theirs], layout


def half_sends(terms, ks):
    n = terms[0][0].shape[0] // 2
    keep = [[t[:n] for t in ts] for ts in terms]
    return keep, [(to(k), add(*(t[n:] for t in ts)).astype(BF)) for k, ts in zip(ks, terms)]


def joined(keep, got):
    return [ts + [g] for ts, g in zip(keep, got)]


def last_sends(terms):
    both = jnp.concatenate([add(*ts) for ts in terms], 1)
    n = both.shape[0] // 4
    send = both[n:].astype(BF)
    return both[:n], [(to(4 * i), send[(i - 1) * n : i * n]) for i in (1, 2, 3)]


def gather_plain(slab):
    whole = lax.all_gather(slab, "dp", axis=0, tiled=True)
    return [whole, swap(whole)], [(0, 0, None), (1, 0, None)]


def scatter_plain(a, b):
    both = jnp.concatenate([add(*a), add(*b)], 1)
    return lax.psum_scatter(both, "dp", scatter_dimension=0, tiled=True)


def local(
    hidden_in, segment_ids, qkv_weight, out_weight, mlp_weight, down_weight, attn_gain, mlp_gain,
    cotangent, *, cube,
):
    t, me = lax.axis_index("tensor"), lax.axis_index("dp")
    info = jnp.stack([t, me]).astype(jnp.int32)
    rows, width = qkv_weight.shape[1:]
    d = hidden_in.shape[2]
    units_here = mlp_weight.shape[2]
    units = up_to(units_here)
    s = segment_ids.shape[1]

    def placed(own, got):
        first = t == 0
        return jnp.stack([jnp.where(first, own, got), jnp.where(first, got, own)])

    def other(x):
        return lax.dynamic_index_in_dim(x, 1 - t, 0, False)

    x_recv = swap(other(hidden_in))
    gain_cols = jnp.stack([attn_gain, mlp_gain], 1)
    gain_cols = jnp.pad(gain_cols, ((0, 0), (0, LANES - 2)))
    slab1 = jnp.concatenate([qkv_weight[0], qkv_weight[1], qkv_weight[2], gain_cols], 1)

    def wide(w):
        return jnp.pad(w, ((0, 0), (0, units - units_here)))

    def second_slab(out_weight, mlp_weight, down_weight):
        return jnp.concatenate(
            [out_weight.T, wide(mlp_weight[0]), wide(mlp_weight[1]), wide(down_weight.T)], 1
        )

    weights2 = out_weight, mlp_weight, down_weight
    total1, total2 = slab1.shape[1], width + 3 * units
    split1, split2 = total1 // 2 // LANES * LANES, total2 // 2 // LANES * LANES
    seg = lax.dynamic_index_in_dim(segment_ids, t, 0, False)
    index = jnp.arange(s, dtype=jnp.int32)
    start = jnp.sum((seg[None, :] < seg[:, None]).astype(jnp.int32), axis=1)
    freqs = THETA ** (-2.0 * jnp.arange(HEAD_DIM // 2, dtype=F32) / HEAD_DIM)
    angles = (index - start).astype(F32)[:, None] * freqs[None, :]
    cos, sin = jnp.cos(angles), jnp.sin(angles)
    cos = jnp.concatenate([cos, cos, cos, cos], 1)
    sin = jnp.concatenate([-sin, sin, -sin, sin], 1)
    col = jnp.broadcast_to(seg[:, None], (s, LANES))
    row = jnp.broadcast_to(seg[None, :], (8, s))
    ends = seg.reshape(s // QB, QB)
    first, last = ends[:, 0], ends[:, -1]
    meet = (first[:, None] <= last[None, :]) & (first[None, :] <= last[:, None])
    block = jnp.arange(s // QB, dtype=jnp.int32)[None, :]
    low = jnp.min(jnp.where(meet, block, s), axis=1)
    high = jnp.max(jnp.where(meet, block, -1), axis=1)
    ranges = jnp.stack([low * QB, high - low + 1], 1).astype(jnp.int32)

    def project(w1):
        return qkv_call(info, w1, layout1, rows, width, hidden_in, x_recv, cos, sin)

    def attend(qkv):
        return attend_call(ranges, col, row, qkv)

    if cube:
        g1 = Gather(split1)
        g2 = Gather(split2)
        sends = g1.near(jnp.concatenate([slab1] + [peer(slab1, k) for k in (4, 8, 12)], 0))
        (weights2, x_recv), g1.ab = after(((weights2, x_recv), [x for _, x in sends]))
        got = [f(x) for (f, _), x in zip(sends, g1.ab)]
        slab2 = second_slab(*weights2)
        block2 = jnp.concatenate([slab2] + [peer(slab2, k) for k in (4, 8, 12)], 0)
        sends = g1.far(got)
        got = [f(x) for f, x in sends]
        got, g1.ab = after((got, g1.ab))
        w1, layout1 = g1.pieces(got, [swap(x) for x in g1.ab], [swap(x) for x in got])
        (qkv, h1, gains), (*got, dy_recv) = under(
            w1, project, *g2.near(block2), (swap, other(cotangent))
        )
        far = g2.far(got)
        (o, lse), got = under(qkv, attend, *far, *((swap, x) for _, x in far))
        w2, layout2 = g2.pieces(got[:2], got[2:], [swap(x) for x in got[:2]])
    else:
        w1, layout1 = gather_plain(slab1)
        w2, layout2 = gather_plain(second_slab(*weights2))
        dy_recv = swap(other(cotangent))
        qkv, h1, gains = project(w1)
        o, lse = attend(qkv)
    out_own, out_other, dr, do0, do1, h2, dy, da, dgu0, dgu1, m0, m1, gg = mlp_call(
        info, w2, layout2, rows, width, units, hidden_in, x_recv, cotangent, dy_recv, o, gains
    )
    orders = (ORDER_A, ORDER_B) if cube else (None, None)

    def grads2(r):
        return lambda o: weight_grad_call(
            "mlp_weight_grad", 60, info, rows, orders,
            [(da, None), (h2, None), (dy, None), (o, r), ((dgu0, dgu1)[r], None), ((m0, m1)[r], None)],
            [(0, 3, 0), (1, 4, width), (2, 5, width + 2 * units)], split2, total2,
        )

    def grads1(draw):
        return weight_grad_call(
            "qkv_weight_grad", 6, info, rows, orders,
            [(h1, None), (draw[0], None), (draw[1], None)],
            [(0, 1, 0), (0, 2, width)], split1, total1 - LANES,
        )

    def back(r):
        return lambda do: attend_back_call(r, ranges, col, row, qkv, do, o, lse, cos, sin)

    def input_back(dr):
        return input_call(
            info, w1, layout1, rows, width, hidden_in, x_recv, (*draw0, *draw1), dr, gains, gg, orders[1]
        )

    sent = grads2(1)(o)
    mine, (*theirs, out_recv) = under(o, grads2(0), *((swap, g) for g in sent), (swap, out_other))
    layer_out = placed(out_own, out_recv)
    sums2 = [[a, b] for a, b in zip(mine, theirs)]
    if cube:
        keep, sends = half_sends(sums2, (2, 1))
        draw1, got = under(do1, back(1), *sends)
        keep, sends = half_sends(joined(keep, got), (1, 2))
        do0, sends2 = after((do0, [x for _, x in sends]))
        sent = grads1(after(draw1, sends2))
        draw0, got = under(
            after(do0, sent), back(0), *((f, x) for (f, _), x in zip(sends, sends2)), *((swap, g) for g in sent)
        )
        keep2, sends2 = last_sends(joined(keep, got[:2]))
        draw0, last = after((draw0, [x for _, x in sends2]))
        mine = grads1(draw0)
        keep, sends = half_sends([[a, b] for a, b in zip(mine, got[2:])], (2, 1))
        (in_own, in_other, gcol), got = under(
            dr, input_back, *((f, x) for (f, _), x in zip(sends2, last)), *sends
        )
        sum2 = add(keep2, *got[:3])
        keep, sends = half_sends(joined(keep, got[3:]), (1, 2))

        def gain_sums(gcol):
            both = add(gcol, swap(gcol))
            for k in (1, 2):
                n = both.shape[0] // 2
                both = add(both[:n], peer(both[n:].astype(BF), k))
            return both

        gain_sum, (*got, in_recv) = under(gcol, gain_sums, *sends, (swap, in_other))
        keep = joined(keep, got)
        keep, sends = last_sends([keep[0], [jnp.concatenate([add(*keep[1]), gain_sum], 1)]])
        input_grad, got = under(in_recv, lambda got: placed(in_own, got), *sends)
        sum1 = add(keep, *got)
    else:
        sum2 = scatter_plain(*sums2)
        draw1, draw0 = back(1)(do1), back(0)(do0)
        theirs = [swap(g) for g in grads1(draw1)]
        mine = grads1(draw0)
        in_own, in_other, gcol = input_back(dr)
        input_grad = placed(in_own, swap(in_other))
        b = [jnp.concatenate([g, c], 1) for g, c in zip((mine[1], theirs[1]), (gcol, swap(gcol)))]
        sum1 = scatter_plain((mine[0], theirs[0]), b)
    qkv_grad = sum1[:, : 3 * width].reshape(rows, 3, width).transpose(1, 0, 2)
    c = width
    proj_grad = sum2[:, :c].T
    mlp_grad = jnp.stack([sum2[:, c : c + units_here], sum2[:, c + units : c + units + units_here]])
    down_grad = sum2[:, c + 2 * units : c + 2 * units + units_here].T
    return (
        layer_out,
        input_grad,
        qkv_grad,
        proj_grad,
        mlp_grad,
        down_grad,
        sum1[:, 3 * width],
        sum1[:, 3 * width + 1],
    )


def solution(mesh):
    rows = P(None, ("dp", "tensor"), None)
    in_specs = (
        rows,
        P(None, "dp"),
        P(None, "dp", "tensor"),
        P("tensor", "dp"),
        P(None, "dp", "tensor"),
        P("tensor", "dp"),
        P("dp"),
        P("dp"),
        rows,
    )
    out_specs = (
        rows,
        rows,
        P(None, "dp", "tensor"),
        P("tensor", "dp"),
        P(None, "dp", "tensor"),
        P("tensor", "dp"),
        P("dp"),
        P("dp"),
    )
    cube = mesh.shape["dp"] == 16
    return jax.shard_map(
        functools.partial(local, cube=cube), mesh=mesh, in_specs=in_specs, out_specs=out_specs, check_vma=False
    )
```
